32 devices in a mesh: wide: 8 (over z, x), narrow: 4 (over y, core).
Axes of the slice: x: 2, y: 2, z: 4, core: 2. Of those that a mesh axis runs over, the one named last changes fastest.
Arguments:
- moments: float32 [4096, 2048], P('wide', 'narrow'), as said below
- eigen_basis: float32 [4096, 2048], P('wide', 'narrow'), may hold values from -0.125 to 0.125
- slot_order: int32 [2], replicated, may hold values 0 or 1
Outputs:
- halves: float32 [4096, 1024], P('wide', 'narrow')
The draws below stay inside these ranges and needn't reach their ends.
Inputs may be any that keep to these rules, and one draw needn't show every extreme that they name: Each block of 2048 rows of moments is symmetric.
All inputs are finite; a program needn't handle non-finite values.
Results may differ from the reference program's by a relative error of at most 0.0001.
Values sent between devices are 32-bit elements; how exact they have to be, the bound alone decides.
A program may use at most 64 MiB of HBM per device.

```python
import jax
import jax.numpy as jnp
from jax import lax

M = 2048
K = 1024
GROUPS = 2


def draw_moments(key, part):
    base_key = jax.random.fold_in(jax.random.fold_in(key, 11), 0)
    entries = jax.random.normal(base_key, (GROUPS, M, M), jnp.float32)
    symmetric = (entries + jnp.swapaxes(entries, 1, 2)) * 0.7071
    return symmetric.reshape(GROUPS * M, M)


def with_ends(values, rng, least, top_value):
    place = [jax.random.randint(jax.random.fold_in(rng, axis), (), 0, length) for axis, length in enumerate(values.shape)]
    longest = values.shape.index(max(values.shape))
    beside = place[:longest] + [(place[longest] + 1) % values.shape[longest]] + place[longest + 1:]
    return values.at[tuple(place)].set(least).at[tuple(beside)].set(top_value)


def block_scale(stream_key, dims, cuts, low, largest):
    gain = 1.0
    for position, blocks in cuts:
        heights = jax.random.uniform(jax.random.fold_in(jax.random.fold_in(stream_key, 6), position), (blocks,), jnp.float32, low / len(cuts), largest / len(cuts))
        gain = gain * jnp.repeat(jnp.exp(heights), dims[position] // blocks).reshape((-1,) + (1,) * (len(dims) - 1 - position))
    return gain


def gaussian(own_key, dims, scale, limit, pieces=(), held_as=jnp.bfloat16):
    values = jax.random.normal(own_key, dims, jnp.float32) * scale
    if len(pieces) > 0:
        values = block_scale(own_key, dims, pieces, -0.22, 0.18) * values
    return jnp.clip(values, min=-limit, max=limit).astype(held_as)


def setup_inputs(seed: int = 0) -> dict:
    key_list = jax.random.split(jax.random.key(seed), 4)
    return {
        "moments": draw_moments(jax.random.fold_in(key_list[3], 71), 0),
        "eigen_basis": gaussian(key_list[1], (GROUPS * M, M), M ** -0.5, 0.125, ((0, 8), (1, 4)), jnp.float32),
        "slot_order": with_ends((jax.random.randint(key_list[2], (GROUPS,), 0, 2) < 1).astype(jnp.int32), jax.random.fold_in(key_list[2], 1), 0, 1),
    }


def reference(moments, eigen_basis, slot_order):
    outputs = []
    for subproblem in range(GROUPS):
        matrix = moments[subproblem * M:(subproblem + 1) * M]
        vectors = eigen_basis[subproblem * M:(subproblem + 1) * M]
        product = jnp.dot(matrix, vectors, precision=lax.Precision.HIGHEST, preferred_element_type=jnp.float32)
        first_block = jnp.dot(vectors[:, :K].T, product[:, :K], precision=lax.Precision.HIGHEST, preferred_element_type=jnp.float32)
        second = jnp.dot(vectors[:, K:].T, product[:, K:], precision=lax.Precision.HIGHEST, preferred_element_type=jnp.float32)
        swapped = slot_order[subproblem] == 1
        outputs.append(jnp.where(swapped, second, first_block))
        outputs.append(jnp.where(swapped, first_block, second))
    return jnp.concatenate(outputs, axis=0)
```

```python
import jax
import jax.numpy as jnp
from jax import lax
from jax.experimental import pallas as pl
from jax.experimental.pallas import tpu as pltpu
from jax.sharding import PartitionSpec as P

GROUP_WIDE = 4
K = 1024
MESH = pl.DeviceIdType.MESH
CHUNKS = 8
PIECES = 4
LAG = 1
EARLY = 5
COPIES = 8 * PIECES + 4 * PIECES + 2 + 7 * CHUNKS


def split(value):
    high = value.astype(jnp.bfloat16)
    low = (value - high.astype(jnp.float32)).astype(jnp.bfloat16)
    return high, low


def dot3(left, right):
    def dot(a, b):
        return jnp.dot(a, b, preferred_element_type=jnp.float32)

    return dot(left[0], right[0]) + (dot(left[0], right[1]) + dot(left[1], right[0]))


def kernel(
    slot_ref, a_ref, v_ref, o_ref,
    abuf, aparts, opp, oparts, vbuf, sibling_x, left, left_t, leftx_t,
    csend, cmine, crecv, sums, gsame, gother, zsend, zrecv,
    local_sem, send_sem, recv_sem,
):
    rows, cols = a_ref.shape
    wide_half = cols // 2
    piece = rows // PIECES
    chunk = rows // CHUNKS
    w = lax.axis_index("wide")
    n = lax.axis_index("narrow")
    x = w % 2
    z = (w // 2) % 2
    y = n // 2
    core = n % 2
    p = w % 4
    wx = w + 1 - 2 * x
    wz = w + 2 - 4 * z
    px = p + 1 - 2 * x
    pz = p + 2 - 4 * z
    pd = 3 - p
    ns = n + 1 - 2 * core
    ny = n + 2 - 4 * y
    q = 2 * y + core
    qy = 2 * (1 - y) + core
    near = z == y
    far = z != y
    third = jnp.where(near, pz, px)
    first = jnp.where(near, px, pz)

    barrier = pltpu.get_barrier_semaphore()
    for target in ((wx, n), (wz, n), (w, ns), (w, ny), (w, 3 - n)):
        pl.semaphore_signal(barrier, inc=1, device_id=target, device_id_type=MESH)

    def part(i):
        return pl.ds(i * piece, piece)

    def side(t):
        return pl.ds(t * wide_half, wide_half)

    local = [
        pltpu.make_async_copy(v_ref, left.at[core], local_sem.at[0]),
        pltpu.make_async_copy(a_ref, abuf.at[q], local_sem.at[1]),
        pltpu.make_async_copy(v_ref.at[:, side(0)], vbuf.at[p, 0], local_sem.at[2]),
        pltpu.make_async_copy(v_ref.at[:, side(1)], vbuf.at[p, 1], local_sem.at[3]),
    ]
    for copy in local:
        copy.start()

    used = []

    def remote(src, dst, target):
        index = len(used)
        used.append(index)
        return pltpu.make_async_remote_copy(
            src_ref=src, dst_ref=dst, send_sem=send_sem.at[index], recv_sem=recv_sem.at[index],
            device_id=target, device_id_type=MESH,
        )

    pieces = range(PIECES)
    vx = [[remote(v_ref.at[part(i), side(t)], vbuf.at[p, t, part(i)], (wx, n)) for i in pieces] for t in range(2)]
    vz = [[remote(v_ref.at[part(i), side(t)], vbuf.at[p, t, part(i)], (wz, n)) for i in pieces] for t in range(2)]
    vxs = [[remote(vbuf.at[px, t, part(i)], sibling_x.at[t, part(i)], (w, ns)) for i in pieces] for t in range(2)]
    ay = [remote(a_ref.at[part(i)], abuf.at[q, part(i)], (w, ny)) for i in pieces]
    ayr = [remote(abuf.at[qy, part(i)], abuf.at[qy, part(i)], (w, ns)) for i in pieces]
    zo = [remote(abuf.at[pd, part(i)], opp.at[part(i)], (wz, n)) for i in pieces]
    so = [remote(opp.at[part(i)], opp.at[part(i)], (w, ns)) for i in pieces]
    vs = remote(v_ref, left.at[core], (w, ns))
    as_ = remote(a_ref, abuf.at[q], (w, ns))
    cx = [[remote(csend.at[t, j], crecv.at[t, j], (wx, n)) for j in range(CHUNKS)] for t in range(2)]
    keep = [[remote(sums.at[t, j], gsame.at[j], (w, ns)) for j in range(CHUNKS)] for t in range(2)]
    cross = [[remote(sums.at[t, j], gother.at[j], (w, 2 * (1 - y) + t)) for j in range(CHUNKS)] for t in range(2)]
    zc = [remote(zsend.at[j], zrecv.at[j], (wz, n)) for j in range(CHUNKS)]

    def owned(i):
        return core == i // (PIECES // 2)

    def split_a(block, i):
        value = abuf[block, i * piece : (i + 1) * piece, :]
        high, low = split(value)
        aparts[block, 0, i * piece : (i + 1) * piece, :] = high
        aparts[block, 1, i * piece : (i + 1) * piece, :] = low

    def turn_left(half, t, i, value):
        high, low = split(value.T)
        leftx_t[half, 0, t * wide_half : (t + 1) * wide_half, i * piece : (i + 1) * piece] = high
        leftx_t[half, 1, t * wide_half : (t + 1) * wide_half, i * piece : (i + 1) * piece] = low

    def turn_own(t, i):
        turn_left(core, t, i, vbuf[px, t, i * piece : (i + 1) * piece, :])

    def turn_sibling(t, i):
        turn_left(1 - core, t, i, sibling_x[t, i * piece : (i + 1) * piece, :])

    def turn_opp(i):
        high, low = split(opp[i * piece : (i + 1) * piece, :].T)
        oparts[0, :, i * piece : (i + 1) * piece] = high
        oparts[1, :, i * piece : (i + 1) * piece] = low

    late_ay = far & (core == x)
    early_recv = near & (core != x)
    early_relay = near & (core == x)

    pl.semaphore_wait(barrier, 5)
    for i in pieces:
        vx[0][i].start()
        vz[0][i].start()

    @pl.when(jnp.logical_not(late_ay))
    def _():
        for copy in ay:
            copy.start()

    as_.start()
    vs.start()
    for i in pieces:
        vx[1][i].start()
    for copy in local:
        copy.wait()
    as_.wait_recv()

    @pl.when(far)
    def _():
        for i in pieces:
            @pl.when(owned(i))
            def _():
                zo[i].start()

    left_t[core, 0], left_t[core, 1] = split(left[core].T)
    for i in pieces:
        split_a(first, i)

    @pl.when(near)
    def _():
        for i in pieces:
            split_a(p, i)

    vs.wait_recv()
    left_t[1 - core, 0], left_t[1 - core, 1] = split(left[1 - core].T)
    for i in pieces:
        vx[0][i].wait_recv()
        vxs[0][i].start()
        turn_own(0, i)

    @pl.when(late_ay)
    def _():
        for copy in ay:
            copy.start()

    @pl.when(early_recv)
    def _():
        for i in pieces:
            ay[i].wait_recv()
            ayr[i].start()

            @pl.when(owned(i))
            def _():
                zo[i].start()

    @pl.when(early_relay)
    def _():
        for i in pieces:
            ayr[i].wait_recv()

            @pl.when(owned(i))
            def _():
                zo[i].start()

    for i in pieces:
        vz[1][i].start()
    for i in pieces:
        vxs[0][i].wait_recv()
        turn_sibling(0, i)
    for i in pieces:
        vz[0][i].wait_recv()

    def term(t, block):
        return dot3((aparts[block, 0], aparts[block, 1]), split(vbuf[block, t]))

    total = term(0, first)

    def consume(i):
        @pl.when(jnp.logical_not(early_relay))
        def _():
            ayr[i].wait_recv()

        split_a(third, i)

        @pl.when(far)
        def _():
            split_a(p, i)

        vxs[1][i].wait_recv()
        turn_sibling(1, i)

    for i in pieces:
        @pl.when(jnp.logical_not(early_recv))
        def _():
            ay[i].wait_recv()
            ayr[i].start()

        vx[1][i].wait_recv()
        vxs[1][i].start()
        turn_own(1, i)
        if i > 0:
            consume(i - 1)
    for i in pieces:
        @pl.when(owned(i))
        def _():
            zo[i].wait_recv()
            so[i].start()
            turn_opp(i)

    consume(PIECES - 1)
    total += term(0, p)
    total += term(0, third)
    for i in pieces:
        @pl.when(jnp.logical_not(owned(i)))
        def _():
            so[i].wait_recv()
            turn_opp(i)

    def images(t, total):
        other = dot3((oparts[0], oparts[1]), split(vbuf[pz, t]))
        return split(total), split(other)

    def block_of(half, start, size, image):
        span = pl.ds(start, size)
        own, other = image
        return dot3((left_t[half, 0, span], left_t[half, 1, span]), own) + dot3(
            (leftx_t[half, 0, span], leftx_t[half, 1, span]), other
        )

    def send_partials(t, image):
        group = CHUNKS // 2
        for j in range(0, CHUNKS, group):
            block = block_of(1 - x, j * chunk, group * chunk, image)
            for k in range(group):
                csend[t, j + k] = block[k * chunk : (k + 1) * chunk]
                cx[t][j + k].start()

    def keep_partials(t, image):
        block = block_of(x, 0, rows, image)
        for j in range(CHUNKS):
            cmine[t, j] = block[j * chunk : (j + 1) * chunk]

    swapped = slot_ref[w // GROUP_WIDE]
    same_flag = (((z + swapped + y) % 2) == 0).astype(jnp.int32)
    stays = core == y
    leaves = core != y

    def reduce_x(t, j):
        cx[t][j].wait_recv()
        total = cmine[t, j] + crecv[t, j]
        sums[t, j] = total

        @pl.when(leaves)
        def _():
            cross[t][j].start()

        @pl.when(stays & (core != t))
        def _():
            keep[t][j].start()

        @pl.when(stays & (core == t))
        def _():
            gsame[j] = total

    def select_z(t, j):
        @pl.when(core == t)
        def _():
            @pl.when(leaves)
            def _():
                keep[t][j].wait_recv()

            cross[t][j].wait_recv()
            same, other = gsame[j], gother[j]
            mask = jnp.full(same.shape, same_flag) == 1
            zsend[j] = jnp.where(mask, other, same)
            zc[j].start()
            o_ref[pl.ds(j * chunk, chunk), :] = jnp.where(mask, same, other)

    def finish(t, j):
        @pl.when(core == t)
        def _():
            zc[j].wait_recv()
            o_ref[pl.ds(j * chunk, chunk), :] += zrecv[j]

    image = images(0, total)
    send_partials(0, image)
    keep_partials(0, image)
    total = term(1, p) + term(1, px)
    for j in range(EARLY):
        reduce_x(0, j)
    for i in pieces:
        vz[1][i].wait_recv()
    image = images(1, total + term(1, pz))
    send_partials(1, image)
    keep_partials(1, image)

    for j in range(EARLY, CHUNKS):
        reduce_x(0, j)
    for j in range(CHUNKS):
        select_z(0, j)
    for j in range(CHUNKS):
        reduce_x(1, j)
        if j >= LAG:
            select_z(1, j - LAG)
    for j in range(CHUNKS - LAG, CHUNKS):
        select_z(1, j)
    for j in range(CHUNKS):
        finish(0, j)
    for j in range(CHUNKS):
        finish(1, j)

    flat = [copy for group in (*vx, *vz, *vxs, *cx) for copy in group]
    for copy in (*flat, *ay, *ayr, vs, as_, *zc):
        copy.wait_send()
    for i in pieces:
        @pl.when(owned(i))
        def _():
            zo[i].wait_send()
            so[i].wait_send()

    for t in range(2):
        @pl.when(leaves)
        def _():
            for copy in cross[t]:
                copy.wait_send()

        @pl.when(stays & (core != t))
        def _():
            for copy in keep[t]:
                copy.wait_send()


def fast_body(moments, eigen_basis, slot_order):
    rows, cols = moments.shape
    f32 = jnp.float32
    chunk = rows // CHUNKS
    wide_half = cols // 2
    return pl.pallas_call(
        kernel,
        out_shape=jax.ShapeDtypeStruct((rows, wide_half), f32),
        in_specs=[
            pl.BlockSpec(memory_space=pltpu.SMEM),
            pl.BlockSpec(memory_space=pl.ANY),
            pl.BlockSpec(memory_space=pl.ANY),
        ],
        out_specs=pl.BlockSpec(memory_space=pltpu.VMEM),
        scratch_shapes=[
            pltpu.VMEM((4, rows, cols), f32),
            pltpu.VMEM((4, 2, rows, cols), jnp.bfloat16),
            pltpu.VMEM((rows, cols), f32),
            pltpu.VMEM((2, cols, rows), jnp.bfloat16),
            pltpu.VMEM((4, 2, rows, wide_half), f32),
            pltpu.VMEM((2, rows, wide_half), f32),
            pltpu.VMEM((2, rows, cols), f32),
            pltpu.VMEM((2, 2, cols, rows), jnp.bfloat16),
            pltpu.VMEM((2, 2, cols, rows), jnp.bfloat16),
            *[pltpu.VMEM((2, CHUNKS, chunk, wide_half), f32)] * 4,
            *[pltpu.VMEM((CHUNKS, chunk, wide_half), f32)] * 4,
            pltpu.SemaphoreType.DMA((4,)),
            pltpu.SemaphoreType.DMA((COPIES,)),
            pltpu.SemaphoreType.DMA((COPIES,)),
        ],
        compiler_params=pltpu.CompilerParams(
            collective_id=0, has_side_effects=True, vmem_limit_bytes=56 * 1024 * 1024
        ),
        name="rayleigh",
    )(slot_order, moments, eigen_basis)


def partner(value, axis, stride):
    mask = 2**stride
    pairs = [(source, source ^ mask) for source in range(lax.axis_size(axis))]
    return lax.ppermute(value, axis, pairs)


def body(moments, eigen_basis, slot_order):
    wide_pos = lax.axis_index("wide")
    subproblem = wide_pos // GROUP_WIDE
    position = wide_pos % GROUP_WIDE
    swapped = lax.dynamic_index_in_dim(slot_order, subproblem, 0, keepdims=False)
    narrow_pos = lax.axis_index("narrow")
    col_count = eigen_basis.shape[1]
    half_cols = col_count // 2
    full_basis = lax.all_gather(eigen_basis, "narrow", axis=1, tiled=True)
    first_half = lax.dynamic_slice_in_dim(full_basis, narrow_pos * half_cols, half_cols, 1)
    second_half = lax.dynamic_slice_in_dim(full_basis, K + narrow_pos * half_cols, half_cols, 1)
    local_panel = jnp.concatenate([first_half, second_half], axis=1)
    pair_block = partner(local_panel, "wide", 0)
    joined = jnp.where(
        position % 2 == 0,
        jnp.concatenate([local_panel, pair_block], axis=0),
        jnp.concatenate([pair_block, local_panel], axis=0),
    )
    quad_block = partner(joined, "wide", 1)
    col_panel = jnp.where(
        position // 2 % 2 == 0,
        jnp.concatenate([joined, quad_block], axis=0),
        jnp.concatenate([quad_block, joined], axis=0),
    )
    products = jnp.dot(
        lax.all_gather(moments, "narrow", axis=1, tiled=True),
        col_panel,
        precision=lax.Precision.HIGHEST,
        preferred_element_type=jnp.float32,
    )
    partials = []
    for slot_index in range(2):
        half_panel = products[:, slot_index * half_cols : (slot_index + 1) * half_cols]
        vectors_half = full_basis[:, slot_index * K : (slot_index + 1) * K]
        partials.append(
            lax.dot_general(
                vectors_half,
                half_panel,
                (((0,), (0,)), ((), ())),
                precision=lax.Precision.HIGHEST,
                preferred_element_type=jnp.float32,
            )
        )
    stacked = jnp.stack(partials)
    slot_pick = (position // 2 + swapped) % 2
    row_part = position % 2
    summed = stacked + partner(stacked, "wide", 0)
    summed = summed + partner(summed, "wide", 1)
    chosen = lax.dynamic_index_in_dim(summed, slot_pick, 0, keepdims=False)
    return lax.dynamic_slice_in_dim(chosen, row_part * (K // 2), K // 2, 0)


def solution(mesh):
    placed = (P("wide", "narrow"), P("wide", "narrow"), P())
    cube = mesh.shape["narrow"] == 4
    return jax.shard_map(
        fast_body if cube else body, mesh=mesh, in_specs=placed, out_specs=P("wide", "narrow"), check_vma=False
    )
```

```python
import jax
import jax.numpy as jnp
from jax import lax
from jax.experimental import pallas as pl
from jax.experimental.pallas import tpu as pltpu
from jax.sharding import PartitionSpec as P

GROUP_WIDE = 4
K = 1024
MESH = pl.DeviceIdType.MESH
CHUNKS = 8
HALF = CHUNKS // 2
PIECES = 4
OVER_X = 256
COPIES = 12 * PIECES + 28 + 3 * PIECES + 2 + 4 * CHUNKS + 4 * CHUNKS + CHUNKS + HALF


def split(value):
    high = value.astype(jnp.bfloat16)
    low = (value - high.astype(jnp.float32)).astype(jnp.bfloat16)
    return high, low


def dot3(left, right):
    def dot(a, b):
        return jnp.dot(a, b, preferred_element_type=jnp.float32)

    return dot(left[0], right[0]) + (dot(left[0], right[1]) + dot(left[1], right[0]))


def kernel(
    slot_ref, a_ref, v_ref, o_ref,
    abuf, aparts, opp_x, opp_z, oparts, vbuf, sibling_x, left, left_t, leftx_t,
    csend, ckeep, far_rows, near_rows, zsend, zrecv, msend, mirror,
    local_sem, send_sem, recv_sem,
):
    rows, cols = a_ref.shape
    wide_half = cols // 2
    piece = rows // PIECES
    chunk = rows // CHUNKS
    w = lax.axis_index("wide")
    n = lax.axis_index("narrow")
    x = w % 2
    z = (w // 2) % 2
    y = n // 2
    core = n % 2
    p = w % 4
    wx = w + 1 - 2 * x
    wz = w + 2 - 4 * z
    px = p + 1 - 2 * x
    pz = p + 2 - 4 * z
    pd = 3 - p
    ns = n + 1 - 2 * core
    ny = n + 2 - 4 * y
    q = 2 * y + core
    qy = 2 * (1 - y) + core
    near = z == y
    far = z != y
    third = jnp.where(near, pz, px)
    first = jnp.where(near, px, pz)

    barrier = pltpu.get_barrier_semaphore()
    for target in ((wz, n), (w, ns), (w, ny), (w, 3 - n), *((wx, m) for m in range(4))):
        pl.semaphore_signal(barrier, inc=1, device_id=target, device_id_type=MESH)

    def part(i):
        return pl.ds(i * piece, piece)

    def side(t):
        return pl.ds(t * wide_half, wide_half)

    local = [
        pltpu.make_async_copy(v_ref, left.at[core], local_sem.at[0]),
        pltpu.make_async_copy(a_ref, abuf.at[q], local_sem.at[1]),
        pltpu.make_async_copy(v_ref.at[:, side(0)], vbuf.at[p, 0], local_sem.at[2]),
        pltpu.make_async_copy(v_ref.at[:, side(1)], vbuf.at[p, 1], local_sem.at[3]),
    ]
    for copy in local:
        copy.start()

    used = []

    def remote(src, dst, target, arrival=None):
        index = len(used)
        used.append(index)
        return pltpu.make_async_remote_copy(
            src_ref=src, dst_ref=dst, send_sem=send_sem.at[index], recv_sem=recv_sem.at[index if arrival is None else arrival],
            device_id=target, device_id_type=MESH,
        )

    pieces = range(PIECES)
    vx = [[remote(v_ref.at[part(i), side(t)], vbuf.at[p, t, part(i)], (wx, n)) for i in pieces] for t in range(2)]
    vz = [[remote(v_ref.at[part(i), side(t)], vbuf.at[p, t, part(i)], (wz, n)) for i in pieces] for t in range(2)]
    vxs = [[remote(vbuf.at[px, t, part(i)], sibling_x.at[t, part(i)], (w, ns)) for i in pieces] for t in range(2)]
    ay = [remote(a_ref.at[part(i)], abuf.at[q, part(i)], (w, ny)) for i in pieces]
    ayr = [remote(abuf.at[qy, part(i)], abuf.at[qy, part(i)], (w, ns)) for i in pieces]
    quarter = OVER_X // 2
    turned = pl.ds(OVER_X, cols - OVER_X)
    xo = [remote(abuf.at[pd, pl.ds(k * quarter, quarter)], opp_x.at[pl.ds(k * quarter, quarter)], (wx, n)) for k in range(2)]
    xos = [remote(opp_x.at[pl.ds(k * quarter, quarter)], opp_x.at[pl.ds(k * quarter, quarter)], (w, ns)) for k in range(2)]
    zo = [remote(abuf.at[pd, part(i), turned], opp_z.at[part(i)], (wz, n)) for i in pieces]
    zos = [remote(opp_z.at[part(i)], opp_z.at[part(i)], (w, ns)) for i in pieces]
    vs = remote(v_ref, left.at[core], (w, ns))
    as_ = remote(a_ref, abuf.at[q], (w, ns))
    arrivals = len(used)
    used.extend(range(arrivals, arrivals + 4 * CHUNKS))
    steps = range(CHUNKS)
    send_far = [[remote(csend.at[t, j], far_rows.at[y, j], (wx, 2 * core + t), arrivals + 2 * j + y) for j in steps] for t in range(2)]
    send_near = [[remote(ckeep.at[t, j], near_rows.at[y, j], (w, 2 * core + t), arrivals + 2 * CHUNKS + 2 * j + y) for j in steps] for t in range(2)]
    zc = [remote(zsend.at[j], zrecv.at[j], (wz, n)) for j in steps]
    reflect = [remote(msend.at[pl.ds(j * chunk, chunk)], mirror.at[pl.ds(j * chunk, chunk)], (w, ns)) for j in range(HALF)]

    def await_rows(buffer, offset, plane, j):
        pltpu.make_async_remote_copy(
            src_ref=csend.at[0, j], dst_ref=buffer.at[plane, j], send_sem=send_sem.at[0],
            recv_sem=recv_sem.at[arrivals + offset + 2 * j + plane], device_id=(w, ns), device_id_type=MESH,
        ).wait_recv()

    def owned(i):
        return core == i // (PIECES // 2)

    def split_a(block, i):
        value = abuf[block, i * piece : (i + 1) * piece, :]
        high, low = split(value)
        aparts[block, 0, i * piece : (i + 1) * piece, :] = high
        aparts[block, 1, i * piece : (i + 1) * piece, :] = low

    def turn_left(half, t, i, value):
        high, low = split(value.T)
        leftx_t[half, 0, t * wide_half : (t + 1) * wide_half, i * piece : (i + 1) * piece] = high
        leftx_t[half, 1, t * wide_half : (t + 1) * wide_half, i * piece : (i + 1) * piece] = low

    def turn_own(t, i):
        turn_left(core, t, i, vbuf[px, t, i * piece : (i + 1) * piece, :])

    def turn_sibling(t, i):
        turn_left(1 - core, t, i, sibling_x[t, i * piece : (i + 1) * piece, :])

    def turn_opp(i):
        high, low = split(opp_z[i * piece : (i + 1) * piece, :].T)
        oparts[0, OVER_X:, i * piece : (i + 1) * piece] = high
        oparts[1, OVER_X:, i * piece : (i + 1) * piece] = low

    def split_opp(k):
        high, low = split(opp_x[k * quarter : (k + 1) * quarter, :])
        oparts[0, k * quarter : (k + 1) * quarter, :] = high
        oparts[1, k * quarter : (k + 1) * quarter, :] = low

    def start_opp(i):
        for k in range(2):
            if ((k + 1) * quarter - 1) // piece == i:
                @pl.when(core == k)
                def _():
                    xo[k].start()

        @pl.when(owned(i))
        def _():
            zo[i].start()

    late_ay = far & (core == x)
    early_recv = near & (core != x)
    early_relay = near & (core == x)

    pl.semaphore_wait(barrier, 8)
    for i in pieces:
        vx[0][i].start()
        vz[0][i].start()

    @pl.when(jnp.logical_not(late_ay))
    def _():
        for copy in ay:
            copy.start()

    as_.start()
    vs.start()
    for copy in local:
        copy.wait()
    as_.wait_recv()

    @pl.when(far)
    def _():
        for i in pieces:
            start_opp(i)

    left_t[core, 0], left_t[core, 1] = split(left[core].T)
    for i in pieces:
        split_a(first, i)

    @pl.when(near)
    def _():
        for i in pieces:
            split_a(p, i)

    vs.wait_recv()
    left_t[1 - core, 0], left_t[1 - core, 1] = split(left[1 - core].T)
    for i in pieces:
        vx[0][i].wait_recv()
        vxs[0][i].start()
        turn_own(0, i)
        if i == 1:
            @pl.when(late_ay)
            def _():
                for copy in ay:
                    copy.start()

    @pl.when(early_recv)
    def _():
        for i in pieces:
            ay[i].wait_recv()
            ayr[i].start()
            start_opp(i)

    @pl.when(early_relay)
    def _():
        for i in pieces:
            ayr[i].wait_recv()
            start_opp(i)

    for i in pieces:
        vx[1][i].start()
        vz[1][i].start()
    for i in pieces:
        vxs[0][i].wait_recv()
        turn_sibling(0, i)
    for i in pieces:
        vz[0][i].wait_recv()

    def term(t, block):
        return dot3((aparts[block, 0], aparts[block, 1]), split(vbuf[block, t]))

    total = term(0, first)

    def consume(i):
        @pl.when(jnp.logical_not(early_relay))
        def _():
            ayr[i].wait_recv()

        split_a(third, i)

        @pl.when(far)
        def _():
            split_a(p, i)

        vxs[1][i].wait_recv()
        turn_sibling(1, i)

    for i in pieces:
        @pl.when(jnp.logical_not(early_recv))
        def _():
            ay[i].wait_recv()
            ayr[i].start()

        vx[1][i].wait_recv()
        vxs[1][i].start()
        turn_own(1, i)
        if i > 0:
            consume(i - 1)
    for k in range(2):
        @pl.when(core == k)
        def _():
            xo[k].wait_recv()
            xos[k].start()
            split_opp(k)

    for i in pieces:
        @pl.when(owned(i))
        def _():
            zo[i].wait_recv()
            zos[i].start()
            turn_opp(i)

    consume(PIECES - 1)
    total += term(0, p)
    total += term(0, third)
    for k in range(2):
        @pl.when(core != k)
        def _():
            xos[k].wait_recv()
            split_opp(k)

    for i in pieces:
        @pl.when(jnp.logical_not(owned(i)))
        def _():
            zos[i].wait_recv()
            turn_opp(i)

    def images(t, total):
        other = dot3((oparts[0], oparts[1]), split(vbuf[pz, t]))
        return split(total), split(other)

    def block_of(half, start, size, image):
        span = pl.ds(start, size)
        own, other = image
        return dot3((left_t[half, 0, span], left_t[half, 1, span]), own) + dot3(
            (leftx_t[half, 0, span], leftx_t[half, 1, span]), other
        )

    swapped = slot_ref[w // GROUP_WIDE]
    same_flag = (((z + swapped + y) % 2) == 0).astype(jnp.int32)
    home = core == y
    diagonal = x == y

    def each_group(t, skipped, body):
        body(0)
        if t == 0:
            pl.when(jnp.logical_not(skipped))(lambda: body(HALF))
        else:
            body(HALF)

    def send_partials(t, image):
        def group(j):
            block = block_of(1 - x, j * chunk, HALF * chunk, image)
            for k in range(HALF):
                csend[t, j + k] = block[k * chunk : (k + 1) * chunk]
                send_far[t][j + k].start()

        each_group(t, core != x, group)

    def keep_partials(t, image):
        def group(j):
            block = block_of(x, j * chunk, HALF * chunk, image)

            @pl.when(home & (core == t))
            def _():
                for k in range(HALF):
                    near_rows[y, j + k] = block[k * chunk : (k + 1) * chunk]

            @pl.when(jnp.logical_not(home & (core == t)))
            def _():
                for k in range(HALF):
                    ckeep[t, j + k] = block[k * chunk : (k + 1) * chunk]
                    send_near[t][j + k].start()

        each_group(t, core == x, group)

    def gather_rows(j):
        for plane in range(2):
            await_rows(far_rows, 0, plane, j)

            @pl.when(jnp.logical_not(home & (y == plane)))
            def _():
                await_rows(near_rows, 2 * CHUNKS, plane, j)

        same = near_rows[y, j] + far_rows[y, j]
        other = near_rows[1 - y, j] + far_rows[1 - y, j]
        mask = jnp.full(same.shape, same_flag) == 1
        zsend[j] = jnp.where(mask, other, same)
        zc[j].start()
        o_ref[pl.ds(j * chunk, chunk), :] = jnp.where(mask, same, other)

    def finish(j):
        zc[j].wait_recv()
        total = o_ref[pl.ds(j * chunk, chunk), :] + zrecv[j]
        o_ref[pl.ds(j * chunk, chunk), :] = total
        if j < HALF:
            @pl.when(diagonal & (core == 1))
            def _():
                msend[pl.ds(j * chunk, chunk)] = total
                reflect[j].start()

    image = images(0, total)
    send_partials(0, image)
    keep_partials(0, image)
    total = term(1, p) + term(1, px)
    for i in pieces:
        vz[1][i].wait_recv()
    image = images(1, total + term(1, pz))
    send_partials(1, image)
    keep_partials(1, image)

    whole = jnp.logical_not(diagonal & (core == 0))
    for j in range(HALF):
        gather_rows(j)

    @pl.when(whole)
    def _():
        for j in range(HALF, CHUNKS):
            gather_rows(j)

    for j in range(HALF):
        finish(j)

    @pl.when(whole)
    def _():
        for j in range(HALF, CHUNKS):
            finish(j)
            zc[j].wait_send()

    @pl.when(jnp.logical_not(whole))
    def _():
        for copy in reflect:
            copy.wait_recv()
        o_ref[pl.ds(HALF * chunk, HALF * chunk), :] = mirror[...].T

    @pl.when(diagonal & (core == 1))
    def _():
        for copy in reflect:
            copy.wait_send()

    flat = [copy for group in (*vx, *vz, *vxs) for copy in group]
    for copy in (*flat, *ay, *ayr, vs, as_, *zc[:HALF], *send_far[0][:HALF], *send_far[1]):
        copy.wait_send()
    for k in range(2):
        @pl.when(core == k)
        def _():
            xo[k].wait_send()
            xos[k].wait_send()

    for i in pieces:
        @pl.when(owned(i))
        def _():
            zo[i].wait_send()
            zos[i].wait_send()

    @pl.when(core == x)
    def _():
        for copy in send_far[0][HALF:]:
            copy.wait_send()

    for t in range(2):
        @pl.when(jnp.logical_not(home & (core == t)))
        def _():
            for copy in send_near[t][:HALF]:
                copy.wait_send()

            def rest():
                for copy in send_near[t][HALF:]:
                    copy.wait_send()

            if t == 0:
                pl.when(core != x)(rest)
            else:
                rest()


def fast_body(moments, eigen_basis, slot_order):
    rows, cols = moments.shape
    f32 = jnp.float32
    chunk = rows // CHUNKS
    wide_half = cols // 2
    return pl.pallas_call(
        kernel,
        out_shape=jax.ShapeDtypeStruct((rows, wide_half), f32),
        in_specs=[
            pl.BlockSpec(memory_space=pltpu.SMEM),
            pl.BlockSpec(memory_space=pl.ANY),
            pl.BlockSpec(memory_space=pl.ANY),
        ],
        out_specs=pl.BlockSpec(memory_space=pltpu.VMEM),
        scratch_shapes=[
            pltpu.VMEM((4, rows, cols), f32),
            pltpu.VMEM((4, 2, rows, cols), jnp.bfloat16),
            pltpu.VMEM((OVER_X, cols), f32),
            pltpu.VMEM((rows, cols - OVER_X), f32),
            pltpu.VMEM((2, cols, rows), jnp.bfloat16),
            pltpu.VMEM((4, 2, rows, wide_half), f32),
            pltpu.VMEM((2, rows, wide_half), f32),
            pltpu.VMEM((2, rows, cols), f32),
            pltpu.VMEM((2, 2, cols, rows), jnp.bfloat16),
            pltpu.VMEM((2, 2, cols, rows), jnp.bfloat16),
            *[pltpu.VMEM((2, CHUNKS, chunk, wide_half), f32)] * 4,
            *[pltpu.VMEM((CHUNKS, chunk, wide_half), f32)] * 2,
            *[pltpu.VMEM((HALF * chunk, wide_half), f32)] * 2,
            pltpu.SemaphoreType.DMA((4,)),
            pltpu.SemaphoreType.DMA((COPIES,)),
            pltpu.SemaphoreType.DMA((COPIES,)),
        ],
        compiler_params=pltpu.CompilerParams(
            collective_id=0, has_side_effects=True, vmem_limit_bytes=56 * 1024 * 1024
        ),
        name="rayleigh",
    )(slot_order, moments, eigen_basis)


def partner(value, axis, stride):
    mask = 2**stride
    pairs = [(source, source ^ mask) for source in range(lax.axis_size(axis))]
    return lax.ppermute(value, axis, pairs)


def body(moments, eigen_basis, slot_order):
    wide_pos = lax.axis_index("wide")
    subproblem = wide_pos // GROUP_WIDE
    position = wide_pos % GROUP_WIDE
    swapped = lax.dynamic_index_in_dim(slot_order, subproblem, 0, keepdims=False)
    narrow_pos = lax.axis_index("narrow")
    col_count = eigen_basis.shape[1]
    half_cols = col_count // 2
    full_basis = lax.all_gather(eigen_basis, "narrow", axis=1, tiled=True)
    first_half = lax.dynamic_slice_in_dim(full_basis, narrow_pos * half_cols, half_cols, 1)
    second_half = lax.dynamic_slice_in_dim(full_basis, K + narrow_pos * half_cols, half_cols, 1)
    local_panel = jnp.concatenate([first_half, second_half], axis=1)
    pair_block = partner(local_panel, "wide", 0)
    joined = jnp.where(
        position % 2 == 0,
        jnp.concatenate([local_panel, pair_block], axis=0),
        jnp.concatenate([pair_block, local_panel], axis=0),
    )
    quad_block = partner(joined, "wide", 1)
    col_panel = jnp.where(
        position // 2 % 2 == 0,
        jnp.concatenate([joined, quad_block], axis=0),
        jnp.concatenate([quad_block, joined], axis=0),
    )
    products = jnp.dot(
        lax.all_gather(moments, "narrow", axis=1, tiled=True),
        col_panel,
        precision=lax.Precision.HIGHEST,
        preferred_element_type=jnp.float32,
    )
    partials = []
    for slot_index in range(2):
        half_panel = products[:, slot_index * half_cols : (slot_index + 1) * half_cols]
        vectors_half = full_basis[:, slot_index * K : (slot_index + 1) * K]
        partials.append(
            lax.dot_general(
                vectors_half,
                half_panel,
                (((0,), (0,)), ((), ())),
                precision=lax.Precision.HIGHEST,
                preferred_element_type=jnp.float32,
            )
        )
    stacked = jnp.stack(partials)
    slot_pick = (position // 2 + swapped) % 2
    row_part = position % 2
    summed = stacked + partner(stacked, "wide", 0)
    summed = summed + partner(summed, "wide", 1)
    chosen = lax.dynamic_index_in_dim(summed, slot_pick, 0, keepdims=False)
    return lax.dynamic_slice_in_dim(chosen, row_part * (K // 2), K // 2, 0)


def solution(mesh):
    placed = (P("wide", "narrow"), P("wide", "narrow"), P())
    cube = mesh.shape["narrow"] == 4
    return jax.shard_map(
        fast_body if cube else body, mesh=mesh, in_specs=placed, out_specs=P("wide", "narrow"), check_vma=False
    )
```

```python
import jax
import jax.numpy as jnp
from jax import lax
from jax.experimental import pallas as pl
from jax.experimental.pallas import tpu as pltpu
from jax.sharding import PartitionSpec as P

GROUP_WIDE = 4
K = 1024
MESH = pl.DeviceIdType.MESH
CHUNKS = 8
HALF = CHUNKS // 2
PIECES = 4
OVER_X = 256
AHEAD = 1
COPIES = 10 * PIECES + 6 + 2 * PIECES + 4 * CHUNKS + 4 * CHUNKS + CHUNKS + HALF


def split(value):
    high = value.astype(jnp.bfloat16)
    low = (value - high.astype(jnp.float32)).astype(jnp.bfloat16)
    return high, low


def dot3(left, right):
    def dot(a, b):
        return jnp.dot(a, b, preferred_element_type=jnp.float32)

    return dot(left[0], right[0]) + (dot(left[0], right[1]) + dot(left[1], right[0]))


def kernel(
    slot_ref, a_ref, v_ref, o_ref,
    abuf, aparts, opp_x, opp_z, oparts, vbuf, sibling_x, left, left_t, leftx_t,
    partials, rows_in, zsend, zrecv, msend, mirror, obuf,
    local_sem, out_sem, send_sem, recv_sem,
):
    rows, cols = a_ref.shape
    wide_half = cols // 2
    piece = rows // PIECES
    chunk = rows // CHUNKS
    w = lax.axis_index("wide")
    n = lax.axis_index("narrow")
    x = w % 2
    z = (w // 2) % 2
    y = n // 2
    core = n % 2
    p = w % 4
    wx = w + 1 - 2 * x
    wz = w + 2 - 4 * z
    px = p + 1 - 2 * x
    pz = p + 2 - 4 * z
    pd = 3 - p
    ns = n + 1 - 2 * core
    ny = n + 2 - 4 * y
    q = 2 * y + core
    qy = 2 * (1 - y) + core
    near = z == y
    far = z != y
    third = jnp.where(near, pz, px)
    first = jnp.where(near, px, pz)

    barrier = pltpu.get_barrier_semaphore()
    for target in ((wz, n), (w, ns), (w, ny), (w, 3 - n), *((wx, m) for m in range(4))):
        pl.semaphore_signal(barrier, inc=1, device_id=target, device_id_type=MESH)

    def part(i):
        return pl.ds(i * piece, piece)

    def side(t):
        return pl.ds(t * wide_half, wide_half)

    local = [
        pltpu.make_async_copy(v_ref, left.at[core], local_sem.at[0]),
        pltpu.make_async_copy(a_ref, abuf.at[q], local_sem.at[1]),
        pltpu.make_async_copy(v_ref.at[:, side(0)], vbuf.at[p, 0], local_sem.at[2]),
        pltpu.make_async_copy(v_ref.at[:, side(1)], vbuf.at[p, 1], local_sem.at[3]),
    ]
    for copy in local:
        copy.start()

    used = []

    def remote(src, dst, target, arrival=None):
        index = len(used)
        used.append(index)
        return pltpu.make_async_remote_copy(
            src_ref=src, dst_ref=dst, send_sem=send_sem.at[index], recv_sem=recv_sem.at[index if arrival is None else arrival],
            device_id=target, device_id_type=MESH,
        )

    pieces = range(PIECES)
    vx = [[remote(v_ref.at[part(i), side(t)], vbuf.at[p, t, part(i)], (wx, n)) for i in pieces] for t in range(2)]
    vz = [[remote(v_ref.at[part(i), side(t)], vbuf.at[p, t, part(i)], (wz, n)) for i in pieces] for t in range(2)]
    vxs = [[remote(vbuf.at[px, t, part(i)], sibling_x.at[t, part(i)], (w, ns)) for i in pieces] for t in range(2)]
    ay = [remote(a_ref.at[part(i)], abuf.at[q, part(i)], (w, ny)) for i in pieces]
    ayr = [remote(abuf.at[qy, part(i)], abuf.at[qy, part(i)], (w, ns)) for i in pieces]
    quarter = OVER_X // 2
    turned = pl.ds(OVER_X, cols - OVER_X)
    xo = [remote(abuf.at[pd, pl.ds(k * quarter, quarter)], opp_x.at[pl.ds(k * quarter, quarter)], (wx, n)) for k in range(2)]
    xos = [remote(opp_x.at[pl.ds(k * quarter, quarter)], opp_x.at[pl.ds(k * quarter, quarter)], (w, ns)) for k in range(2)]
    zo = [remote(abuf.at[pd, part(i), turned], opp_z.at[part(i)], (wz, n)) for i in pieces]
    zos = [remote(opp_z.at[part(i)], opp_z.at[part(i)], (w, ns)) for i in pieces]
    vs = remote(v_ref, left.at[core], (w, ns))
    as_ = remote(a_ref, abuf.at[q], (w, ns))
    arrivals = len(used)
    used.extend(range(arrivals, arrivals + 4 * CHUNKS))
    steps = range(CHUNKS)
    outside = core != y
    lead = jnp.where(outside, x, 1 - x)
    halves = (lead, 1 - lead)
    same_x = (outside.astype(jnp.int32), 1 - outside.astype(jnp.int32))
    sends = [
        [
            [
                remote(
                    partials.at[t, s, j], rows_in.at[1 - same_x[s], y, j],
                    (jnp.where(same_x[s] == 1, w, wx), 2 * core + t), arrivals + (2 * (1 - same_x[s]) + y) * CHUNKS + j,
                )
                for j in steps
            ]
            for s in range(2)
        ]
        for t in range(2)
    ]
    zc = [remote(zsend.at[j], zrecv.at[j], (wz, n)) for j in steps]
    reflect = [remote(msend.at[pl.ds(j * chunk, chunk)], mirror.at[pl.ds(j * chunk, chunk)], (w, ns)) for j in range(HALF)]
    leave = [pltpu.make_async_copy(obuf.at[pl.ds(j * chunk, chunk)], o_ref.at[pl.ds(j * chunk, chunk)], out_sem.at[j]) for j in steps]

    def await_rows(apart, plane, j):
        pltpu.make_async_remote_copy(
            src_ref=partials.at[0, 0, j], dst_ref=rows_in.at[apart, plane, j], send_sem=send_sem.at[0],
            recv_sem=recv_sem.at[arrivals + (2 * apart + plane) * CHUNKS + j], device_id=(w, ns), device_id_type=MESH,
        ).wait_recv()

    def owned(i):
        return core == i // (PIECES // 2)

    def split_a(block, i):
        value = abuf[block, i * piece : (i + 1) * piece, :]
        high, low = split(value)
        aparts[block, 0, i * piece : (i + 1) * piece, :] = high
        aparts[block, 1, i * piece : (i + 1) * piece, :] = low

    def turn_left(half, t, i, value):
        high, low = split(value.T)
        leftx_t[half, 0, t * wide_half : (t + 1) * wide_half, i * piece : (i + 1) * piece] = high
        leftx_t[half, 1, t * wide_half : (t + 1) * wide_half, i * piece : (i + 1) * piece] = low

    def turn_own(t, i):
        turn_left(core, t, i, vbuf[px, t, i * piece : (i + 1) * piece, :])

    def turn_sibling(t, i):
        turn_left(1 - core, t, i, sibling_x[t, i * piece : (i + 1) * piece, :])

    def turn_opp(i):
        high, low = split(opp_z[i * piece : (i + 1) * piece, :].T)
        oparts[0, OVER_X:, i * piece : (i + 1) * piece] = high
        oparts[1, OVER_X:, i * piece : (i + 1) * piece] = low

    def split_opp(k):
        high, low = split(opp_x[k * quarter : (k + 1) * quarter, :])
        oparts[0, k * quarter : (k + 1) * quarter, :] = high
        oparts[1, k * quarter : (k + 1) * quarter, :] = low

    def start_opp(i):
        for k in range(2):
            if ((k + 1) * quarter - 1) // piece == i:
                @pl.when(core == k)
                def _():
                    xo[k].start()

        @pl.when(owned(i))
        def _():
            zo[i].start()

    late_ay = far & (core == x)
    early_recv = near & (core != x)
    early_relay = near & (core == x)

    pl.semaphore_wait(barrier, 8)
    for i in pieces:
        vx[0][i].start()
        vz[0][i].start()

    @pl.when(jnp.logical_not(late_ay))
    def _():
        for copy in ay:
            copy.start()

    as_.start()
    vs.start()
    for i in range(AHEAD):
        vx[1][i].start()
        vz[1][i].start()
    for copy in local:
        copy.wait()
    as_.wait_recv()

    @pl.when(far)
    def _():
        for i in pieces:
            start_opp(i)

    left_t[core, 0], left_t[core, 1] = split(left[core].T)
    for i in pieces:
        split_a(first, i)

    @pl.when(near)
    def _():
        for i in pieces:
            split_a(p, i)

    vs.wait_recv()
    left_t[1 - core, 0], left_t[1 - core, 1] = split(left[1 - core].T)
    for i in pieces:
        vx[0][i].wait_recv()
        vxs[0][i].start()
        turn_own(0, i)
        if i == 1:
            @pl.when(late_ay)
            def _():
                for copy in ay:
                    copy.start()

    @pl.when(early_recv)
    def _():
        for i in pieces:
            ay[i].wait_recv()
            ayr[i].start()
            start_opp(i)

    @pl.when(early_relay)
    def _():
        for i in pieces:
            ayr[i].wait_recv()
            start_opp(i)

    for i in range(AHEAD, PIECES):
        vx[1][i].start()
        vz[1][i].start()
    for i in pieces:
        vxs[0][i].wait_recv()
        turn_sibling(0, i)
    for i in pieces:
        vz[0][i].wait_recv()

    def term(t, block):
        return dot3((aparts[block, 0], aparts[block, 1]), split(vbuf[block, t]))

    total = term(0, first)

    def consume_x(i):
        vxs[1][i].wait_recv()
        turn_sibling(1, i)

    def forward_x(i):
        vx[1][i].wait_recv()
        vxs[1][i].start()
        turn_own(1, i)

    for i in pieces:
        @pl.when(jnp.logical_not(early_recv))
        def _():
            ay[i].wait_recv()
            ayr[i].start()

        if i < 2:
            forward_x(i)

        @pl.when(jnp.logical_not(early_relay))
        def _():
            ayr[i].wait_recv()

        split_a(third, i)

        @pl.when(far)
        def _():
            split_a(p, i)

        if i < 2:
            consume_x(i)

    for k in range(2):
        @pl.when(core == k)
        def _():
            xo[k].wait_recv()
            xos[k].start()
            split_opp(k)

    for i in pieces:
        @pl.when(owned(i))
        def _():
            zo[i].wait_recv()
            zos[i].start()
            turn_opp(i)

    total += term(0, p)
    total += term(0, third)
    for k in range(2):
        @pl.when(core != k)
        def _():
            xos[k].wait_recv()
            split_opp(k)

    for i in pieces:
        @pl.when(jnp.logical_not(owned(i)))
        def _():
            zos[i].wait_recv()
            turn_opp(i)

    own_image = split(total)
    other_image = split(dot3((oparts[0], oparts[1]), split(vbuf[pz, 0])))

    def block_of(half, start, size, image):
        span = pl.ds(start, size)
        own, other = image
        return dot3((left_t[half, 0, span], left_t[half, 1, span]), own) + dot3(
            (leftx_t[half, 0, span], leftx_t[half, 1, span]), other
        )

    swapped = slot_ref[w // GROUP_WIDE]
    same_flag = (((z + swapped + y) % 2) == 0).astype(jnp.int32)
    local_t = jnp.logical_not(outside)
    diagonal = x == y
    whole = jnp.logical_not(diagonal & (core == 1))

    def needed(t, s, g, body):
        if t == 1 and g == 0:
            pl.when(halves[s] != core)(body)
        else:
            body()

    def send_block(t, s, g, image):
        def body():
            block = block_of(halves[s], g * HALF * chunk, HALF * chunk, image)

            def ship():
                for k in range(HALF):
                    partials[t, s, g * HALF + k] = block[k * chunk : (k + 1) * chunk]
                    sends[t][s][g * HALF + k].start()

            if s == 0:
                ship()
            else:
                pl.when(jnp.logical_not(local_t & (core == t)))(ship)

                @pl.when(local_t & (core == t))
                def _():
                    for k in range(HALF):
                        rows_in[0, y, g * HALF + k] = block[k * chunk : (k + 1) * chunk]

        needed(t, s, g, body)

    def drain_block(t, s, g):
        def body():
            for k in range(HALF):
                sends[t][s][g * HALF + k].wait_send()

        def drain():
            if s == 0:
                body()
            else:
                pl.when(jnp.logical_not(local_t & (core == t)))(body)

        needed(t, s, g, drain)

    def gather_rows(j):
        for plane in range(2):
            await_rows(1, plane, j)

            @pl.when(jnp.logical_not(local_t & (y == plane)))
            def _():
                await_rows(0, plane, j)

        same = rows_in[0, y, j] + rows_in[1, y, j]
        other = rows_in[0, 1 - y, j] + rows_in[1, 1 - y, j]
        mask = jnp.full(same.shape, same_flag) == 1
        zsend[j] = jnp.where(mask, other, same)
        zc[j].start()
        obuf[pl.ds(j * chunk, chunk), :] = jnp.where(mask, same, other)

    def finish(j):
        zc[j].wait_recv()
        total = obuf[pl.ds(j * chunk, chunk), :] + zrecv[j]
        obuf[pl.ds(j * chunk, chunk), :] = total
        leave[j].start()
        if j >= HALF:
            @pl.when(diagonal & (core == 0))
            def _():
                msend[pl.ds((j - HALF) * chunk, chunk)] = total
                reflect[j - HALF].start()

    image = (own_image, other_image)
    for s in range(2):
        send_block(0, s, 0, image)
    for i in range(2, PIECES):
        forward_x(i)
    for i in range(2, PIECES):
        consume_x(i)
    for s in range(2):
        send_block(0, s, 1, image)
    total = term(1, p) + term(1, px)

    def half_term(left, t, k):
        span = pl.ds(k * wide_half, wide_half)
        return dot3((left.at[0, :, span][...], left.at[1, :, span][...]), split(vbuf[pz, t, span]))

    other = None
    for k in range(2):
        for i in range(k * PIECES // 2, (k + 1) * PIECES // 2):
            vz[1][i].wait_recv()
        total += half_term(aparts.at[pz], 1, k)
        more = half_term(oparts, 1, k)
        other = more if other is None else other + more
    image = (split(total), split(other))
    for g in range(2):
        for s in range(2):
            send_block(1, s, g, image)

    @pl.when(whole)
    def _():
        for j in range(HALF):
            gather_rows(j)

    for j in range(HALF, CHUNKS):
        gather_rows(j)

    @pl.when(whole)
    def _():
        for j in range(HALF):
            finish(j)
            zc[j].wait_send()

    for j in range(HALF, CHUNKS):
        finish(j)

    @pl.when(jnp.logical_not(whole))
    def _():
        for copy in reflect:
            copy.wait_recv()
        obuf[pl.ds(0, HALF * chunk), :] = mirror[...].T
        for j in range(HALF):
            leave[j].start()

    @pl.when(diagonal & (core == 0))
    def _():
        for copy in reflect:
            copy.wait_send()

    flat = [copy for group in (*vx, *vz, *vxs) for copy in group]
    for copy in (*flat, *ay, *ayr, vs, as_, *zc[HALF:]):
        copy.wait_send()
    for k in range(2):
        @pl.when(core == k)
        def _():
            xo[k].wait_send()
            xos[k].wait_send()

    for i in pieces:
        @pl.when(owned(i))
        def _():
            zo[i].wait_send()
            zos[i].wait_send()

    for t in range(2):
        for s in range(2):
            for g in range(2):
                drain_block(t, s, g)
    for copy in leave:
        copy.wait()


def fast_body(moments, eigen_basis, slot_order):
    rows, cols = moments.shape
    f32 = jnp.float32
    chunk = rows // CHUNKS
    wide_half = cols // 2
    return pl.pallas_call(
        kernel,
        out_shape=jax.ShapeDtypeStruct((rows, wide_half), f32),
        in_specs=[
            pl.BlockSpec(memory_space=pltpu.SMEM),
            pl.BlockSpec(memory_space=pl.ANY),
            pl.BlockSpec(memory_space=pl.ANY),
        ],
        out_specs=pl.BlockSpec(memory_space=pl.ANY),
        scratch_shapes=[
            pltpu.VMEM((4, rows, cols), f32),
            pltpu.VMEM((4, 2, rows, cols), jnp.bfloat16),
            pltpu.VMEM((OVER_X, cols), f32),
            pltpu.VMEM((rows, cols - OVER_X), f32),
            pltpu.VMEM((2, cols, rows), jnp.bfloat16),
            pltpu.VMEM((4, 2, rows, wide_half), f32),
            pltpu.VMEM((2, rows, wide_half), f32),
            pltpu.VMEM((2, rows, cols), f32),
            pltpu.VMEM((2, 2, cols, rows), jnp.bfloat16),
            pltpu.VMEM((2, 2, cols, rows), jnp.bfloat16),
            *[pltpu.VMEM((2, 2, CHUNKS, chunk, wide_half), f32)] * 2,
            *[pltpu.VMEM((CHUNKS, chunk, wide_half), f32)] * 2,
            *[pltpu.VMEM((HALF * chunk, wide_half), f32)] * 2,
            pltpu.VMEM((rows, wide_half), f32),
            pltpu.SemaphoreType.DMA((4,)),
            pltpu.SemaphoreType.DMA((CHUNKS,)),
            pltpu.SemaphoreType.DMA((COPIES,)),
            pltpu.SemaphoreType.DMA((COPIES,)),
        ],
        compiler_params=pltpu.CompilerParams(
            collective_id=0, has_side_effects=True, vmem_limit_bytes=56 * 1024 * 1024
        ),
        name="rayleigh",
    )(slot_order, moments, eigen_basis)


def partner(value, axis, stride):
    mask = 2**stride
    pairs = [(source, source ^ mask) for source in range(lax.axis_size(axis))]
    return lax.ppermute(value, axis, pairs)


def body(moments, eigen_basis, slot_order):
    wide_pos = lax.axis_index("wide")
    subproblem = wide_pos // GROUP_WIDE
    position = wide_pos % GROUP_WIDE
    swapped = lax.dynamic_index_in_dim(slot_order, subproblem, 0, keepdims=False)
    narrow_pos = lax.axis_index("narrow")
    col_count = eigen_basis.shape[1]
    half_cols = col_count // 2
    full_basis = lax.all_gather(eigen_basis, "narrow", axis=1, tiled=True)
    first_half = lax.dynamic_slice_in_dim(full_basis, narrow_pos * half_cols, half_cols, 1)
    second_half = lax.dynamic_slice_in_dim(full_basis, K + narrow_pos * half_cols, half_cols, 1)
    local_panel = jnp.concatenate([first_half, second_half], axis=1)
    pair_block = partner(local_panel, "wide", 0)
    joined = jnp.where(
        position % 2 == 0,
        jnp.concatenate([local_panel, pair_block], axis=0),
        jnp.concatenate([pair_block, local_panel], axis=0),
    )
    quad_block = partner(joined, "wide", 1)
    col_panel = jnp.where(
        position // 2 % 2 == 0,
        jnp.concatenate([joined, quad_block], axis=0),
        jnp.concatenate([quad_block, joined], axis=0),
    )
    products = jnp.dot(
        lax.all_gather(moments, "narrow", axis=1, tiled=True),
        col_panel,
        precision=lax.Precision.HIGHEST,
        preferred_element_type=jnp.float32,
    )
    partials = []
    for slot_index in range(2):
        half_panel = products[:, slot_index * half_cols : (slot_index + 1) * half_cols]
        vectors_half = full_basis[:, slot_index * K : (slot_index + 1) * K]
        partials.append(
            lax.dot_general(
                vectors_half,
                half_panel,
                (((0,), (0,)), ((), ())),
                precision=lax.Precision.HIGHEST,
                preferred_element_type=jnp.float32,
            )
        )
    stacked = jnp.stack(partials)
    slot_pick = (position // 2 + swapped) % 2
    row_part = position % 2
    summed = stacked + partner(stacked, "wide", 0)
    summed = summed + partner(summed, "wide", 1)
    chosen = lax.dynamic_index_in_dim(summed, slot_pick, 0, keepdims=False)
    return lax.dynamic_slice_in_dim(chosen, row_part * (K // 2), K // 2, 0)


def solution(mesh):
    placed = (P("wide", "narrow"), P("wide", "narrow"), P())
    cube = mesh.shape["narrow"] == 4
    return jax.shard_map(
        fast_body if cube else body, mesh=mesh, in_specs=placed, out_specs=P("wide", "narrow"), check_vma=False
    )
```

```python
import jax
import jax.numpy as jnp
from jax import lax
from jax.experimental import pallas as pl
from jax.experimental.pallas import tpu as pltpu
from jax.sharding import PartitionSpec as P

GROUP_WIDE = 4
K = 1024
MESH = pl.DeviceIdType.MESH
CHUNKS = 8
HALF = CHUNKS // 2
PIECES = 4
OVER_X = 256
AHEAD = 1
SENDS = 22
RECVS = 52


def split(value):
    high = value.astype(jnp.bfloat16)
    low = (value - high.astype(jnp.float32)).astype(jnp.bfloat16)
    return high, low


def dot3(left, right):
    def dot(a, b):
        return jnp.dot(a, b, preferred_element_type=jnp.float32)

    return dot(left[0], right[0]) + (dot(left[0], right[1]) + dot(left[1], right[0]))


def kernel(
    slot_ref, a_ref, v_ref, o_ref,
    abuf, aparts, opp_x, opp_z, oparts, vbuf, sibling_x, left, left_t, leftx_t,
    partials, rows_in, zsend, zrecv, msend, mirror, obuf,
    local_sem, out_sem, send_sem, recv_sem,
):
    rows, cols = a_ref.shape
    wide_half = cols // 2
    piece = rows // PIECES
    chunk = rows // CHUNKS
    w = lax.axis_index("wide")
    n = lax.axis_index("narrow")
    x = w % 2
    z = (w // 2) % 2
    y = n // 2
    core = n % 2
    p = w % 4
    wx = w + 1 - 2 * x
    wz = w + 2 - 4 * z
    px = p + 1 - 2 * x
    pz = p + 2 - 4 * z
    pd = 3 - p
    ns = n + 1 - 2 * core
    ny = n + 2 - 4 * y
    q = 2 * y + core
    qy = 2 * (1 - y) + core
    near = z == y
    far = z != y
    third = jnp.where(near, pz, px)
    first = jnp.where(near, px, pz)

    barrier = pltpu.get_barrier_semaphore()
    for target in ((wz, n), (w, ns), (w, ny), (w, 3 - n), *((wx, m) for m in range(4))):
        pl.semaphore_signal(barrier, inc=1, device_id=target, device_id_type=MESH)

    def part(i):
        return pl.ds(i * piece, piece)

    def side(t):
        return pl.ds(t * wide_half, wide_half)

    local = [
        pltpu.make_async_copy(v_ref, left.at[core], local_sem.at[0]),
        pltpu.make_async_copy(a_ref, abuf.at[q], local_sem.at[1]),
        pltpu.make_async_copy(v_ref.at[:, side(0)], vbuf.at[p, 0], local_sem.at[2]),
        pltpu.make_async_copy(v_ref.at[:, side(1)], vbuf.at[p, 1], local_sem.at[3]),
    ]
    for copy in local:
        copy.start()

    taken = [0, 0]
    origin = []

    def fresh(kind, count=1):
        start = taken[kind]
        taken[kind] += count
        return start

    def remote(src, dst, target, send, recv):
        copy = pltpu.make_async_remote_copy(
            src_ref=src, dst_ref=dst, send_sem=send_sem.at[send], recv_sem=recv_sem.at[recv],
            device_id=target, device_id_type=MESH,
        )
        origin.append((copy, send))
        return copy

    def family(make, count, arrivals):
        send, recv = fresh(0), fresh(1, max(arrivals) + 1)
        return [remote(*make(i), send, recv + arrivals[i]) for i in range(count)]

    pieces = range(PIECES)
    each = list(pieces)
    half_each = [i % (PIECES // 2) for i in pieces]
    pairs = [(t, i) for t in range(2) for i in pieces]

    def both(flat):
        return [flat[:PIECES], flat[PIECES:]]

    def basis(i, target):
        t, k = pairs[i]
        return v_ref.at[part(k), side(t)], vbuf.at[p, t, part(k)], target

    def shared_x(i):
        t, k = pairs[i]
        return vbuf.at[px, t, part(k)], sibling_x.at[t, part(k)], (w, ns)

    count = 2 * PIECES
    vx = both(family(lambda i: basis(i, (wx, n)), count, list(range(count))))
    z_arrivals = [0] * PIECES + [1 + 2 * i // PIECES for i in pieces]
    taken_z = taken[1]
    vz = both(family(lambda i: basis(i, (wz, n)), count, z_arrivals))
    vxs = both(family(shared_x, count, list(range(count))))
    ay = family(lambda i: (a_ref.at[part(i)], abuf.at[q, part(i)], (w, ny)), PIECES, each)
    ayr = family(lambda i: (abuf.at[qy, part(i)], abuf.at[qy, part(i)], (w, ns)), PIECES, each)
    quarter = OVER_X // 2
    turned = pl.ds(OVER_X, cols - OVER_X)

    def rows_x(k):
        return pl.ds(k * quarter, quarter)

    xo = family(lambda k: (abuf.at[pd, rows_x(k)], opp_x.at[rows_x(k)], (wx, n)), 2, [0, 0])
    xos = family(lambda k: (opp_x.at[rows_x(k)], opp_x.at[rows_x(k)], (w, ns)), 2, [0, 0])
    zo = family(lambda i: (abuf.at[pd, part(i), turned], opp_z.at[part(i)], (wz, n)), PIECES, half_each)
    zos = family(lambda i: (opp_z.at[part(i)], opp_z.at[part(i)], (w, ns)), PIECES, half_each)
    vs = family(lambda i: (v_ref, left.at[core], (w, ns)), 1, [0])[0]
    as_ = family(lambda i: (a_ref, abuf.at[q], (w, ns)), 1, [0])[0]
    steps = range(CHUNKS)
    arrivals = fresh(1, CHUNKS)
    outside = core != y
    lead = jnp.where(outside, x, 1 - x)
    halves = (lead, 1 - lead)
    same_x = (outside.astype(jnp.int32), 1 - outside.astype(jnp.int32))
    block_sends = fresh(0, 8)
    sends = [
        [
            [
                remote(
                    partials.at[t, s, j], rows_in.at[2 * (1 - same_x[s]) + y, j],
                    (jnp.where(same_x[s] == 1, w, wx), 2 * core + t), block_sends + 4 * t + 2 * s + j // HALF, arrivals + j,
                )
                for j in steps
            ]
            for s in range(2)
        ]
        for t in range(2)
    ]
    z_sends, z_recvs = fresh(0, 2), fresh(1, CHUNKS)
    zc = [remote(zsend.at[j], zrecv.at[j], (wz, n), z_sends + j // HALF, z_recvs + j) for j in steps]
    reflect_send, reflect_recv = fresh(0), fresh(1)
    reflect = [
        remote(msend.at[pl.ds(j * chunk, chunk)], mirror.at[pl.ds(j * chunk, chunk)], (w, ns), reflect_send, reflect_recv)
        for j in range(HALF)
    ]
    leave = [
        pltpu.make_async_copy(obuf.at[pl.ds(j * chunk, chunk)], o_ref.at[pl.ds(j * chunk, chunk)], out_sem.at[j // HALF])
        for j in steps
    ]

    def all_sent(copies, ref):
        send = next(index for copy, index in origin if copy is copies[0])
        pltpu.make_async_remote_copy(
            src_ref=ref, dst_ref=ref, send_sem=send_sem.at[send], recv_sem=recv_sem.at[0], device_id=(w, ns), device_id_type=MESH,
        ).wait_send()

    def all_here(recv, ref):
        pltpu.make_async_remote_copy(
            src_ref=ref, dst_ref=ref, send_sem=send_sem.at[0], recv_sem=recv_sem.at[recv], device_id=(w, ns), device_id_type=MESH,
        ).wait_recv()

    def owned(i):
        return core == i // (PIECES // 2)

    def split_a(block, i):
        value = abuf[block, i * piece : (i + 1) * piece, :]
        high, low = split(value)
        aparts[block, 0, i * piece : (i + 1) * piece, :] = high
        aparts[block, 1, i * piece : (i + 1) * piece, :] = low

    def turn_left(half, t, i, value):
        high, low = split(value.T)
        leftx_t[half, 0, t * wide_half : (t + 1) * wide_half, i * piece : (i + 1) * piece] = high
        leftx_t[half, 1, t * wide_half : (t + 1) * wide_half, i * piece : (i + 1) * piece] = low

    def turn_own(t, i):
        turn_left(core, t, i, vbuf[px, t, i * piece : (i + 1) * piece, :])

    def turn_sibling(t, i):
        turn_left(1 - core, t, i, sibling_x[t, i * piece : (i + 1) * piece, :])

    def turn_opp(i):
        high, low = split(opp_z[i * piece : (i + 1) * piece, :].T)
        oparts[0, OVER_X:, i * piece : (i + 1) * piece] = high
        oparts[1, OVER_X:, i * piece : (i + 1) * piece] = low

    def split_opp(k):
        high, low = split(opp_x[k * quarter : (k + 1) * quarter, :])
        oparts[0, k * quarter : (k + 1) * quarter, :] = high
        oparts[1, k * quarter : (k + 1) * quarter, :] = low

    def start_opp(i):
        for k in range(2):
            if ((k + 1) * quarter - 1) // piece == i:
                @pl.when(core == k)
                def _():
                    xo[k].start()

        @pl.when(owned(i))
        def _():
            zo[i].start()

    late_ay = far & (core == x)
    early_recv = near & (core != x)
    early_relay = near & (core == x)

    pl.semaphore_wait(barrier, 8)
    for i in pieces:
        vx[0][i].start()
        vz[0][i].start()

    @pl.when(jnp.logical_not(late_ay))
    def _():
        for copy in ay:
            copy.start()

    as_.start()
    vs.start()
    for i in range(AHEAD):
        vx[1][i].start()
        vz[1][i].start()
    for copy in local:
        copy.wait()
    as_.wait_recv()

    @pl.when(far)
    def _():
        for i in pieces:
            start_opp(i)

    left_t[core, 0], left_t[core, 1] = split(left[core].T)
    for i in pieces:
        split_a(first, i)

    @pl.when(near)
    def _():
        for i in pieces:
            split_a(p, i)

    vs.wait_recv()
    left_t[1 - core, 0], left_t[1 - core, 1] = split(left[1 - core].T)
    for i in pieces:
        vx[0][i].wait_recv()
        vxs[0][i].start()
        turn_own(0, i)
        if i == 1:
            @pl.when(late_ay)
            def _():
                for copy in ay:
                    copy.start()

    @pl.when(early_recv)
    def _():
        for i in pieces:
            ay[i].wait_recv()
            ayr[i].start()
            start_opp(i)

    @pl.when(early_relay)
    def _():
        for i in pieces:
            ayr[i].wait_recv()
            start_opp(i)

    for i in range(AHEAD, PIECES):
        vx[1][i].start()
        vz[1][i].start()
    for i in pieces:
        vxs[0][i].wait_recv()
        turn_sibling(0, i)
    all_here(taken_z, vbuf.at[pz, 0])

    def term(t, block):
        return dot3((aparts[block, 0], aparts[block, 1]), split(vbuf[block, t]))

    total = term(0, first)
    right_p = split(vbuf[p, 0])
    right_third = split(vbuf[third, 0])

    def consume_x(i):
        vxs[1][i].wait_recv()
        turn_sibling(1, i)

    def forward_x(i):
        vx[1][i].wait_recv()
        vxs[1][i].start()
        turn_own(1, i)

    images = []

    def finish_rows(i):
        @pl.when(jnp.logical_not(early_recv))
        def _():
            ay[i].wait_recv()
            ayr[i].start()

        @pl.when(jnp.logical_not(early_relay))
        def _():
            ayr[i].wait_recv()

        split_a(third, i)

        @pl.when(far)
        def _():
            split_a(p, i)

        span = part(i)
        value = total[i * piece : (i + 1) * piece]
        value += dot3((aparts[p, 0, span], aparts[p, 1, span]), right_p)
        value += dot3((aparts[third, 0, span], aparts[third, 1, span]), right_third)
        images.append(split(value))

    for i in range(PIECES - 1):
        finish_rows(i)
    for k in range(2):
        @pl.when(core == k)
        def _():
            xo[k].wait_recv()
            xos[k].start()
            split_opp(k)

    for i in pieces:
        @pl.when(owned(i))
        def _():
            zo[i].wait_recv()
            zos[i].start()
            turn_opp(i)

    for i in range(AHEAD):
        forward_x(i)
    finish_rows(PIECES - 1)
    for k in range(2):
        @pl.when(core != k)
        def _():
            xos[k].wait_recv()
            split_opp(k)

    for i in pieces:
        @pl.when(jnp.logical_not(owned(i)))
        def _():
            zos[i].wait_recv()
            turn_opp(i)

    own_image = tuple(jnp.concatenate([pair[k] for pair in images], axis=0) for k in range(2))
    other_image = split(dot3((oparts[0], oparts[1]), split(vbuf[pz, 0])))

    def block_of(half, start, size, image):
        span = pl.ds(start, size)
        own, other = image
        return dot3((left_t[half, 0, span], left_t[half, 1, span]), own) + dot3(
            (leftx_t[half, 0, span], leftx_t[half, 1, span]), other
        )

    swapped = slot_ref[w // GROUP_WIDE]
    same_flag = (((z + swapped + y) % 2) == 0).astype(jnp.int32)
    local_t = jnp.logical_not(outside)
    diagonal = x == y
    whole = jnp.logical_not(diagonal & (core == 1))

    def needed(t, s, g, body):
        if t == 1 and g == 0:
            pl.when(halves[s] != core)(body)
        else:
            body()

    def send_block(t, s, g, image):
        def body():
            block = block_of(halves[s], g * HALF * chunk, HALF * chunk, image)

            def ship():
                for k in range(HALF):
                    partials[t, s, g * HALF + k] = block[k * chunk : (k + 1) * chunk]
                    sends[t][s][g * HALF + k].start()

            if s == 0:
                ship()
            else:
                pl.when(jnp.logical_not(local_t & (core == t)))(ship)

                @pl.when(local_t & (core == t))
                def _():
                    for k in range(HALF):
                        rows_in[y, g * HALF + k] = block[k * chunk : (k + 1) * chunk]

        needed(t, s, g, body)

    def drain_block(t, s, g):
        def body():
            group = pl.ds(g * HALF, HALF)
            all_sent(sends[t][s][g * HALF :], partials.at[t, s, group])

        def drain():
            if s == 0:
                body()
            else:
                pl.when(jnp.logical_not(local_t & (core == t)))(body)

        needed(t, s, g, drain)

    def gather_rows(j):
        @pl.when(local_t)
        def _():
            all_here(arrivals + j, rows_in.at[pl.ds(0, 3), j])

        @pl.when(outside)
        def _():
            all_here(arrivals + j, rows_in.at[:, j])

        same = rows_in[y, j] + rows_in[2 + y, j]
        other = rows_in[1 - y, j] + rows_in[3 - y, j]
        mask = jnp.full(same.shape, same_flag) == 1
        zsend[j] = jnp.where(mask, other, same)
        zc[j].start()
        obuf[pl.ds(j * chunk, chunk), :] = jnp.where(mask, same, other)

    def finish(j):
        zc[j].wait_recv()
        total = obuf[pl.ds(j * chunk, chunk), :] + zrecv[j]
        obuf[pl.ds(j * chunk, chunk), :] = total
        leave[j].start()
        if j >= HALF:
            @pl.when(diagonal & (core == 0))
            def _():
                msend[pl.ds((j - HALF) * chunk, chunk)] = total
                reflect[j - HALF].start()

    image = (own_image, other_image)
    for s in range(2):
        send_block(0, s, 0, image)
    for i in range(AHEAD, PIECES):
        forward_x(i)
    for i in pieces:
        consume_x(i)
    for s in range(2):
        send_block(0, s, 1, image)
    total = term(1, p) + term(1, px)

    def half_term(left, t, k):
        span = pl.ds(k * wide_half, wide_half)
        return dot3((left.at[0, :, span][...], left.at[1, :, span][...]), split(vbuf[pz, t, span]))

    other = None
    for k in range(2):
        all_here(taken_z + 1 + k, vbuf.at[pz, 1, pl.ds(k * wide_half, wide_half)])
        total += half_term(aparts.at[pz], 1, k)
        more = half_term(oparts, 1, k)
        other = more if other is None else other + more
    image = (split(total), split(other))
    for g in range(2):
        for s in range(2):
            send_block(1, s, g, image)

    @pl.when(whole)
    def _():
        for j in range(HALF):
            gather_rows(j)

    for j in range(HALF, CHUNKS):
        gather_rows(j)

    @pl.when(whole)
    def _():
        for j in range(HALF):
            finish(j)
        all_sent(zc[:HALF], zsend.at[pl.ds(0, HALF)])

    for j in range(HALF, CHUNKS):
        finish(j)

    @pl.when(jnp.logical_not(whole))
    def _():
        all_here(reflect_recv, mirror)
        obuf[pl.ds(0, HALF * chunk), :] = mirror[...].T
        for j in range(HALF):
            leave[j].start()

    @pl.when(diagonal & (core == 0))
    def _():
        all_sent(reflect, msend)

    for copies in (vx[0], vz[0], vxs[0], ay, ayr, [vs], [as_]):
        all_sent(copies, abuf.at[0])
    all_sent(xo, opp_x.at[pl.ds(0, quarter)])
    all_sent(xos, opp_x.at[pl.ds(0, quarter)])
    all_sent(zo, opp_z.at[pl.ds(0, rows // 2)])
    all_sent(zos, opp_z.at[pl.ds(0, rows // 2)])
    all_sent(zc[HALF:], zsend.at[pl.ds(HALF, HALF)])
    for t in range(2):
        for s in range(2):
            for g in range(2):
                drain_block(t, s, g)
    for g in range(2):
        group = pl.ds(g * HALF * chunk, HALF * chunk)
        pltpu.make_async_copy(obuf.at[group], o_ref.at[group], out_sem.at[g]).wait()


def fast_body(moments, eigen_basis, slot_order):
    rows, cols = moments.shape
    f32 = jnp.float32
    chunk = rows // CHUNKS
    wide_half = cols // 2
    return pl.pallas_call(
        kernel,
        out_shape=jax.ShapeDtypeStruct((rows, wide_half), f32),
        in_specs=[
            pl.BlockSpec(memory_space=pltpu.SMEM),
            pl.BlockSpec(memory_space=pl.ANY),
            pl.BlockSpec(memory_space=pl.ANY),
        ],
        out_specs=pl.BlockSpec(memory_space=pl.ANY),
        scratch_shapes=[
            pltpu.VMEM((4, rows, cols), f32),
            pltpu.VMEM((4, 2, rows, cols), jnp.bfloat16),
            pltpu.VMEM((OVER_X, cols), f32),
            pltpu.VMEM((rows, cols - OVER_X), f32),
            pltpu.VMEM((2, cols, rows), jnp.bfloat16),
            pltpu.VMEM((4, 2, rows, wide_half), f32),
            pltpu.VMEM((2, rows, wide_half), f32),
            pltpu.VMEM((2, rows, cols), f32),
            pltpu.VMEM((2, 2, cols, rows), jnp.bfloat16),
            pltpu.VMEM((2, 2, cols, rows), jnp.bfloat16),
            pltpu.VMEM((2, 2, CHUNKS, chunk, wide_half), f32),
            pltpu.VMEM((4, CHUNKS, chunk, wide_half), f32),
            *[pltpu.VMEM((CHUNKS, chunk, wide_half), f32)] * 2,
            *[pltpu.VMEM((HALF * chunk, wide_half), f32)] * 2,
            pltpu.VMEM((rows, wide_half), f32),
            pltpu.SemaphoreType.DMA((4,)),
            pltpu.SemaphoreType.DMA((2,)),
            pltpu.SemaphoreType.DMA((SENDS,)),
            pltpu.SemaphoreType.DMA((RECVS,)),
        ],
        compiler_params=pltpu.CompilerParams(
            collective_id=0, has_side_effects=True, vmem_limit_bytes=56 * 1024 * 1024
        ),
        name="rayleigh",
    )(slot_order, moments, eigen_basis)


def partner(value, axis, stride):
    mask = 2**stride
    pairs = [(source, source ^ mask) for source in range(lax.axis_size(axis))]
    return lax.ppermute(value, axis, pairs)


def body(moments, eigen_basis, slot_order):
    wide_pos = lax.axis_index("wide")
    subproblem = wide_pos // GROUP_WIDE
    position = wide_pos % GROUP_WIDE
    swapped = lax.dynamic_index_in_dim(slot_order, subproblem, 0, keepdims=False)
    narrow_pos = lax.axis_index("narrow")
    col_count = eigen_basis.shape[1]
    half_cols = col_count // 2
    full_basis = lax.all_gather(eigen_basis, "narrow", axis=1, tiled=True)
    first_half = lax.dynamic_slice_in_dim(full_basis, narrow_pos * half_cols, half_cols, 1)
    second_half = lax.dynamic_slice_in_dim(full_basis, K + narrow_pos * half_cols, half_cols, 1)
    local_panel = jnp.concatenate([first_half, second_half], axis=1)
    pair_block = partner(local_panel, "wide", 0)
    joined = jnp.where(
        position % 2 == 0,
        jnp.concatenate([local_panel, pair_block], axis=0),
        jnp.concatenate([pair_block, local_panel], axis=0),
    )
    quad_block = partner(joined, "wide", 1)
    col_panel = jnp.where(
        position // 2 % 2 == 0,
        jnp.concatenate([joined, quad_block], axis=0),
        jnp.concatenate([quad_block, joined], axis=0),
    )
    products = jnp.dot(
        lax.all_gather(moments, "narrow", axis=1, tiled=True),
        col_panel,
        precision=lax.Precision.HIGHEST,
        preferred_element_type=jnp.float32,
    )
    partials = []
    for slot_index in range(2):
        half_panel = products[:, slot_index * half_cols : (slot_index + 1) * half_cols]
        vectors_half = full_basis[:, slot_index * K : (slot_index + 1) * K]
        partials.append(
            lax.dot_general(
                vectors_half,
                half_panel,
                (((0,), (0,)), ((), ())),
                precision=lax.Precision.HIGHEST,
                preferred_element_type=jnp.float32,
            )
        )
    stacked = jnp.stack(partials)
    slot_pick = (position // 2 + swapped) % 2
    row_part = position % 2
    summed = stacked + partner(stacked, "wide", 0)
    summed = summed + partner(summed, "wide", 1)
    chosen = lax.dynamic_index_in_dim(summed, slot_pick, 0, keepdims=False)
    return lax.dynamic_slice_in_dim(chosen, row_part * (K // 2), K // 2, 0)


def solution(mesh):
    placed = (P("wide", "narrow"), P("wide", "narrow"), P())
    cube = mesh.shape["narrow"] == 4
    return jax.shard_map(
        fast_body if cube else body, mesh=mesh, in_specs=placed, out_specs=P("wide", "narrow"), check_vma=False
    )
```

```python
import jax
import jax.numpy as jnp
from jax import lax
from jax.experimental import pallas as pl
from jax.experimental.pallas import tpu as pltpu
from jax.sharding import PartitionSpec as P

GROUP_WIDE = 4
K = 1024
MESH = pl.DeviceIdType.MESH
CHUNKS = 8
HALF = CHUNKS // 2
PIECES = 4
OVER_X = 128
AHEAD_X = 1
AHEAD_Z = 0
SENDS = 22
RECVS = 52


def split(value):
    high = value.astype(jnp.bfloat16)
    low = (value - high.astype(jnp.float32)).astype(jnp.bfloat16)
    return high, low


def dot3(left, right):
    def dot(a, b):
        return jnp.dot(a, b, preferred_element_type=jnp.float32)

    return dot(left[0], right[0]) + (dot(left[0], right[1]) + dot(left[1], right[0]))


def kernel(
    slot_ref, a_ref, v_ref, o_ref,
    abuf, aparts, opp_x, opp_z, oparts, vbuf, sibling_x, left, left_t, leftx_t,
    partials, rows_in, zsend, zrecv, msend, mirror, obuf,
    local_sem, out_sem, send_sem, recv_sem,
):
    rows, cols = a_ref.shape
    wide_half = cols // 2
    piece = rows // PIECES
    chunk = rows // CHUNKS
    w = lax.axis_index("wide")
    n = lax.axis_index("narrow")
    x = w % 2
    z = (w // 2) % 2
    y = n // 2
    core = n % 2
    p = w % 4
    wx = w + 1 - 2 * x
    wz = w + 2 - 4 * z
    px = p + 1 - 2 * x
    pz = p + 2 - 4 * z
    pd = 3 - p
    ns = n + 1 - 2 * core
    ny = n + 2 - 4 * y
    q = 2 * y + core
    qy = 2 * (1 - y) + core
    near = z == y
    far = z != y
    third = jnp.where(near, pz, px)
    first = jnp.where(near, px, pz)

    barrier = pltpu.get_barrier_semaphore()
    for target in ((wz, n), (w, ns), (w, ny), (w, 3 - n), *((wx, m) for m in range(4))):
        pl.semaphore_signal(barrier, inc=1, device_id=target, device_id_type=MESH)

    def part(i):
        return pl.ds(i * piece, piece)

    def side(t):
        return pl.ds(t * wide_half, wide_half)

    local = [
        pltpu.make_async_copy(v_ref, left.at[core], local_sem.at[0]),
        pltpu.make_async_copy(a_ref, abuf.at[q], local_sem.at[1]),
        pltpu.make_async_copy(v_ref.at[:, side(0)], vbuf.at[p, 0], local_sem.at[2]),
        pltpu.make_async_copy(v_ref.at[:, side(1)], vbuf.at[p, 1], local_sem.at[3]),
    ]
    for copy in local:
        copy.start()

    taken = [0, 0]
    origin = []

    def fresh(kind, count=1):
        start = taken[kind]
        taken[kind] += count
        return start

    def remote(src, dst, target, send, recv):
        copy = pltpu.make_async_remote_copy(
            src_ref=src, dst_ref=dst, send_sem=send_sem.at[send], recv_sem=recv_sem.at[recv],
            device_id=target, device_id_type=MESH,
        )
        origin.append((copy, send))
        return copy

    def family(make, count, arrivals):
        send, recv = fresh(0), fresh(1, max(arrivals) + 1)
        return [remote(*make(i), send, recv + arrivals[i]) for i in range(count)]

    pieces = range(PIECES)
    each = list(pieces)
    half_each = [i % (PIECES // 2) for i in pieces]
    pairs = [(t, i) for t in range(2) for i in pieces]

    def both(flat):
        return [flat[:PIECES], flat[PIECES:]]

    def basis(i, target):
        t, k = pairs[i]
        return v_ref.at[part(k), side(t)], vbuf.at[p, t, part(k)], target

    def shared_x(i):
        t, k = pairs[i]
        return vbuf.at[px, t, part(k)], sibling_x.at[t, part(k)], (w, ns)

    count = 2 * PIECES
    vx = both(family(lambda i: basis(i, (wx, n)), count, list(range(count))))
    z_arrivals = [0] * PIECES + [1 + 2 * i // PIECES for i in pieces]
    taken_z = taken[1]
    vz = both(family(lambda i: basis(i, (wz, n)), count, z_arrivals))
    vxs = both(family(shared_x, count, list(range(count))))
    quarter = OVER_X // 2
    turned = pl.ds(OVER_X, cols - OVER_X)
    lean_rows = (OVER_X * cols + (rows - OVER_X) * (cols - OVER_X)) // cols
    lean_out = near == (core == x)
    lean_in = far == (core == x)
    lean_relay = far == (core != x)
    ay_sems, ayr_sems = (fresh(0), fresh(1, PIECES)), (fresh(0), fresh(1, PIECES))

    def lean(i):
        return i * piece >= OVER_X

    def moments_y(i, wanted):
        return remote(a_ref.at[part(i), wanted], abuf.at[q, part(i), wanted], (w, ny), ay_sems[0], ay_sems[1] + i)

    def moments_core(i, wanted):
        return remote(abuf.at[qy, part(i), wanted], abuf.at[qy, part(i), wanted], (w, ns), ayr_sems[0], ayr_sems[1] + i)

    full = pl.ds(0, cols)
    ay = [moments_y(i, full) for i in pieces]
    ayr = [moments_core(i, full) for i in pieces]
    ay_lean = [moments_y(i, turned) if lean(i) else ay[i] for i in pieces]
    ayr_lean = [moments_core(i, turned) if lean(i) else ayr[i] for i in pieces]

    def choose(condition, when_true, when_false):
        pl.when(condition)(when_true)
        pl.when(jnp.logical_not(condition))(when_false)

    def start_y(i):
        if lean(i):
            choose(lean_out, ay_lean[i].start, ay[i].start)
        else:
            ay[i].start()

    def relay_y(i):
        if lean(i):
            choose(lean_in, ay_lean[i].wait_recv, ay[i].wait_recv)
            choose(lean_in, ayr_lean[i].start, ayr[i].start)
        else:
            ay[i].wait_recv()
            ayr[i].start()

    def receive_relay(i):
        if lean(i):
            choose(lean_relay, ayr_lean[i].wait_recv, ayr[i].wait_recv)
        else:
            ayr[i].wait_recv()

    def rows_x(k):
        return pl.ds(k * quarter, quarter)

    xo = family(lambda k: (abuf.at[pd, rows_x(k)], opp_x.at[rows_x(k)], (wx, n)), 2, [0, 0])
    xos = family(lambda k: (opp_x.at[rows_x(k)], opp_x.at[rows_x(k)], (w, ns)), 2, [0, 0])
    zo = family(lambda i: (abuf.at[pd, part(i), turned], opp_z.at[part(i)], (wz, n)), PIECES, half_each)
    zos = family(lambda i: (opp_z.at[part(i)], opp_z.at[part(i)], (w, ns)), PIECES, half_each)
    vs = family(lambda i: (v_ref, left.at[core], (w, ns)), 1, [0])[0]
    as_ = family(lambda i: (a_ref, abuf.at[q], (w, ns)), 1, [0])[0]
    steps = range(CHUNKS)
    arrivals = fresh(1, CHUNKS)
    outside = core != y
    lead = jnp.where(outside, x, 1 - x)
    halves = (lead, 1 - lead)
    same_x = (outside.astype(jnp.int32), 1 - outside.astype(jnp.int32))
    block_sends = fresh(0, 8)
    sends = [
        [
            [
                remote(
                    partials.at[t, s, j], rows_in.at[2 * (1 - same_x[s]) + y, j],
                    (jnp.where(same_x[s] == 1, w, wx), 2 * core + t), block_sends + 4 * t + 2 * s + j // HALF, arrivals + j,
                )
                for j in steps
            ]
            for s in range(2)
        ]
        for t in range(2)
    ]
    z_sends, z_recvs = fresh(0, 2), fresh(1, CHUNKS)
    zc = [remote(zsend.at[j], zrecv.at[j], (wz, n), z_sends + j // HALF, z_recvs + j) for j in steps]
    reflect_send, reflect_recv = fresh(0), fresh(1)
    reflect = [
        remote(msend.at[pl.ds(j * chunk, chunk)], mirror.at[pl.ds(j * chunk, chunk)], (w, ns), reflect_send, reflect_recv)
        for j in range(HALF)
    ]
    leave = [
        pltpu.make_async_copy(obuf.at[pl.ds(j * chunk, chunk)], o_ref.at[pl.ds(j * chunk, chunk)], out_sem.at[j // HALF])
        for j in steps
    ]

    def all_sent(copies, ref):
        send = next(index for copy, index in origin if copy is copies[0])
        pltpu.make_async_remote_copy(
            src_ref=ref, dst_ref=ref, send_sem=send_sem.at[send], recv_sem=recv_sem.at[0], device_id=(w, ns), device_id_type=MESH,
        ).wait_send()

    def all_here(recv, ref):
        pltpu.make_async_remote_copy(
            src_ref=ref, dst_ref=ref, send_sem=send_sem.at[0], recv_sem=recv_sem.at[recv], device_id=(w, ns), device_id_type=MESH,
        ).wait_recv()

    def owned(i):
        return core == i // (PIECES // 2)

    def split_a(block, i):
        value = abuf[block, i * piece : (i + 1) * piece, :]
        high, low = split(value)
        aparts[block, 0, i * piece : (i + 1) * piece, :] = high
        aparts[block, 1, i * piece : (i + 1) * piece, :] = low

    def split_own(i):
        if not lean(i):
            split_a(p, i)
            return
        span = slice(i * piece, (i + 1) * piece)
        high, low = split(abuf[p, span, OVER_X:])
        aparts[p, 0, span, OVER_X:] = high
        aparts[p, 1, span, OVER_X:] = low
        high, low = split(abuf[p, :OVER_X, span].T)
        aparts[p, 0, span, :OVER_X] = high
        aparts[p, 1, span, :OVER_X] = low

    def turn_left(half, t, i, value):
        high, low = split(value.T)
        leftx_t[half, 0, t * wide_half : (t + 1) * wide_half, i * piece : (i + 1) * piece] = high
        leftx_t[half, 1, t * wide_half : (t + 1) * wide_half, i * piece : (i + 1) * piece] = low

    def turn_own(t, i):
        turn_left(core, t, i, vbuf[px, t, i * piece : (i + 1) * piece, :])

    def turn_sibling(t, i):
        turn_left(1 - core, t, i, sibling_x[t, i * piece : (i + 1) * piece, :])

    def turn_opp(i):
        high, low = split(opp_z[i * piece : (i + 1) * piece, :].T)
        oparts[0, OVER_X:, i * piece : (i + 1) * piece] = high
        oparts[1, OVER_X:, i * piece : (i + 1) * piece] = low

    def split_opp(k):
        high, low = split(opp_x[k * quarter : (k + 1) * quarter, :])
        oparts[0, k * quarter : (k + 1) * quarter, :] = high
        oparts[1, k * quarter : (k + 1) * quarter, :] = low

    def start_opp(i):
        for k in range(2):
            if ((k + 1) * quarter - 1) // piece == i:
                @pl.when(core == k)
                def _():
                    xo[k].start()

        @pl.when(owned(i))
        def _():
            zo[i].start()

    late_ay = far & (core == x)
    early_recv = near & (core != x)
    early_relay = near & (core == x)

    pl.semaphore_wait(barrier, 8)
    for i in pieces:
        vx[0][i].start()
        vz[0][i].start()

    @pl.when(jnp.logical_not(late_ay))
    def _():
        for i in pieces:
            start_y(i)

    as_.start()
    vs.start()
    for i in range(AHEAD_X):
        vx[1][i].start()
    for i in range(AHEAD_Z):
        vz[1][i].start()
    for copy in local:
        copy.wait()
    as_.wait_recv()

    @pl.when(far)
    def _():
        for i in pieces:
            start_opp(i)

    left_t[core, 0], left_t[core, 1] = split(left[core].T)
    for i in pieces:
        split_a(first, i)

    @pl.when(near)
    def _():
        for i in pieces:
            split_a(p, i)

    vs.wait_recv()
    left_t[1 - core, 0], left_t[1 - core, 1] = split(left[1 - core].T)
    for i in pieces:
        @pl.when(early_recv)
        def _():
            relay_y(i)
            start_opp(i)

        vx[0][i].wait_recv()
        vxs[0][i].start()
        turn_own(0, i)

        @pl.when(early_relay)
        def _():
            receive_relay(i)
            start_opp(i)

        if i == 1:
            @pl.when(late_ay)
            def _():
                for k in pieces:
                    start_y(k)

    for i in range(AHEAD_X, PIECES):
        vx[1][i].start()
    for i in range(AHEAD_Z, PIECES):
        vz[1][i].start()
    for i in pieces:
        vxs[0][i].wait_recv()
        turn_sibling(0, i)
    all_here(taken_z, vbuf.at[pz, 0])

    def term(t, block):
        return dot3((aparts[block, 0], aparts[block, 1]), split(vbuf[block, t]))

    total = term(0, first)
    right_p = split(vbuf[p, 0])
    right_third = split(vbuf[third, 0])

    def consume_x(i):
        vxs[1][i].wait_recv()
        turn_sibling(1, i)

    def forward_x(i):
        vx[1][i].wait_recv()
        vxs[1][i].start()
        turn_own(1, i)

    images = []

    def pass_rows(i):
        @pl.when(jnp.logical_not(early_recv))
        def _():
            relay_y(i)

    def finish_rows(i):
        @pl.when(jnp.logical_not(early_relay))
        def _():
            receive_relay(i)

        split_a(third, i)

        @pl.when(far)
        def _():
            split_own(i)

        span = part(i)
        value = total[i * piece : (i + 1) * piece]
        value += dot3((aparts[p, 0, span], aparts[p, 1, span]), right_p)
        value += dot3((aparts[third, 0, span], aparts[third, 1, span]), right_third)
        images.append(split(value))

    pass_rows(0)
    for i in range(PIECES - 1):
        pass_rows(i + 1)
        finish_rows(i)
    for k in range(2):
        @pl.when(core == k)
        def _():
            xo[k].wait_recv()
            xos[k].start()
            split_opp(k)

    for i in pieces:
        @pl.when(owned(i))
        def _():
            zo[i].wait_recv()
            zos[i].start()
            turn_opp(i)

    for i in range(AHEAD_X):
        forward_x(i)
    finish_rows(PIECES - 1)
    for k in range(2):
        @pl.when(core != k)
        def _():
            xos[k].wait_recv()
            split_opp(k)

    for i in pieces:
        @pl.when(jnp.logical_not(owned(i)))
        def _():
            zos[i].wait_recv()
            turn_opp(i)

    own_image = tuple(jnp.concatenate([pair[k] for pair in images], axis=0) for k in range(2))
    other_image = split(dot3((oparts[0], oparts[1]), split(vbuf[pz, 0])))

    def block_of(half, start, size, image):
        span = pl.ds(start, size)
        own, other = image
        return dot3((left_t[half, 0, span], left_t[half, 1, span]), own) + dot3(
            (leftx_t[half, 0, span], leftx_t[half, 1, span]), other
        )

    swapped = slot_ref[w // GROUP_WIDE]
    same_flag = (((z + swapped + y) % 2) == 0).astype(jnp.int32)
    local_t = jnp.logical_not(outside)
    diagonal = x == y
    whole = jnp.logical_not(diagonal & (core == 1))

    def needed(t, s, g, body):
        if t == 1 and g == 0:
            pl.when(halves[s] != core)(body)
        else:
            body()

    def send_block(t, s, g, image):
        def body():
            block = block_of(halves[s], g * HALF * chunk, HALF * chunk, image)

            def ship():
                for k in range(HALF):
                    partials[t, s, g * HALF + k] = block[k * chunk : (k + 1) * chunk]
                    sends[t][s][g * HALF + k].start()

            if s == 0:
                ship()
            else:
                pl.when(jnp.logical_not(local_t & (core == t)))(ship)

                @pl.when(local_t & (core == t))
                def _():
                    for k in range(HALF):
                        rows_in[y, g * HALF + k] = block[k * chunk : (k + 1) * chunk]

        needed(t, s, g, body)

    def drain_block(t, s, g):
        def body():
            group = pl.ds(g * HALF, HALF)
            all_sent(sends[t][s][g * HALF :], partials.at[t, s, group])

        def drain():
            if s == 0:
                body()
            else:
                pl.when(jnp.logical_not(local_t & (core == t)))(body)

        needed(t, s, g, drain)

    def gather_rows(j):
        @pl.when(local_t)
        def _():
            all_here(arrivals + j, rows_in.at[pl.ds(0, 3), j])

        @pl.when(outside)
        def _():
            all_here(arrivals + j, rows_in.at[:, j])

        same = rows_in[y, j] + rows_in[2 + y, j]
        other = rows_in[1 - y, j] + rows_in[3 - y, j]
        mask = jnp.full(same.shape, same_flag) == 1
        zsend[j] = jnp.where(mask, other, same)
        zc[j].start()
        obuf[pl.ds(j * chunk, chunk), :] = jnp.where(mask, same, other)

    def finish(j):
        zc[j].wait_recv()
        total = obuf[pl.ds(j * chunk, chunk), :] + zrecv[j]
        obuf[pl.ds(j * chunk, chunk), :] = total
        leave[j].start()
        if j >= HALF:
            @pl.when(diagonal & (core == 0))
            def _():
                msend[pl.ds((j - HALF) * chunk, chunk)] = total
                reflect[j - HALF].start()

    image = (own_image, other_image)
    for s in range(2):
        send_block(0, s, 0, image)
    for i in range(AHEAD_X, PIECES):
        forward_x(i)
    for i in pieces:
        consume_x(i)
    for s in range(2):
        send_block(0, s, 1, image)
    total = term(1, p) + term(1, px)

    def half_term(left, t, k):
        span = pl.ds(k * wide_half, wide_half)
        return dot3((left.at[0, :, span][...], left.at[1, :, span][...]), split(vbuf[pz, t, span]))

    other = None
    for k in range(2):
        all_here(taken_z + 1 + k, vbuf.at[pz, 1, pl.ds(k * wide_half, wide_half)])
        total += half_term(aparts.at[pz], 1, k)
        more = half_term(oparts, 1, k)
        other = more if other is None else other + more
    image = (split(total), split(other))
    for g in range(2):
        for s in range(2):
            send_block(1, s, g, image)

    @pl.when(whole)
    def _():
        for j in range(HALF):
            gather_rows(j)

    for j in range(HALF, CHUNKS):
        gather_rows(j)

    @pl.when(whole)
    def _():
        for j in range(HALF):
            finish(j)
        all_sent(zc[:HALF], zsend.at[pl.ds(0, HALF)])

    for j in range(HALF, CHUNKS):
        finish(j)

    @pl.when(jnp.logical_not(whole))
    def _():
        all_here(reflect_recv, mirror)
        obuf[pl.ds(0, HALF * chunk), :] = mirror[...].T
        for j in range(HALF):
            leave[j].start()

    @pl.when(diagonal & (core == 0))
    def _():
        all_sent(reflect, msend)

    for copies in (vx[0], vz[0], vxs[0], [vs], [as_]):
        all_sent(copies, abuf.at[0])
    for copies, condition in ((ay, lean_out), (ayr, lean_in)):
        choose(
            condition,
            lambda: all_sent(copies, abuf.at[0, pl.ds(0, lean_rows)]),
            lambda: all_sent(copies, abuf.at[0]),
        )
    all_sent(xo, opp_x.at[pl.ds(0, quarter)])
    all_sent(xos, opp_x.at[pl.ds(0, quarter)])
    all_sent(zo, opp_z.at[pl.ds(0, rows // 2)])
    all_sent(zos, opp_z.at[pl.ds(0, rows // 2)])
    all_sent(zc[HALF:], zsend.at[pl.ds(HALF, HALF)])
    for t in range(2):
        for s in range(2):
            for g in range(2):
                drain_block(t, s, g)
    for g in range(2):
        group = pl.ds(g * HALF * chunk, HALF * chunk)
        pltpu.make_async_copy(obuf.at[group], o_ref.at[group], out_sem.at[g]).wait()


def fast_body(moments, eigen_basis, slot_order):
    rows, cols = moments.shape
    f32 = jnp.float32
    chunk = rows // CHUNKS
    wide_half = cols // 2
    return pl.pallas_call(
        kernel,
        out_shape=jax.ShapeDtypeStruct((rows, wide_half), f32),
        in_specs=[
            pl.BlockSpec(memory_space=pltpu.SMEM),
            pl.BlockSpec(memory_space=pl.ANY),
            pl.BlockSpec(memory_space=pl.ANY),
        ],
        out_specs=pl.BlockSpec(memory_space=pl.ANY),
        scratch_shapes=[
            pltpu.VMEM((4, rows, cols), f32),
            pltpu.VMEM((4, 2, rows, cols), jnp.bfloat16),
            pltpu.VMEM((OVER_X, cols), f32),
            pltpu.VMEM((rows, cols - OVER_X), f32),
            pltpu.VMEM((2, cols, rows), jnp.bfloat16),
            pltpu.VMEM((4, 2, rows, wide_half), f32),
            pltpu.VMEM((2, rows, wide_half), f32),
            pltpu.VMEM((2, rows, cols), f32),
            pltpu.VMEM((2, 2, cols, rows), jnp.bfloat16),
            pltpu.VMEM((2, 2, cols, rows), jnp.bfloat16),
            pltpu.VMEM((2, 2, CHUNKS, chunk, wide_half), f32),
            pltpu.VMEM((4, CHUNKS, chunk, wide_half), f32),
            *[pltpu.VMEM((CHUNKS, chunk, wide_half), f32)] * 2,
            *[pltpu.VMEM((HALF * chunk, wide_half), f32)] * 2,
            pltpu.VMEM((rows, wide_half), f32),
            pltpu.SemaphoreType.DMA((4,)),
            pltpu.SemaphoreType.DMA((2,)),
            pltpu.SemaphoreType.DMA((SENDS,)),
            pltpu.SemaphoreType.DMA((RECVS,)),
        ],
        compiler_params=pltpu.CompilerParams(
            collective_id=0, has_side_effects=True, vmem_limit_bytes=53 * 1024 * 1024
        ),
        name="rayleigh",
    )(slot_order, moments, eigen_basis)


def partner(value, axis, stride):
    mask = 2**stride
    pairs = [(source, source ^ mask) for source in range(lax.axis_size(axis))]
    return lax.ppermute(value, axis, pairs)


def body(moments, eigen_basis, slot_order):
    wide_pos = lax.axis_index("wide")
    subproblem = wide_pos // GROUP_WIDE
    position = wide_pos % GROUP_WIDE
    swapped = lax.dynamic_index_in_dim(slot_order, subproblem, 0, keepdims=False)
    narrow_pos = lax.axis_index("narrow")
    col_count = eigen_basis.shape[1]
    half_cols = col_count // 2
    full_basis = lax.all_gather(eigen_basis, "narrow", axis=1, tiled=True)
    first_half = lax.dynamic_slice_in_dim(full_basis, narrow_pos * half_cols, half_cols, 1)
    second_half = lax.dynamic_slice_in_dim(full_basis, K + narrow_pos * half_cols, half_cols, 1)
    local_panel = jnp.concatenate([first_half, second_half], axis=1)
    pair_block = partner(local_panel, "wide", 0)
    joined = jnp.where(
        position % 2 == 0,
        jnp.concatenate([local_panel, pair_block], axis=0),
        jnp.concatenate([pair_block, local_panel], axis=0),
    )
    quad_block = partner(joined, "wide", 1)
    col_panel = jnp.where(
        position // 2 % 2 == 0,
        jnp.concatenate([joined, quad_block], axis=0),
        jnp.concatenate([quad_block, joined], axis=0),
    )
    products = jnp.dot(
        lax.all_gather(moments, "narrow", axis=1, tiled=True),
        col_panel,
        precision=lax.Precision.HIGHEST,
        preferred_element_type=jnp.float32,
    )
    partials = []
    for slot_index in range(2):
        half_panel = products[:, slot_index * half_cols : (slot_index + 1) * half_cols]
        vectors_half = full_basis[:, slot_index * K : (slot_index + 1) * K]
        partials.append(
            lax.dot_general(
                vectors_half,
                half_panel,
                (((0,), (0,)), ((), ())),
                precision=lax.Precision.HIGHEST,
                preferred_element_type=jnp.float32,
            )
        )
    stacked = jnp.stack(partials)
    slot_pick = (position // 2 + swapped) % 2
    row_part = position % 2
    summed = stacked + partner(stacked, "wide", 0)
    summed = summed + partner(summed, "wide", 1)
    chosen = lax.dynamic_index_in_dim(summed, slot_pick, 0, keepdims=False)
    return lax.dynamic_slice_in_dim(chosen, row_part * (K // 2), K // 2, 0)


def solution(mesh):
    placed = (P("wide", "narrow"), P("wide", "narrow"), P())
    cube = mesh.shape["narrow"] == 4
    return jax.shard_map(
        fast_body if cube else body, mesh=mesh, in_specs=placed, out_specs=P("wide", "narrow"), check_vma=False
    )
```

```python
import jax
import jax.numpy as jnp
from jax import lax
from jax.experimental import pallas as pl
from jax.experimental.pallas import tpu as pltpu
from jax.sharding import PartitionSpec as P

GROUP_WIDE = 4
K = 1024
MESH = pl.DeviceIdType.MESH
CHUNKS = 8
HALF = CHUNKS // 2
PIECES = 4
OVER_X = 128
AHEAD_X = 1
AHEAD_Z = 0
SENDS = 22
RECVS = 52


def split(value):
    high = value.astype(jnp.bfloat16)
    low = (value - high.astype(jnp.float32)).astype(jnp.bfloat16)
    return high, low


def dot3(left, right):
    def dot(a, b):
        return jnp.dot(a, b, preferred_element_type=jnp.float32)

    return dot(left[0], right[0]) + (dot(left[0], right[1]) + dot(left[1], right[0]))


def kernel(
    slot_ref, a_ref, v_ref, o_ref,
    abuf, aparts, opp_x, opp_z, oparts, vbuf, sibling_x, left, left_t, leftx_t,
    partials, rows_in, zsend, zrecv, msend, mirror, obuf,
    local_sem, out_sem, send_sem, recv_sem,
):
    rows, cols = a_ref.shape
    wide_half = cols // 2
    piece = rows // PIECES
    chunk = rows // CHUNKS
    w = lax.axis_index("wide")
    n = lax.axis_index("narrow")
    x = w % 2
    z = (w // 2) % 2
    y = n // 2
    core = n % 2
    p = w % 4
    wx = w + 1 - 2 * x
    wz = w + 2 - 4 * z
    px = p + 1 - 2 * x
    pz = p + 2 - 4 * z
    pd = 3 - p
    ns = n + 1 - 2 * core
    ny = n + 2 - 4 * y
    q = 2 * y + core
    qy = 2 * (1 - y) + core
    near = z == y
    far = z != y
    third = jnp.where(near, pz, px)
    first = jnp.where(near, px, pz)

    barrier = pltpu.get_barrier_semaphore()
    for target in ((wz, n), (w, ns), (w, ny), (w, 3 - n), *((wx, m) for m in range(4))):
        pl.semaphore_signal(barrier, inc=1, device_id=target, device_id_type=MESH)

    def part(i):
        return pl.ds(i * piece, piece)

    def side(t):
        return pl.ds(t * wide_half, wide_half)

    local = [
        pltpu.make_async_copy(v_ref, left.at[core], local_sem.at[0]),
        pltpu.make_async_copy(a_ref, abuf.at[q], local_sem.at[1]),
        pltpu.make_async_copy(v_ref.at[:, side(0)], vbuf.at[p, 0], local_sem.at[2]),
        pltpu.make_async_copy(v_ref.at[:, side(1)], vbuf.at[p, 1], local_sem.at[3]),
    ]
    for copy in local:
        copy.start()

    taken = [0, 0]
    origin = []

    def fresh(kind, count=1):
        start = taken[kind]
        taken[kind] += count
        return start

    def remote(src, dst, target, send, recv):
        copy = pltpu.make_async_remote_copy(
            src_ref=src, dst_ref=dst, send_sem=send_sem.at[send], recv_sem=recv_sem.at[recv],
            device_id=target, device_id_type=MESH,
        )
        origin.append((copy, send))
        return copy

    def family(make, count, arrivals):
        send, recv = fresh(0), fresh(1, max(arrivals) + 1)
        return [remote(*make(i), send, recv + arrivals[i]) for i in range(count)]

    pieces = range(PIECES)
    each = list(pieces)
    half_each = [i % (PIECES // 2) for i in pieces]
    pairs = [(t, i) for t in range(2) for i in pieces]

    def both(flat):
        return [flat[:PIECES], flat[PIECES:]]

    def basis(i, target):
        t, k = pairs[i]
        return v_ref.at[part(k), side(t)], vbuf.at[p, t, part(k)], target

    def shared_x(i):
        t, k = pairs[i]
        return vbuf.at[px, t, part(k)], sibling_x.at[t, part(k)], (w, ns)

    count = 2 * PIECES
    vx = both(family(lambda i: basis(i, (wx, n)), count, list(range(count))))
    z_arrivals = [0] * PIECES + [1 + 2 * i // PIECES for i in pieces]
    taken_z = taken[1]
    vz = both(family(lambda i: basis(i, (wz, n)), count, z_arrivals))
    vxs = both(family(shared_x, count, list(range(count))))
    quarter = OVER_X // 2
    turned = pl.ds(OVER_X, cols - OVER_X)
    lean_rows = (OVER_X * cols + (rows - OVER_X) * (cols - OVER_X)) // cols
    lean_out = near == (core == x)
    lean_in = far == (core == x)
    lean_relay = far == (core != x)
    ay_sems, ayr_sems = (fresh(0), fresh(1, PIECES)), (fresh(0), fresh(1, PIECES))

    def lean(i):
        return i * piece >= OVER_X

    def moments_y(i, wanted):
        return remote(a_ref.at[part(i), wanted], abuf.at[q, part(i), wanted], (w, ny), ay_sems[0], ay_sems[1] + i)

    def moments_core(i, wanted):
        return remote(abuf.at[qy, part(i), wanted], abuf.at[qy, part(i), wanted], (w, ns), ayr_sems[0], ayr_sems[1] + i)

    full = pl.ds(0, cols)
    ay = [moments_y(i, full) for i in pieces]
    ayr = [moments_core(i, full) for i in pieces]
    ay_lean = [moments_y(i, turned) if lean(i) else ay[i] for i in pieces]
    ayr_lean = [moments_core(i, turned) if lean(i) else ayr[i] for i in pieces]

    def choose(condition, when_true, when_false):
        pl.when(condition)(when_true)
        pl.when(jnp.logical_not(condition))(when_false)

    def start_y(i):
        if lean(i):
            choose(lean_out, ay_lean[i].start, ay[i].start)
        else:
            ay[i].start()

    def relay_y(i):
        if lean(i):
            choose(lean_in, ay_lean[i].wait_recv, ay[i].wait_recv)
            choose(lean_in, ayr_lean[i].start, ayr[i].start)
        else:
            ay[i].wait_recv()
            ayr[i].start()

    def receive_relay(i):
        if lean(i):
            choose(lean_relay, ayr_lean[i].wait_recv, ayr[i].wait_recv)
        else:
            ayr[i].wait_recv()

    def rows_x(k):
        return pl.ds(k * quarter, quarter)

    xo = family(lambda k: (abuf.at[pd, rows_x(k)], opp_x.at[rows_x(k)], (wx, n)), 2, [0, 0])
    xos = family(lambda k: (opp_x.at[rows_x(k)], opp_x.at[rows_x(k)], (w, ns)), 2, [0, 0])
    zo = family(lambda i: (abuf.at[pd, part(i), turned], opp_z.at[part(i)], (wz, n)), PIECES, half_each)
    zos = family(lambda i: (opp_z.at[part(i)], opp_z.at[part(i)], (w, ns)), PIECES, half_each)
    vs = family(lambda i: (v_ref, left.at[core], (w, ns)), 1, [0])[0]
    as_ = family(lambda i: (a_ref, abuf.at[q], (w, ns)), 1, [0])[0]
    steps = range(CHUNKS)
    arrivals = fresh(1, CHUNKS)
    outside = core != y
    lead = jnp.where(outside, x, 1 - x)
    halves = (lead, 1 - lead)
    same_x = (outside.astype(jnp.int32), 1 - outside.astype(jnp.int32))
    block_sends = fresh(0, 8)
    sends = [
        [
            [
                remote(
                    partials.at[t, s, j], rows_in.at[2 * (1 - same_x[s]) + y, j],
                    (jnp.where(same_x[s] == 1, w, wx), 2 * core + t), block_sends + 4 * t + 2 * s + j // HALF, arrivals + j,
                )
                for j in steps
            ]
            for s in range(2)
        ]
        for t in range(2)
    ]
    z_sends, z_recvs = fresh(0, 2), fresh(1, CHUNKS)
    zc = [remote(zsend.at[j], zrecv.at[j], (wz, n), z_sends + j // HALF, z_recvs + j) for j in steps]
    reflect_send, reflect_recv = fresh(0), fresh(1)
    reflect = [
        remote(msend.at[pl.ds(j * chunk, chunk)], mirror.at[pl.ds(j * chunk, chunk)], (w, ns), reflect_send, reflect_recv)
        for j in range(HALF)
    ]
    leave = [
        pltpu.make_async_copy(obuf.at[pl.ds(j * chunk, chunk)], o_ref.at[pl.ds(j * chunk, chunk)], out_sem.at[j // HALF])
        for j in steps
    ]

    def all_sent(copies, ref):
        send = next(index for copy, index in origin if copy is copies[0])
        pltpu.make_async_remote_copy(
            src_ref=ref, dst_ref=ref, send_sem=send_sem.at[send], recv_sem=recv_sem.at[0], device_id=(w, ns), device_id_type=MESH,
        ).wait_send()

    def all_here(recv, ref):
        pltpu.make_async_remote_copy(
            src_ref=ref, dst_ref=ref, send_sem=send_sem.at[0], recv_sem=recv_sem.at[recv], device_id=(w, ns), device_id_type=MESH,
        ).wait_recv()

    def owned(i):
        return core == i // (PIECES // 2)

    def split_a(block, i):
        value = abuf[block, i * piece : (i + 1) * piece, :]
        high, low = split(value)
        aparts[block, 0, i * piece : (i + 1) * piece, :] = high
        aparts[block, 1, i * piece : (i + 1) * piece, :] = low

    def split_own(i):
        if not lean(i):
            split_a(p, i)
            return
        span = slice(i * piece, (i + 1) * piece)
        high, low = split(abuf[p, span, OVER_X:])
        aparts[p, 0, span, OVER_X:] = high
        aparts[p, 1, span, OVER_X:] = low
        high, low = split(abuf[p, :OVER_X, span].T)
        aparts[p, 0, span, :OVER_X] = high
        aparts[p, 1, span, :OVER_X] = low

    def turn_left(half, t, i, value):
        high, low = split(value.T)
        leftx_t[half, 0, t * wide_half : (t + 1) * wide_half, i * piece : (i + 1) * piece] = high
        leftx_t[half, 1, t * wide_half : (t + 1) * wide_half, i * piece : (i + 1) * piece] = low

    def turn_own(t, i):
        turn_left(core, t, i, vbuf[px, t, i * piece : (i + 1) * piece, :])

    def turn_sibling(t, i):
        turn_left(1 - core, t, i, sibling_x[t, i * piece : (i + 1) * piece, :])

    def turn_opp(i):
        high, low = split(opp_z[i * piece : (i + 1) * piece, :].T)
        oparts[0, OVER_X:, i * piece : (i + 1) * piece] = high
        oparts[1, OVER_X:, i * piece : (i + 1) * piece] = low

    def split_opp(k):
        high, low = split(opp_x[k * quarter : (k + 1) * quarter, :])
        oparts[0, k * quarter : (k + 1) * quarter, :] = high
        oparts[1, k * quarter : (k + 1) * quarter, :] = low

    def start_opp(i):
        for k in range(2):
            if ((k + 1) * quarter - 1) // piece == i:
                @pl.when(core == k)
                def _():
                    xo[k].start()

        @pl.when(owned(i))
        def _():
            zo[i].start()

    late_ay = far & (core == x)
    early_recv = near & (core != x)
    early_relay = near & (core == x)

    pl.semaphore_wait(barrier, 8)
    for i in pieces:
        vx[0][i].start()
        vz[0][i].start()

    @pl.when(jnp.logical_not(late_ay))
    def _():
        for i in pieces:
            start_y(i)

    as_.start()
    vs.start()
    for i in range(AHEAD_X):
        vx[1][i].start()
    for i in range(AHEAD_Z):
        vz[1][i].start()
    for copy in local:
        copy.wait()
    as_.wait_recv()

    @pl.when(far)
    def _():
        for i in pieces:
            start_opp(i)

    left_t[core, 0], left_t[core, 1] = split(left[core].T)
    for i in pieces:
        split_a(first, i)

    @pl.when(near)
    def _():
        for i in pieces:
            split_a(p, i)

    vs.wait_recv()
    left_t[1 - core, 0], left_t[1 - core, 1] = split(left[1 - core].T)
    for i in pieces:
        @pl.when(early_recv)
        def _():
            relay_y(i)
            start_opp(i)

        vx[0][i].wait_recv()
        vxs[0][i].start()
        turn_own(0, i)

        @pl.when(early_relay)
        def _():
            receive_relay(i)
            start_opp(i)

        if i == 1:
            @pl.when(late_ay)
            def _():
                for k in pieces:
                    start_y(k)

    for i in range(AHEAD_X, PIECES):
        vx[1][i].start()
    for i in range(AHEAD_Z, PIECES):
        vz[1][i].start()
    for i in pieces:
        vxs[0][i].wait_recv()
        turn_sibling(0, i)
    all_here(taken_z, vbuf.at[pz, 0])

    def term(t, block):
        return dot3((aparts[block, 0], aparts[block, 1]), split(vbuf[block, t]))

    total = term(0, first)
    right_p = split(vbuf[p, 0])
    right_third = split(vbuf[third, 0])

    def consume_x(i):
        vxs[1][i].wait_recv()
        turn_sibling(1, i)

    def forward_x(i):
        vx[1][i].wait_recv()
        vxs[1][i].start()
        turn_own(1, i)

    images = []

    def pass_rows(i):
        @pl.when(jnp.logical_not(early_recv))
        def _():
            relay_y(i)

    def finish_rows(i):
        @pl.when(jnp.logical_not(early_relay))
        def _():
            receive_relay(i)

        split_a(third, i)

        @pl.when(far)
        def _():
            split_own(i)

        span = part(i)
        value = total[i * piece : (i + 1) * piece]
        value += dot3((aparts[p, 0, span], aparts[p, 1, span]), right_p)
        value += dot3((aparts[third, 0, span], aparts[third, 1, span]), right_third)
        images.append(split(value))

    def other_part(t, k):
        span = pl.ds(pl.multiple_of(k * wide_half, wide_half), wide_half)
        return dot3((oparts.at[0, :, span][...], oparts.at[1, :, span][...]), split(vbuf[pz, t, span]))

    pass_rows(0)
    pass_rows(1)
    finish_rows(0)
    pass_rows(2)
    finish_rows(1)
    finish_rows(2)
    for k in range(2):
        @pl.when(core == k)
        def _():
            xo[k].wait_recv()
            xos[k].start()
            split_opp(k)

    pass_rows(3)
    for k in range(2):
        @pl.when(core != k)
        def _():
            xos[k].wait_recv()
            split_opp(k)

    for i in pieces:
        @pl.when(owned(i))
        def _():
            zo[i].wait_recv()
            zos[i].start()
            turn_opp(i)

    other = other_part(0, core)
    finish_rows(3)
    for i in pieces:
        @pl.when(jnp.logical_not(owned(i)))
        def _():
            zos[i].wait_recv()
            turn_opp(i)

    own_image = tuple(jnp.concatenate([pair[k] for pair in images], axis=0) for k in range(2))
    other_image = split(other + other_part(0, 1 - core))

    def block_of(half, start, size, image):
        span = pl.ds(start, size)
        own, other = image
        return dot3((left_t[half, 0, span], left_t[half, 1, span]), own) + dot3(
            (leftx_t[half, 0, span], leftx_t[half, 1, span]), other
        )

    swapped = slot_ref[w // GROUP_WIDE]
    same_flag = (((z + swapped + y) % 2) == 0).astype(jnp.int32)
    local_t = jnp.logical_not(outside)
    diagonal = x == y
    whole = jnp.logical_not(diagonal & (core == 1))

    def needed(t, s, g, body):
        if t == 1 and g == 0:
            pl.when(halves[s] != core)(body)
        else:
            body()

    def send_block(t, s, g, image):
        def body():
            cuts = 2 if (t, s, g) == (0, 0, 0) else 1
            count = HALF // cuts
            for c in range(cuts):
                first_j = g * HALF + c * count
                block = block_of(halves[s], first_j * chunk, count * chunk, image)
                if s == 0:
                    ship(block, first_j, count)
            if s == 1:
                place(block)

        def ship(block, first_j, count):
            for k in range(count):
                partials[t, s, first_j + k] = block[k * chunk : (k + 1) * chunk]
                sends[t][s][first_j + k].start()

        def place(block):
            pl.when(jnp.logical_not(local_t & (core == t)))(lambda: ship(block, g * HALF, HALF))

            @pl.when(local_t & (core == t))
            def _():
                for k in range(HALF):
                    rows_in[y, g * HALF + k] = block[k * chunk : (k + 1) * chunk]

        needed(t, s, g, body)

    def drain_block(t, s, g):
        def body():
            group = pl.ds(g * HALF, HALF)
            all_sent(sends[t][s][g * HALF :], partials.at[t, s, group])

        def drain():
            if s == 0:
                body()
            else:
                pl.when(jnp.logical_not(local_t & (core == t)))(body)

        needed(t, s, g, drain)

    def gather_rows(j):
        @pl.when(local_t)
        def _():
            all_here(arrivals + j, rows_in.at[pl.ds(0, 3), j])

        @pl.when(outside)
        def _():
            all_here(arrivals + j, rows_in.at[:, j])

        same = rows_in[y, j] + rows_in[2 + y, j]
        other = rows_in[1 - y, j] + rows_in[3 - y, j]
        mask = jnp.full(same.shape, same_flag) == 1
        zsend[j] = jnp.where(mask, other, same)
        zc[j].start()
        obuf[pl.ds(j * chunk, chunk), :] = jnp.where(mask, same, other)

    def finish(j):
        zc[j].wait_recv()
        total = obuf[pl.ds(j * chunk, chunk), :] + zrecv[j]
        obuf[pl.ds(j * chunk, chunk), :] = total
        leave[j].start()
        if j >= HALF:
            @pl.when(diagonal & (core == 0))
            def _():
                msend[pl.ds((j - HALF) * chunk, chunk)] = total
                reflect[j - HALF].start()

    image = (own_image, other_image)
    for s in range(2):
        send_block(0, s, 0, image)
    for i in pieces:
        forward_x(i)
    for i in pieces:
        consume_x(i)
    for s in range(2):
        send_block(0, s, 1, image)
    total = term(1, p) + term(1, px)

    def half_term(left, t, k):
        span = pl.ds(k * wide_half, wide_half)
        return dot3((left.at[0, :, span][...], left.at[1, :, span][...]), split(vbuf[pz, t, span]))

    other = None
    for k in range(2):
        all_here(taken_z + 1 + k, vbuf.at[pz, 1, pl.ds(k * wide_half, wide_half)])
        total += half_term(aparts.at[pz], 1, k)
        more = half_term(oparts, 1, k)
        other = more if other is None else other + more
    image = (split(total), split(other))
    for g in range(2):
        for s in range(2):
            send_block(1, s, g, image)

    @pl.when(whole)
    def _():
        for j in range(HALF):
            gather_rows(j)

    for j in range(HALF, CHUNKS):
        gather_rows(j)

    @pl.when(whole)
    def _():
        for j in range(HALF):
            finish(j)
        all_sent(zc[:HALF], zsend.at[pl.ds(0, HALF)])

    for j in range(HALF, CHUNKS):
        finish(j)

    @pl.when(jnp.logical_not(whole))
    def _():
        all_here(reflect_recv, mirror)
        obuf[pl.ds(0, HALF * chunk), :] = mirror[...].T
        for j in range(HALF):
            leave[j].start()

    @pl.when(diagonal & (core == 0))
    def _():
        all_sent(reflect, msend)

    for copies in (vx[0], vz[0], vxs[0], [vs], [as_]):
        all_sent(copies, abuf.at[0])
    for copies, condition in ((ay, lean_out), (ayr, lean_in)):
        choose(
            condition,
            lambda: all_sent(copies, abuf.at[0, pl.ds(0, lean_rows)]),
            lambda: all_sent(copies, abuf.at[0]),
        )
    all_sent(xo, opp_x.at[pl.ds(0, quarter)])
    all_sent(xos, opp_x.at[pl.ds(0, quarter)])
    all_sent(zo, opp_z.at[pl.ds(0, rows // 2)])
    all_sent(zos, opp_z.at[pl.ds(0, rows // 2)])
    all_sent(zc[HALF:], zsend.at[pl.ds(HALF, HALF)])
    for t in range(2):
        for s in range(2):
            for g in range(2):
                drain_block(t, s, g)
    for g in range(2):
        group = pl.ds(g * HALF * chunk, HALF * chunk)
        pltpu.make_async_copy(obuf.at[group], o_ref.at[group], out_sem.at[g]).wait()


def fast_body(moments, eigen_basis, slot_order):
    rows, cols = moments.shape
    f32 = jnp.float32
    chunk = rows // CHUNKS
    wide_half = cols // 2
    return pl.pallas_call(
        kernel,
        out_shape=jax.ShapeDtypeStruct((rows, wide_half), f32),
        in_specs=[
            pl.BlockSpec(memory_space=pltpu.SMEM),
            pl.BlockSpec(memory_space=pl.ANY),
            pl.BlockSpec(memory_space=pl.ANY),
        ],
        out_specs=pl.BlockSpec(memory_space=pl.ANY),
        scratch_shapes=[
            pltpu.VMEM((4, rows, cols), f32),
            pltpu.VMEM((4, 2, rows, cols), jnp.bfloat16),
            pltpu.VMEM((OVER_X, cols), f32),
            pltpu.VMEM((rows, cols - OVER_X), f32),
            pltpu.VMEM((2, cols, rows), jnp.bfloat16),
            pltpu.VMEM((4, 2, rows, wide_half), f32),
            pltpu.VMEM((2, rows, wide_half), f32),
            pltpu.VMEM((2, rows, cols), f32),
            pltpu.VMEM((2, 2, cols, rows), jnp.bfloat16),
            pltpu.VMEM((2, 2, cols, rows), jnp.bfloat16),
            pltpu.VMEM((2, 2, CHUNKS, chunk, wide_half), f32),
            pltpu.VMEM((4, CHUNKS, chunk, wide_half), f32),
            *[pltpu.VMEM((CHUNKS, chunk, wide_half), f32)] * 2,
            *[pltpu.VMEM((HALF * chunk, wide_half), f32)] * 2,
            pltpu.VMEM((rows, wide_half), f32),
            pltpu.SemaphoreType.DMA((4,)),
            pltpu.SemaphoreType.DMA((2,)),
            pltpu.SemaphoreType.DMA((SENDS,)),
            pltpu.SemaphoreType.DMA((RECVS,)),
        ],
        compiler_params=pltpu.CompilerParams(
            collective_id=0, has_side_effects=True, vmem_limit_bytes=53 * 1024 * 1024
        ),
        name="rayleigh",
    )(slot_order, moments, eigen_basis)


def partner(value, axis, stride):
    mask = 2**stride
    pairs = [(source, source ^ mask) for source in range(lax.axis_size(axis))]
    return lax.ppermute(value, axis, pairs)


def body(moments, eigen_basis, slot_order):
    wide_pos = lax.axis_index("wide")
    subproblem = wide_pos // GROUP_WIDE
    position = wide_pos % GROUP_WIDE
    swapped = lax.dynamic_index_in_dim(slot_order, subproblem, 0, keepdims=False)
    narrow_pos = lax.axis_index("narrow")
    col_count = eigen_basis.shape[1]
    half_cols = col_count // 2
    full_basis = lax.all_gather(eigen_basis, "narrow", axis=1, tiled=True)
    first_half = lax.dynamic_slice_in_dim(full_basis, narrow_pos * half_cols, half_cols, 1)
    second_half = lax.dynamic_slice_in_dim(full_basis, K + narrow_pos * half_cols, half_cols, 1)
    local_panel = jnp.concatenate([first_half, second_half], axis=1)
    pair_block = partner(local_panel, "wide", 0)
    joined = jnp.where(
        position % 2 == 0,
        jnp.concatenate([local_panel, pair_block], axis=0),
        jnp.concatenate([pair_block, local_panel], axis=0),
    )
    quad_block = partner(joined, "wide", 1)
    col_panel = jnp.where(
        position // 2 % 2 == 0,
        jnp.concatenate([joined, quad_block], axis=0),
        jnp.concatenate([quad_block, joined], axis=0),
    )
    products = jnp.dot(
        lax.all_gather(moments, "narrow", axis=1, tiled=True),
        col_panel,
        precision=lax.Precision.HIGHEST,
        preferred_element_type=jnp.float32,
    )
    partials = []
    for slot_index in range(2):
        half_panel = products[:, slot_index * half_cols : (slot_index + 1) * half_cols]
        vectors_half = full_basis[:, slot_index * K : (slot_index + 1) * K]
        partials.append(
            lax.dot_general(
                vectors_half,
                half_panel,
                (((0,), (0,)), ((), ())),
                precision=lax.Precision.HIGHEST,
                preferred_element_type=jnp.float32,
            )
        )
    stacked = jnp.stack(partials)
    slot_pick = (position // 2 + swapped) % 2
    row_part = position % 2
    summed = stacked + partner(stacked, "wide", 0)
    summed = summed + partner(summed, "wide", 1)
    chosen = lax.dynamic_index_in_dim(summed, slot_pick, 0, keepdims=False)
    return lax.dynamic_slice_in_dim(chosen, row_part * (K // 2), K // 2, 0)


def solution(mesh):
    placed = (P("wide", "narrow"), P("wide", "narrow"), P())
    cube = mesh.shape["narrow"] == 4
    return jax.shard_map(
        fast_body if cube else body, mesh=mesh, in_specs=placed, out_specs=P("wide", "narrow"), check_vma=False
    )
```

```python
import jax
import jax.numpy as jnp
from jax import lax
from jax.experimental import pallas as pl
from jax.experimental.pallas import tpu as pltpu
from jax.sharding import PartitionSpec as P

GROUP_WIDE = 4
K = 1024
MESH = pl.DeviceIdType.MESH
CHUNKS = 8
HALF = CHUNKS // 2
THIN = ((0, 2), (0, 3), (1, 6), (1, 7))
PIECES = 4
OVER_X = 128
AHEAD_X = 1
AHEAD_Z = 0
SENDS = 22
RECVS = 52


def split(value):
    high = value.astype(jnp.bfloat16)
    low = (value - high.astype(jnp.float32)).astype(jnp.bfloat16)
    return high, low


def dot3(left, right):
    def dot(a, b):
        return jnp.dot(a, b, preferred_element_type=jnp.float32)

    return dot(left[0], right[0]) + (dot(left[0], right[1]) + dot(left[1], right[0]))


def kernel(
    slot_ref, a_ref, v_ref, o_ref,
    abuf, aparts, opp_x, opp_z, oparts, vbuf, sibling_x, left, left_t, leftx_t,
    partials, rows_in, zsend, zrecv, msend, mirror, obuf,
    local_sem, out_sem, send_sem, recv_sem,
):
    rows, cols = a_ref.shape
    wide_half = cols // 2
    piece = rows // PIECES
    chunk = rows // CHUNKS
    w = lax.axis_index("wide")
    n = lax.axis_index("narrow")
    x = w % 2
    z = (w // 2) % 2
    y = n // 2
    core = n % 2
    p = w % 4
    wx = w + 1 - 2 * x
    wz = w + 2 - 4 * z
    px = p + 1 - 2 * x
    pz = p + 2 - 4 * z
    pd = 3 - p
    ns = n + 1 - 2 * core
    ny = n + 2 - 4 * y
    q = 2 * y + core
    qy = 2 * (1 - y) + core
    near = z == y
    far = z != y
    third = jnp.where(near, pz, px)
    first = jnp.where(near, px, pz)

    barrier = pltpu.get_barrier_semaphore()
    for target in ((wz, n), (w, ns), (w, ny), (w, 3 - n), *((wx, m) for m in range(4))):
        pl.semaphore_signal(barrier, inc=1, device_id=target, device_id_type=MESH)

    def part(i):
        return pl.ds(i * piece, piece)

    def side(t):
        return pl.ds(t * wide_half, wide_half)

    local = [
        pltpu.make_async_copy(v_ref, left.at[core], local_sem.at[0]),
        pltpu.make_async_copy(a_ref, abuf.at[q], local_sem.at[1]),
        pltpu.make_async_copy(v_ref.at[:, side(0)], vbuf.at[p, 0], local_sem.at[2]),
        pltpu.make_async_copy(v_ref.at[:, side(1)], vbuf.at[p, 1], local_sem.at[3]),
    ]
    for copy in local:
        copy.start()

    taken = [0, 0]
    origin = []

    def fresh(kind, count=1):
        start = taken[kind]
        taken[kind] += count
        return start

    def remote(src, dst, target, send, recv):
        copy = pltpu.make_async_remote_copy(
            src_ref=src, dst_ref=dst, send_sem=send_sem.at[send], recv_sem=recv_sem.at[recv],
            device_id=target, device_id_type=MESH,
        )
        origin.append((copy, send))
        return copy

    def family(make, count, arrivals):
        send, recv = fresh(0), fresh(1, max(arrivals) + 1)
        return [remote(*make(i), send, recv + arrivals[i]) for i in range(count)]

    pieces = range(PIECES)
    each = list(pieces)
    half_each = [i % (PIECES // 2) for i in pieces]
    pairs = [(t, i) for t in range(2) for i in pieces]

    def both(flat):
        return [flat[:PIECES], flat[PIECES:]]

    def basis(i, target):
        t, k = pairs[i]
        return v_ref.at[part(k), side(t)], vbuf.at[p, t, part(k)], target

    def shared_x(i):
        t, k = pairs[i]
        return vbuf.at[px, t, part(k)], sibling_x.at[t, part(k)], (w, ns)

    count = 2 * PIECES
    vx = both(family(lambda i: basis(i, (wx, n)), count, list(range(count))))
    z_arrivals = [0] * PIECES + [1 + 2 * i // PIECES for i in pieces]
    taken_z = taken[1]
    vz = both(family(lambda i: basis(i, (wz, n)), count, z_arrivals))
    vxs = both(family(shared_x, count, list(range(count))))
    quarter = OVER_X // 2
    turned = pl.ds(OVER_X, cols - OVER_X)
    lean_rows = (OVER_X * cols + (rows - OVER_X) * (cols - OVER_X)) // cols
    lean_out = near == (core == x)
    lean_in = far == (core == x)
    lean_relay = far == (core != x)
    ay_sems, ayr_sems = (fresh(0), fresh(1, PIECES)), (fresh(0), fresh(1, PIECES))

    def lean(i):
        return i * piece >= OVER_X

    def moments_y(i, wanted):
        return remote(a_ref.at[part(i), wanted], abuf.at[q, part(i), wanted], (w, ny), ay_sems[0], ay_sems[1] + i)

    def moments_core(i, wanted):
        return remote(abuf.at[qy, part(i), wanted], abuf.at[qy, part(i), wanted], (w, ns), ayr_sems[0], ayr_sems[1] + i)

    full = pl.ds(0, cols)
    ay = [moments_y(i, full) for i in pieces]
    ayr = [moments_core(i, full) for i in pieces]
    ay_lean = [moments_y(i, turned) if lean(i) else ay[i] for i in pieces]
    ayr_lean = [moments_core(i, turned) if lean(i) else ayr[i] for i in pieces]

    def choose(condition, when_true, when_false):
        pl.when(condition)(when_true)
        pl.when(jnp.logical_not(condition))(when_false)

    def start_y(i):
        if lean(i):
            choose(lean_out, ay_lean[i].start, ay[i].start)
        else:
            ay[i].start()

    def relay_y(i):
        if lean(i):
            choose(lean_in, ay_lean[i].wait_recv, ay[i].wait_recv)
            choose(lean_in, ayr_lean[i].start, ayr[i].start)
        else:
            ay[i].wait_recv()
            ayr[i].start()

    def receive_relay(i):
        if lean(i):
            choose(lean_relay, ayr_lean[i].wait_recv, ayr[i].wait_recv)
        else:
            ayr[i].wait_recv()

    def rows_x(k):
        return pl.ds(k * quarter, quarter)

    xo = family(lambda k: (abuf.at[pd, rows_x(k)], opp_x.at[rows_x(k)], (wx, n)), 2, [0, 0])
    xos = family(lambda k: (opp_x.at[rows_x(k)], opp_x.at[rows_x(k)], (w, ns)), 2, [0, 0])
    zo = family(lambda i: (abuf.at[pd, part(i), turned], opp_z.at[part(i)], (wz, n)), PIECES, half_each)
    zos = family(lambda i: (opp_z.at[part(i)], opp_z.at[part(i)], (w, ns)), PIECES, half_each)
    vs = family(lambda i: (v_ref, left.at[core], (w, ns)), 1, [0])[0]
    as_ = family(lambda i: (a_ref, abuf.at[q], (w, ns)), 1, [0])[0]
    steps = range(CHUNKS)
    arrivals = fresh(1, CHUNKS)
    outside = core != y
    lead = jnp.where(outside, x, 1 - x)
    halves = (lead, 1 - lead)
    same_x = (outside.astype(jnp.int32), 1 - outside.astype(jnp.int32))
    block_sends = fresh(0, 8)
    block_cols = wide_half // 2
    right_cols = pl.ds(block_cols, block_cols)

    def ship_rows(t, s, j, wanted):
        apart = 1 - same_x[s]
        return remote(
            partials.at[t, s, j, :, wanted], rows_in.at[2 * apart + y, j, :, wanted],
            (jnp.where(same_x[s] == 1, w, wx), 2 * core + t), block_sends + 4 * t + 2 * s + j // HALF, arrivals + j,
        )

    all_cols = pl.ds(0, wide_half)
    sends = [[[ship_rows(t, s, j, all_cols) for j in steps] for s in range(2)] for t in range(2)]
    thin_sends = {(t, s, j): ship_rows(t, s, j, right_cols) for t, j in THIN for s in range(2)}

    def start_rows(t, s, j):
        if (t, j) in THIN:
            choose(halves[s] == core, thin_sends[t, s, j].start, sends[t][s][j].start)
        else:
            sends[t][s][j].start()

    z_sends, z_recvs = fresh(0, 2), fresh(1, CHUNKS)

    def exchange(j, wanted):
        return remote(zsend.at[j, :, wanted], zrecv.at[j, :, wanted], (wz, n), z_sends + j // HALF, z_recvs + j)

    zc = [exchange(j, all_cols) for j in steps]
    thin_zc = {j: exchange(j, right_cols) for _, j in THIN}
    reflect_send, reflect_recv = fresh(0), fresh(1)
    reflect = [
        remote(msend.at[pl.ds(j * chunk, chunk)], mirror.at[pl.ds(j * chunk, chunk)], (w + y - x, 2 * x + 1), reflect_send, reflect_recv)
        for j in range(HALF)
    ]
    leave = [
        pltpu.make_async_copy(obuf.at[pl.ds(j * chunk, chunk)], o_ref.at[pl.ds(j * chunk, chunk)], out_sem.at[j // HALF])
        for j in steps
    ]

    def all_sent(copies, ref):
        send = next(index for copy, index in origin if copy is copies[0])
        pltpu.make_async_remote_copy(
            src_ref=ref, dst_ref=ref, send_sem=send_sem.at[send], recv_sem=recv_sem.at[0], device_id=(w, ns), device_id_type=MESH,
        ).wait_send()

    def all_here(recv, ref):
        pltpu.make_async_remote_copy(
            src_ref=ref, dst_ref=ref, send_sem=send_sem.at[0], recv_sem=recv_sem.at[recv], device_id=(w, ns), device_id_type=MESH,
        ).wait_recv()

    def owned(i):
        return core == i // (PIECES // 2)

    def split_a(block, i):
        value = abuf[block, i * piece : (i + 1) * piece, :]
        high, low = split(value)
        aparts[block, 0, i * piece : (i + 1) * piece, :] = high
        aparts[block, 1, i * piece : (i + 1) * piece, :] = low

    def split_own(i):
        if not lean(i):
            split_a(p, i)
            return
        span = slice(i * piece, (i + 1) * piece)
        high, low = split(abuf[p, span, OVER_X:])
        aparts[p, 0, span, OVER_X:] = high
        aparts[p, 1, span, OVER_X:] = low
        high, low = split(abuf[p, :OVER_X, span].T)
        aparts[p, 0, span, :OVER_X] = high
        aparts[p, 1, span, :OVER_X] = low

    def turn_left(half, t, i, value):
        high, low = split(value.T)
        leftx_t[half, 0, t * wide_half : (t + 1) * wide_half, i * piece : (i + 1) * piece] = high
        leftx_t[half, 1, t * wide_half : (t + 1) * wide_half, i * piece : (i + 1) * piece] = low

    def turn_own(t, i):
        turn_left(core, t, i, vbuf[px, t, i * piece : (i + 1) * piece, :])

    def turn_sibling(t, i):
        turn_left(1 - core, t, i, sibling_x[t, i * piece : (i + 1) * piece, :])

    def turn_opp(i):
        high, low = split(opp_z[i * piece : (i + 1) * piece, :].T)
        oparts[0, OVER_X:, i * piece : (i + 1) * piece] = high
        oparts[1, OVER_X:, i * piece : (i + 1) * piece] = low

    def split_opp(k):
        high, low = split(opp_x[k * quarter : (k + 1) * quarter, :])
        oparts[0, k * quarter : (k + 1) * quarter, :] = high
        oparts[1, k * quarter : (k + 1) * quarter, :] = low

    def start_opp(i):
        for k in range(2):
            if ((k + 1) * quarter - 1) // piece == i:
                @pl.when(core == k)
                def _():
                    xo[k].start()

        @pl.when(owned(i))
        def _():
            zo[i].start()

    late_ay = far & (core == x)
    early_recv = near & (core != x)
    early_relay = near & (core == x)

    pl.semaphore_wait(barrier, 8)
    for i in pieces:
        vx[0][i].start()
        vz[0][i].start()

    @pl.when(jnp.logical_not(late_ay))
    def _():
        for i in pieces:
            start_y(i)

    as_.start()
    vs.start()
    for i in range(AHEAD_X):
        vx[1][i].start()
    for i in range(AHEAD_Z):
        vz[1][i].start()
    for copy in local:
        copy.wait()
    as_.wait_recv()

    @pl.when(far)
    def _():
        for i in pieces:
            start_opp(i)

    left_t[core, 0], left_t[core, 1] = split(left[core].T)
    for i in pieces:
        split_a(first, i)

    @pl.when(near)
    def _():
        for i in pieces:
            split_a(p, i)

    vs.wait_recv()
    left_t[1 - core, 0], left_t[1 - core, 1] = split(left[1 - core].T)
    for i in pieces:
        @pl.when(early_recv)
        def _():
            relay_y(i)
            start_opp(i)

        vx[0][i].wait_recv()
        vxs[0][i].start()
        turn_own(0, i)

        @pl.when(early_relay)
        def _():
            receive_relay(i)
            start_opp(i)

        if i == 1:
            @pl.when(late_ay)
            def _():
                for k in pieces:
                    start_y(k)

    for i in range(AHEAD_X, PIECES):
        vx[1][i].start()
    for i in range(AHEAD_Z, PIECES):
        vz[1][i].start()
    for i in pieces:
        vxs[0][i].wait_recv()
        turn_sibling(0, i)
    all_here(taken_z, vbuf.at[pz, 0])

    def term(t, block):
        return dot3((aparts[block, 0], aparts[block, 1]), split(vbuf[block, t]))

    total = term(0, first)
    right_p = split(vbuf[p, 0])
    right_third = split(vbuf[third, 0])

    def consume_x(i):
        vxs[1][i].wait_recv()
        turn_sibling(1, i)

    def forward_x(i):
        vx[1][i].wait_recv()
        vxs[1][i].start()
        turn_own(1, i)

    images = []

    def pass_rows(i):
        @pl.when(jnp.logical_not(early_recv))
        def _():
            relay_y(i)

    def finish_rows(i):
        @pl.when(jnp.logical_not(early_relay))
        def _():
            receive_relay(i)

        split_a(third, i)

        @pl.when(far)
        def _():
            split_own(i)

        span = part(i)
        value = total[i * piece : (i + 1) * piece]
        value += dot3((aparts[p, 0, span], aparts[p, 1, span]), right_p)
        value += dot3((aparts[third, 0, span], aparts[third, 1, span]), right_third)
        images.append(split(value))

    def other_part(t, k):
        span = pl.ds(pl.multiple_of(k * wide_half, wide_half), wide_half)
        return dot3((oparts.at[0, :, span][...], oparts.at[1, :, span][...]), split(vbuf[pz, t, span]))

    pass_rows(0)
    pass_rows(1)
    finish_rows(0)
    pass_rows(2)
    finish_rows(1)
    finish_rows(2)
    for k in range(2):
        @pl.when(core == k)
        def _():
            xo[k].wait_recv()
            xos[k].start()
            split_opp(k)

    pass_rows(3)
    for k in range(2):
        @pl.when(core != k)
        def _():
            xos[k].wait_recv()
            split_opp(k)

    for i in pieces:
        @pl.when(owned(i))
        def _():
            zo[i].wait_recv()
            zos[i].start()
            turn_opp(i)

    other = other_part(0, core)
    finish_rows(3)
    for i in pieces:
        @pl.when(jnp.logical_not(owned(i)))
        def _():
            zos[i].wait_recv()
            turn_opp(i)

    own_image = tuple(jnp.concatenate([pair[k] for pair in images], axis=0) for k in range(2))
    other_image = split(other + other_part(0, 1 - core))

    def block_of(half, start, size, image):
        span = pl.ds(start, size)
        own, other = image
        return dot3((left_t[half, 0, span], left_t[half, 1, span]), own) + dot3(
            (leftx_t[half, 0, span], leftx_t[half, 1, span]), other
        )

    swapped = slot_ref[w // GROUP_WIDE]
    same_flag = (((z + swapped + y) % 2) == 0).astype(jnp.int32)
    local_t = jnp.logical_not(outside)
    diagonal = x == y
    whole = core == 0

    def needed(t, s, g, body):
        if t == 0 or g == 1:
            body()

    def send_block(t, s, g, image):
        def body():
            cuts = 2 if (t, s, g) == (0, 0, 0) else 1
            count = HALF // cuts
            for c in range(cuts):
                first_j = g * HALF + c * count
                block = block_of(halves[s], first_j * chunk, count * chunk, image)
                if s == 0:
                    ship(block, first_j, count)
            if s == 1:
                place(block)

        def ship(block, first_j, count):
            for k in range(count):
                partials[t, s, first_j + k] = block[k * chunk : (k + 1) * chunk]
                start_rows(t, s, first_j + k)

        def place(block):
            pl.when(jnp.logical_not(local_t & (core == t)))(lambda: ship(block, g * HALF, HALF))

            @pl.when(local_t & (core == t))
            def _():
                for k in range(HALF):
                    rows_in[y, g * HALF + k] = block[k * chunk : (k + 1) * chunk]

        needed(t, s, g, body)

    def drain_block(t, s, g):
        def body():
            def sent(count):
                all_sent(sends[t][s][g * HALF :], partials.at[t, s, pl.ds(g * HALF, count)])

            if t == g:
                choose(halves[s] == core, lambda: sent(HALF - 1), lambda: sent(HALF))
            else:
                sent(HALF)

        def drain():
            if s == 0:
                body()
            else:
                pl.when(jnp.logical_not(local_t & (core == t)))(body)

        needed(t, s, g, drain)

    def by_width(j, body):
        if any(j == thin for _, thin in THIN):
            choose(diagonal & (core == j // HALF), lambda: body(True, block_cols), lambda: body(False, 0))
        else:
            body(False, 0)

    def gather_rows(j):
        def gather(thin, start):
            wanted = pl.ds(start, wide_half - start)

            @pl.when(local_t)
            def _():
                all_here(arrivals + j, rows_in.at[pl.ds(0, 3), j, :, wanted])

            @pl.when(outside)
            def _():
                all_here(arrivals + j, rows_in.at[:, j, :, wanted])

            same = rows_in[y, j, :, start:] + rows_in[2 + y, j, :, start:]
            other = rows_in[1 - y, j, :, start:] + rows_in[3 - y, j, :, start:]
            mask = jnp.full(same.shape, same_flag) == 1
            zsend[j, :, start:] = jnp.where(mask, other, same)
            (thin_zc if thin else zc)[j].start()
            obuf[pl.ds(j * chunk, chunk), start:] = jnp.where(mask, same, other)

        by_width(j, gather)

    def finish(j):
        def close(thin, start):
            (thin_zc if thin else zc)[j].wait_recv()
            total = obuf[pl.ds(j * chunk, chunk), start:] + zrecv[j, :, start:]
            obuf[pl.ds(j * chunk, chunk), start:] = total
            leave[j].start()
            if j >= HALF and not thin:
                @pl.when(core == 0)
                def _():
                    msend[pl.ds((j - HALF) * chunk, chunk)] = total
                    reflect[j - HALF].start()

        by_width(j, close)
        if j % HALF == HALF // 2 - 1:
            @pl.when(diagonal & (core == j // HALF))
            def _():
                top = (j + 1) * chunk
                obuf[top : top + block_cols, :block_cols] = obuf[top - block_cols : top, block_cols:].T

    image = (own_image, other_image)
    for s in range(2):
        send_block(0, s, 0, image)
    for i in pieces:
        forward_x(i)
    for i in pieces:
        consume_x(i)
    for s in range(2):
        send_block(0, s, 1, image)
    total = term(1, p) + term(1, px)

    def half_term(left, t, k):
        span = pl.ds(k * wide_half, wide_half)
        return dot3((left.at[0, :, span][...], left.at[1, :, span][...]), split(vbuf[pz, t, span]))

    other = None
    for k in range(2):
        all_here(taken_z + 1 + k, vbuf.at[pz, 1, pl.ds(k * wide_half, wide_half)])
        total += half_term(aparts.at[pz], 1, k)
        more = half_term(oparts, 1, k)
        other = more if other is None else other + more
    image = (split(total), split(other))
    for g in range(2):
        for s in range(2):
            send_block(1, s, g, image)

    @pl.when(whole)
    def _():
        for j in range(HALF):
            gather_rows(j)

    for j in range(HALF, CHUNKS):
        gather_rows(j)

    @pl.when(whole)
    def _():
        for j in range(HALF):
            finish(j)
        choose(
            diagonal & (core == 0),
            lambda: all_sent(zc[:HALF], zsend.at[pl.ds(0, HALF - 1)]),
            lambda: all_sent(zc[:HALF], zsend.at[pl.ds(0, HALF)]),
        )

    for j in range(HALF, CHUNKS):
        finish(j)

    @pl.when(jnp.logical_not(whole))
    def _():
        all_here(reflect_recv, mirror)
        obuf[pl.ds(0, HALF * chunk), :] = mirror[...].T
        for j in range(HALF):
            leave[j].start()

    @pl.when(core == 0)
    def _():
        all_sent(reflect, msend)

    for copies in (vx[0], vz[0], vxs[0], [vs], [as_]):
        all_sent(copies, abuf.at[0])
    for copies, condition in ((ay, lean_out), (ayr, lean_in)):
        choose(
            condition,
            lambda: all_sent(copies, abuf.at[0, pl.ds(0, lean_rows)]),
            lambda: all_sent(copies, abuf.at[0]),
        )
    all_sent(xo, opp_x.at[pl.ds(0, quarter)])
    all_sent(xos, opp_x.at[pl.ds(0, quarter)])
    all_sent(zo, opp_z.at[pl.ds(0, rows // 2)])
    all_sent(zos, opp_z.at[pl.ds(0, rows // 2)])
    choose(
        diagonal & (core == 1),
        lambda: all_sent(zc[HALF:], zsend.at[pl.ds(HALF, HALF - 1)]),
        lambda: all_sent(zc[HALF:], zsend.at[pl.ds(HALF, HALF)]),
    )
    for t in range(2):
        for s in range(2):
            for g in range(2):
                drain_block(t, s, g)
    for g in range(2):
        group = pl.ds(g * HALF * chunk, HALF * chunk)
        pltpu.make_async_copy(obuf.at[group], o_ref.at[group], out_sem.at[g]).wait()


def fast_body(moments, eigen_basis, slot_order):
    rows, cols = moments.shape
    f32 = jnp.float32
    chunk = rows // CHUNKS
    wide_half = cols // 2
    return pl.pallas_call(
        kernel,
        out_shape=jax.ShapeDtypeStruct((rows, wide_half), f32),
        in_specs=[
            pl.BlockSpec(memory_space=pltpu.SMEM),
            pl.BlockSpec(memory_space=pl.ANY),
            pl.BlockSpec(memory_space=pl.ANY),
        ],
        out_specs=pl.BlockSpec(memory_space=pl.ANY),
        scratch_shapes=[
            pltpu.VMEM((4, rows, cols), f32),
            pltpu.VMEM((4, 2, rows, cols), jnp.bfloat16),
            pltpu.VMEM((OVER_X, cols), f32),
            pltpu.VMEM((rows, cols - OVER_X), f32),
            pltpu.VMEM((2, cols, rows), jnp.bfloat16),
            pltpu.VMEM((4, 2, rows, wide_half), f32),
            pltpu.VMEM((2, rows, wide_half), f32),
            pltpu.VMEM((2, rows, cols), f32),
            pltpu.VMEM((2, 2, cols, rows), jnp.bfloat16),
            pltpu.VMEM((2, 2, cols, rows), jnp.bfloat16),
            pltpu.VMEM((2, 2, CHUNKS, chunk, wide_half), f32),
            pltpu.VMEM((4, CHUNKS, chunk, wide_half), f32),
            *[pltpu.VMEM((CHUNKS, chunk, wide_half), f32)] * 2,
            *[pltpu.VMEM((HALF * chunk, wide_half), f32)] * 2,
            pltpu.VMEM((rows, wide_half), f32),
            pltpu.SemaphoreType.DMA((4,)),
            pltpu.SemaphoreType.DMA((2,)),
            pltpu.SemaphoreType.DMA((SENDS,)),
            pltpu.SemaphoreType.DMA((RECVS,)),
        ],
        compiler_params=pltpu.CompilerParams(
            collective_id=0, has_side_effects=True, vmem_limit_bytes=53 * 1024 * 1024
        ),
        name="rayleigh",
    )(slot_order, moments, eigen_basis)


def partner(value, axis, stride):
    mask = 2**stride
    pairs = [(source, source ^ mask) for source in range(lax.axis_size(axis))]
    return lax.ppermute(value, axis, pairs)


def body(moments, eigen_basis, slot_order):
    wide_pos = lax.axis_index("wide")
    subproblem = wide_pos // GROUP_WIDE
    position = wide_pos % GROUP_WIDE
    swapped = lax.dynamic_index_in_dim(slot_order, subproblem, 0, keepdims=False)
    narrow_pos = lax.axis_index("narrow")
    col_count = eigen_basis.shape[1]
    half_cols = col_count // 2
    full_basis = lax.all_gather(eigen_basis, "narrow", axis=1, tiled=True)
    first_half = lax.dynamic_slice_in_dim(full_basis, narrow_pos * half_cols, half_cols, 1)
    second_half = lax.dynamic_slice_in_dim(full_basis, K + narrow_pos * half_cols, half_cols, 1)
    local_panel = jnp.concatenate([first_half, second_half], axis=1)
    pair_block = partner(local_panel, "wide", 0)
    joined = jnp.where(
        position % 2 == 0,
        jnp.concatenate([local_panel, pair_block], axis=0),
        jnp.concatenate([pair_block, local_panel], axis=0),
    )
    quad_block = partner(joined, "wide", 1)
    col_panel = jnp.where(
        position // 2 % 2 == 0,
        jnp.concatenate([joined, quad_block], axis=0),
        jnp.concatenate([quad_block, joined], axis=0),
    )
    products = jnp.dot(
        lax.all_gather(moments, "narrow", axis=1, tiled=True),
        col_panel,
        precision=lax.Precision.HIGHEST,
        preferred_element_type=jnp.float32,
    )
    partials = []
    for slot_index in range(2):
        half_panel = products[:, slot_index * half_cols : (slot_index + 1) * half_cols]
        vectors_half = full_basis[:, slot_index * K : (slot_index + 1) * K]
        partials.append(
            lax.dot_general(
                vectors_half,
                half_panel,
                (((0,), (0,)), ((), ())),
                precision=lax.Precision.HIGHEST,
                preferred_element_type=jnp.float32,
            )
        )
    stacked = jnp.stack(partials)
    slot_pick = (position // 2 + swapped) % 2
    row_part = position % 2
    summed = stacked + partner(stacked, "wide", 0)
    summed = summed + partner(summed, "wide", 1)
    chosen = lax.dynamic_index_in_dim(summed, slot_pick, 0, keepdims=False)
    return lax.dynamic_slice_in_dim(chosen, row_part * (K // 2), K // 2, 0)


def solution(mesh):
    placed = (P("wide", "narrow"), P("wide", "narrow"), P())
    cube = mesh.shape["narrow"] == 4
    return jax.shard_map(
        fast_body if cube else body, mesh=mesh, in_specs=placed, out_specs=P("wide", "narrow"), check_vma=False
    )
```

```python
import jax
import jax.numpy as jnp
from jax import lax
from jax.experimental import pallas as pl
from jax.experimental.pallas import tpu as pltpu
from jax.sharding import PartitionSpec as P

GROUP_WIDE = 4
K = 1024
MESH = pl.DeviceIdType.MESH
CHUNKS = 16
HALF = CHUNKS // 2
THIN = tuple((t, t * HALF + j) for t in range(2) for j in range(HALF // 2, HALF))
PIECES = 4
OVER_X = 128
AHEAD_X = 1
AHEAD_Z = 0
SENDS = 22
RECVS = 36 + 2 * CHUNKS


def split(value):
    high = value.astype(jnp.bfloat16)
    low = (value - high.astype(jnp.float32)).astype(jnp.bfloat16)
    return high, low


def dot3(left, right):
    def dot(a, b):
        return jnp.dot(a, b, preferred_element_type=jnp.float32)

    return dot(left[0], right[0]) + (dot(left[0], right[1]) + dot(left[1], right[0]))


def kernel(
    slot_ref, a_ref, v_ref, o_ref,
    abuf, aparts, opp_x, opp_z, oparts, vbuf, sibling_x, left, left_t, leftx_t,
    partials, rows_in, zsend, zrecv, msend, mirror, obuf,
    local_sem, out_sem, send_sem, recv_sem,
):
    rows, cols = a_ref.shape
    wide_half = cols // 2
    piece = rows // PIECES
    chunk = rows // CHUNKS
    w = lax.axis_index("wide")
    n = lax.axis_index("narrow")
    x = w % 2
    z = (w // 2) % 2
    y = n // 2
    core = n % 2
    p = w % 4
    wx = w + 1 - 2 * x
    wz = w + 2 - 4 * z
    px = p + 1 - 2 * x
    pz = p + 2 - 4 * z
    pd = 3 - p
    ns = n + 1 - 2 * core
    ny = n + 2 - 4 * y
    q = 2 * y + core
    qy = 2 * (1 - y) + core
    near = z == y
    far = z != y
    third = jnp.where(near, pz, px)
    first = jnp.where(near, px, pz)

    barrier = pltpu.get_barrier_semaphore()
    for target in ((wz, n), (w, ns), (w, ny), (w, 3 - n), *((wx, m) for m in range(4))):
        pl.semaphore_signal(barrier, inc=1, device_id=target, device_id_type=MESH)

    def part(i):
        return pl.ds(i * piece, piece)

    def side(t):
        return pl.ds(t * wide_half, wide_half)

    local = [
        pltpu.make_async_copy(v_ref, left.at[core], local_sem.at[0]),
        pltpu.make_async_copy(a_ref, abuf.at[q], local_sem.at[1]),
        pltpu.make_async_copy(v_ref.at[:, side(0)], vbuf.at[p, 0], local_sem.at[2]),
        pltpu.make_async_copy(v_ref.at[:, side(1)], vbuf.at[p, 1], local_sem.at[3]),
    ]
    for copy in local:
        copy.start()

    taken = [0, 0]
    origin = []

    def fresh(kind, count=1):
        start = taken[kind]
        taken[kind] += count
        return start

    def remote(src, dst, target, send, recv):
        copy = pltpu.make_async_remote_copy(
            src_ref=src, dst_ref=dst, send_sem=send_sem.at[send], recv_sem=recv_sem.at[recv],
            device_id=target, device_id_type=MESH,
        )
        origin.append((copy, send))
        return copy

    def family(make, count, arrivals):
        send, recv = fresh(0), fresh(1, max(arrivals) + 1)
        return [remote(*make(i), send, recv + arrivals[i]) for i in range(count)]

    pieces = range(PIECES)
    each = list(pieces)
    half_each = [i % (PIECES // 2) for i in pieces]
    pairs = [(t, i) for t in range(2) for i in pieces]

    def both(flat):
        return [flat[:PIECES], flat[PIECES:]]

    def basis(i, target):
        t, k = pairs[i]
        return v_ref.at[part(k), side(t)], vbuf.at[p, t, part(k)], target

    def shared_x(i):
        t, k = pairs[i]
        return vbuf.at[px, t, part(k)], sibling_x.at[t, part(k)], (w, ns)

    count = 2 * PIECES
    vx = both(family(lambda i: basis(i, (wx, n)), count, list(range(count))))
    z_arrivals = [0] * PIECES + [1 + 2 * i // PIECES for i in pieces]
    taken_z = taken[1]
    vz = both(family(lambda i: basis(i, (wz, n)), count, z_arrivals))
    vxs = both(family(shared_x, count, list(range(count))))
    quarter = OVER_X // 2
    turned = pl.ds(OVER_X, cols - OVER_X)
    lean_rows = (OVER_X * cols + (rows - OVER_X) * (cols - OVER_X)) // cols
    lean_out = near == (core == x)
    lean_in = far == (core == x)
    lean_relay = far == (core != x)
    ay_sems, ayr_sems = (fresh(0), fresh(1, PIECES)), (fresh(0), fresh(1, PIECES))

    def lean(i):
        return i * piece >= OVER_X

    def moments_y(i, wanted):
        return remote(a_ref.at[part(i), wanted], abuf.at[q, part(i), wanted], (w, ny), ay_sems[0], ay_sems[1] + i)

    def moments_core(i, wanted):
        return remote(abuf.at[qy, part(i), wanted], abuf.at[qy, part(i), wanted], (w, ns), ayr_sems[0], ayr_sems[1] + i)

    full = pl.ds(0, cols)
    ay = [moments_y(i, full) for i in pieces]
    ayr = [moments_core(i, full) for i in pieces]
    ay_lean = [moments_y(i, turned) if lean(i) else ay[i] for i in pieces]
    ayr_lean = [moments_core(i, turned) if lean(i) else ayr[i] for i in pieces]

    def choose(condition, when_true, when_false):
        pl.when(condition)(when_true)
        pl.when(jnp.logical_not(condition))(when_false)

    def start_y(i):
        if lean(i):
            choose(lean_out, ay_lean[i].start, ay[i].start)
        else:
            ay[i].start()

    def relay_y(i):
        if lean(i):
            choose(lean_in, ay_lean[i].wait_recv, ay[i].wait_recv)
            choose(lean_in, ayr_lean[i].start, ayr[i].start)
        else:
            ay[i].wait_recv()
            ayr[i].start()

    def receive_relay(i):
        if lean(i):
            choose(lean_relay, ayr_lean[i].wait_recv, ayr[i].wait_recv)
        else:
            ayr[i].wait_recv()

    def rows_x(k):
        return pl.ds(k * quarter, quarter)

    xo = family(lambda k: (abuf.at[pd, rows_x(k)], opp_x.at[rows_x(k)], (wx, n)), 2, [0, 0])
    xos = family(lambda k: (opp_x.at[rows_x(k)], opp_x.at[rows_x(k)], (w, ns)), 2, [0, 0])
    zo = family(lambda i: (abuf.at[pd, part(i), turned], opp_z.at[part(i)], (wz, n)), PIECES, half_each)
    zos = family(lambda i: (opp_z.at[part(i)], opp_z.at[part(i)], (w, ns)), PIECES, half_each)
    vs = family(lambda i: (v_ref, left.at[core], (w, ns)), 1, [0])[0]
    as_ = family(lambda i: (a_ref, abuf.at[q], (w, ns)), 1, [0])[0]
    steps = range(CHUNKS)
    arrivals = fresh(1, CHUNKS)
    outside = core != y
    lead = jnp.where(outside, x, 1 - x)
    halves = (lead, 1 - lead)
    same_x = (outside.astype(jnp.int32), 1 - outside.astype(jnp.int32))
    block_sends = fresh(0, 8)
    block_cols = wide_half // 2
    right_cols = pl.ds(block_cols, block_cols)

    def ship_rows(t, s, j, wanted):
        apart = 1 - same_x[s]
        return remote(
            partials.at[t, s, j, :, wanted], rows_in.at[2 * apart + y, j, :, wanted],
            (jnp.where(same_x[s] == 1, w, wx), 2 * core + t), block_sends + 4 * t + 2 * s + j // HALF, arrivals + j,
        )

    all_cols = pl.ds(0, wide_half)
    sends = [[[ship_rows(t, s, j, all_cols) for j in steps] for s in range(2)] for t in range(2)]
    thin_sends = {(t, s, j): ship_rows(t, s, j, right_cols) for t, j in THIN for s in range(2)}

    def start_rows(t, s, j):
        if (t, j) in THIN:
            choose(halves[s] == core, thin_sends[t, s, j].start, sends[t][s][j].start)
        else:
            sends[t][s][j].start()

    z_sends, z_recvs = fresh(0, 2), fresh(1, CHUNKS)

    def exchange(j, wanted):
        return remote(zsend.at[j, :, wanted], zrecv.at[j, :, wanted], (wz, n), z_sends + j // HALF, z_recvs + j)

    zc = [exchange(j, all_cols) for j in steps]
    thin_zc = {j: exchange(j, right_cols) for _, j in THIN}
    reflect_send, reflect_recv = fresh(0), fresh(1)
    reflect = [
        remote(msend.at[pl.ds(j * chunk, chunk)], mirror.at[pl.ds(j * chunk, chunk)], (w + y - x, 2 * x + 1), reflect_send, reflect_recv)
        for j in range(HALF)
    ]
    leave = [
        pltpu.make_async_copy(obuf.at[pl.ds(j * chunk, chunk)], o_ref.at[pl.ds(j * chunk, chunk)], out_sem.at[j // HALF])
        for j in steps
    ]

    def all_sent(copies, ref):
        send = next(index for copy, index in origin if copy is copies[0])
        pltpu.make_async_remote_copy(
            src_ref=ref, dst_ref=ref, send_sem=send_sem.at[send], recv_sem=recv_sem.at[0], device_id=(w, ns), device_id_type=MESH,
        ).wait_send()

    def all_here(recv, ref):
        pltpu.make_async_remote_copy(
            src_ref=ref, dst_ref=ref, send_sem=send_sem.at[0], recv_sem=recv_sem.at[recv], device_id=(w, ns), device_id_type=MESH,
        ).wait_recv()

    def owned(i):
        return core == i // (PIECES // 2)

    def split_a(block, i):
        value = abuf[block, i * piece : (i + 1) * piece, :]
        high, low = split(value)
        aparts[block, 0, i * piece : (i + 1) * piece, :] = high
        aparts[block, 1, i * piece : (i + 1) * piece, :] = low

    def split_own(i):
        if not lean(i):
            split_a(p, i)
            return
        span = slice(i * piece, (i + 1) * piece)
        high, low = split(abuf[p, span, OVER_X:])
        aparts[p, 0, span, OVER_X:] = high
        aparts[p, 1, span, OVER_X:] = low
        high, low = split(abuf[p, :OVER_X, span].T)
        aparts[p, 0, span, :OVER_X] = high
        aparts[p, 1, span, :OVER_X] = low

    def turn_left(half, t, i, value):
        high, low = split(value.T)
        leftx_t[half, 0, t * wide_half : (t + 1) * wide_half, i * piece : (i + 1) * piece] = high
        leftx_t[half, 1, t * wide_half : (t + 1) * wide_half, i * piece : (i + 1) * piece] = low

    def turn_own(t, i):
        turn_left(core, t, i, vbuf[px, t, i * piece : (i + 1) * piece, :])

    def turn_sibling(t, i):
        turn_left(1 - core, t, i, sibling_x[t, i * piece : (i + 1) * piece, :])

    def turn_opp(i):
        high, low = split(opp_z[i * piece : (i + 1) * piece, :].T)
        oparts[0, OVER_X:, i * piece : (i + 1) * piece] = high
        oparts[1, OVER_X:, i * piece : (i + 1) * piece] = low

    def split_opp(k):
        high, low = split(opp_x[k * quarter : (k + 1) * quarter, :])
        oparts[0, k * quarter : (k + 1) * quarter, :] = high
        oparts[1, k * quarter : (k + 1) * quarter, :] = low

    def start_opp(i):
        for k in range(2):
            if ((k + 1) * quarter - 1) // piece == i:
                @pl.when(core == k)
                def _():
                    xo[k].start()

        @pl.when(owned(i))
        def _():
            zo[i].start()

    late_ay = far & (core == x)
    early_recv = near & (core != x)
    early_relay = near & (core == x)

    pl.semaphore_wait(barrier, 8)
    for i in pieces:
        vx[0][i].start()
        vz[0][i].start()

    @pl.when(jnp.logical_not(late_ay))
    def _():
        for i in pieces:
            start_y(i)

    as_.start()
    vs.start()
    for i in range(AHEAD_X):
        vx[1][i].start()
    for i in range(AHEAD_Z):
        vz[1][i].start()
    for copy in local:
        copy.wait()
    as_.wait_recv()

    @pl.when(far)
    def _():
        for i in pieces:
            start_opp(i)

    left_t[core, 0], left_t[core, 1] = split(left[core].T)
    for i in pieces:
        split_a(first, i)

    @pl.when(near)
    def _():
        for i in pieces:
            split_a(p, i)

    vs.wait_recv()
    left_t[1 - core, 0], left_t[1 - core, 1] = split(left[1 - core].T)
    for i in pieces:
        @pl.when(early_recv)
        def _():
            relay_y(i)
            start_opp(i)

        vx[0][i].wait_recv()
        vxs[0][i].start()
        turn_own(0, i)

        @pl.when(early_relay)
        def _():
            receive_relay(i)
            start_opp(i)

        if i == 1:
            @pl.when(late_ay)
            def _():
                for k in pieces:
                    start_y(k)

    for i in range(AHEAD_X, PIECES):
        vx[1][i].start()
    for i in range(AHEAD_Z, PIECES):
        vz[1][i].start()
    for i in pieces:
        vxs[0][i].wait_recv()
        turn_sibling(0, i)
    all_here(taken_z, vbuf.at[pz, 0])

    def term(t, block):
        return dot3((aparts[block, 0], aparts[block, 1]), split(vbuf[block, t]))

    total = term(0, first)
    right_p = split(vbuf[p, 0])
    right_third = split(vbuf[third, 0])

    def consume_x(i):
        vxs[1][i].wait_recv()
        turn_sibling(1, i)

    def forward_x(i):
        vx[1][i].wait_recv()
        vxs[1][i].start()
        turn_own(1, i)

    images = []

    def pass_rows(i):
        @pl.when(jnp.logical_not(early_recv))
        def _():
            relay_y(i)

    def finish_rows(i):
        @pl.when(jnp.logical_not(early_relay))
        def _():
            receive_relay(i)

        split_a(third, i)

        @pl.when(far)
        def _():
            split_own(i)

        span = part(i)
        value = total[i * piece : (i + 1) * piece]
        value += dot3((aparts[p, 0, span], aparts[p, 1, span]), right_p)
        value += dot3((aparts[third, 0, span], aparts[third, 1, span]), right_third)
        images.append(split(value))

    def other_part(t, k):
        span = pl.ds(pl.multiple_of(k * wide_half, wide_half), wide_half)
        return dot3((oparts.at[0, :, span][...], oparts.at[1, :, span][...]), split(vbuf[pz, t, span]))

    pass_rows(0)
    pass_rows(1)
    finish_rows(0)
    pass_rows(2)
    finish_rows(1)
    finish_rows(2)
    for k in range(2):
        @pl.when(core == k)
        def _():
            xo[k].wait_recv()
            xos[k].start()
            split_opp(k)

    pass_rows(3)
    for k in range(2):
        @pl.when(core != k)
        def _():
            xos[k].wait_recv()
            split_opp(k)

    for i in pieces:
        @pl.when(owned(i))
        def _():
            zo[i].wait_recv()
            zos[i].start()
            turn_opp(i)

    other = other_part(0, core)
    finish_rows(3)
    for i in pieces:
        @pl.when(jnp.logical_not(owned(i)))
        def _():
            zos[i].wait_recv()
            turn_opp(i)

    own_image = tuple(jnp.concatenate([pair[k] for pair in images], axis=0) for k in range(2))
    other_image = split(other + other_part(0, 1 - core))

    def block_of(half, start, size, image):
        span = pl.ds(start, size)
        own, other = image
        return dot3((left_t[half, 0, span], left_t[half, 1, span]), own) + dot3(
            (leftx_t[half, 0, span], leftx_t[half, 1, span]), other
        )

    swapped = slot_ref[w // GROUP_WIDE]
    same_flag = (((z + swapped + y) % 2) == 0).astype(jnp.int32)
    local_t = jnp.logical_not(outside)
    diagonal = x == y
    whole = core == 0

    def needed(t, s, g, body):
        if t == 0 or g == 1:
            body()

    def send_block(t, s, g, image):
        def body():
            cuts = 2 if (t, s, g) == (0, 0, 0) else 1
            count = HALF // cuts
            for c in range(cuts):
                first_j = g * HALF + c * count
                block = block_of(halves[s], first_j * chunk, count * chunk, image)
                if s == 0:
                    ship(block, first_j, count)
            if s == 1:
                place(block)

        def ship(block, first_j, count):
            for k in range(count):
                partials[t, s, first_j + k] = block[k * chunk : (k + 1) * chunk]
                start_rows(t, s, first_j + k)

        def place(block):
            pl.when(jnp.logical_not(local_t & (core == t)))(lambda: ship(block, g * HALF, HALF))

            @pl.when(local_t & (core == t))
            def _():
                for k in range(HALF):
                    rows_in[y, g * HALF + k] = block[k * chunk : (k + 1) * chunk]

        needed(t, s, g, body)

    def drain_block(t, s, g):
        def body():
            def sent(count):
                all_sent(sends[t][s][g * HALF :], partials.at[t, s, pl.ds(g * HALF, count)])

            if t == g:
                choose(halves[s] == core, lambda: sent(HALF - HALF // 4), lambda: sent(HALF))
            else:
                sent(HALF)

        def drain():
            if s == 0:
                body()
            else:
                pl.when(jnp.logical_not(local_t & (core == t)))(body)

        needed(t, s, g, drain)

    def by_width(j, body):
        if any(j == thin for _, thin in THIN):
            choose(diagonal & (core == j // HALF), lambda: body(True, block_cols), lambda: body(False, 0))
        else:
            body(False, 0)

    def gather_rows(j):
        def gather(thin, start):
            wanted = pl.ds(start, wide_half - start)

            @pl.when(local_t)
            def _():
                all_here(arrivals + j, rows_in.at[pl.ds(0, 3), j, :, wanted])

            @pl.when(outside)
            def _():
                all_here(arrivals + j, rows_in.at[:, j, :, wanted])

            same = rows_in[y, j, :, start:] + rows_in[2 + y, j, :, start:]
            other = rows_in[1 - y, j, :, start:] + rows_in[3 - y, j, :, start:]
            mask = jnp.full(same.shape, same_flag) == 1
            zsend[j, :, start:] = jnp.where(mask, other, same)
            (thin_zc if thin else zc)[j].start()
            obuf[pl.ds(j * chunk, chunk), start:] = jnp.where(mask, same, other)

        by_width(j, gather)

    def finish(j):
        def close(thin, start):
            (thin_zc if thin else zc)[j].wait_recv()
            total = obuf[pl.ds(j * chunk, chunk), start:] + zrecv[j, :, start:]
            obuf[pl.ds(j * chunk, chunk), start:] = total
            leave[j].start()
            if j >= HALF and not thin:
                @pl.when(core == 0)
                def _():
                    if j == HALF:
                        for s in range(2):
                            drain_block(1, s, 1)
                    msend[pl.ds((j - HALF) * chunk, chunk)] = total
                    reflect[j - HALF].start()

        by_width(j, close)
        if j % HALF == HALF // 2 - 1:
            @pl.when(diagonal & (core == j // HALF))
            def _():
                top = (j + 1) * chunk
                obuf[top : top + block_cols, :block_cols] = obuf[top - block_cols : top, block_cols:].T

    image = (own_image, other_image)
    for s in range(2):
        send_block(0, s, 0, image)
    for i in pieces:
        forward_x(i)
    for i in pieces:
        consume_x(i)
    for s in range(2):
        send_block(0, s, 1, image)
    total = term(1, p) + term(1, px)

    def half_term(left, t, k):
        span = pl.ds(k * wide_half, wide_half)
        return dot3((left.at[0, :, span][...], left.at[1, :, span][...]), split(vbuf[pz, t, span]))

    other = None
    for k in range(2):
        all_here(taken_z + 1 + k, vbuf.at[pz, 1, pl.ds(k * wide_half, wide_half)])
        total += half_term(aparts.at[pz], 1, k)
        more = half_term(oparts, 1, k)
        other = more if other is None else other + more
    image = (split(total), split(other))
    send_block(1, 0, 1, image)

    @pl.when(whole)
    def _():
        for j in range(HALF):
            gather_rows(j)

    send_block(1, 1, 1, image)

    for j in range(HALF, CHUNKS):
        gather_rows(j)

    @pl.when(whole)
    def _():
        for j in range(HALF):
            finish(j)
        choose(
            diagonal & (core == 0),
            lambda: all_sent(zc[:HALF], zsend.at[pl.ds(0, HALF - HALF // 4)]),
            lambda: all_sent(zc[:HALF], zsend.at[pl.ds(0, HALF)]),
        )

    for j in range(HALF, CHUNKS):
        finish(j)

    @pl.when(jnp.logical_not(whole))
    def _():
        all_here(reflect_recv, mirror)
        obuf[pl.ds(0, HALF * chunk), :] = mirror[...].T
        for j in range(HALF):
            leave[j].start()

    @pl.when(core == 0)
    def _():
        all_sent(reflect, msend)

    for copies in (vx[0], vz[0], vxs[0], [vs], [as_]):
        all_sent(copies, abuf.at[0])
    for copies, condition in ((ay, lean_out), (ayr, lean_in)):
        choose(
            condition,
            lambda: all_sent(copies, abuf.at[0, pl.ds(0, lean_rows)]),
            lambda: all_sent(copies, abuf.at[0]),
        )
    all_sent(xo, opp_x.at[pl.ds(0, quarter)])
    all_sent(xos, opp_x.at[pl.ds(0, quarter)])
    all_sent(zo, opp_z.at[pl.ds(0, rows // 2)])
    all_sent(zos, opp_z.at[pl.ds(0, rows // 2)])
    choose(
        diagonal & (core == 1),
        lambda: all_sent(zc[HALF:], zsend.at[pl.ds(HALF, HALF - HALF // 4)]),
        lambda: all_sent(zc[HALF:], zsend.at[pl.ds(HALF, HALF)]),
    )
    for s in range(2):
        for g in range(2):
            drain_block(0, s, g)

    @pl.when(core == 1)
    def _():
        for s in range(2):
            drain_block(1, s, 1)

    for g in range(2):
        group = pl.ds(g * HALF * chunk, HALF * chunk)
        pltpu.make_async_copy(obuf.at[group], o_ref.at[group], out_sem.at[g]).wait()


def fast_body(moments, eigen_basis, slot_order):
    rows, cols = moments.shape
    f32 = jnp.float32
    chunk = rows // CHUNKS
    wide_half = cols // 2
    return pl.pallas_call(
        kernel,
        out_shape=jax.ShapeDtypeStruct((rows, wide_half), f32),
        in_specs=[
            pl.BlockSpec(memory_space=pltpu.SMEM),
            pl.BlockSpec(memory_space=pl.ANY),
            pl.BlockSpec(memory_space=pl.ANY),
        ],
        out_specs=pl.BlockSpec(memory_space=pl.ANY),
        scratch_shapes=[
            pltpu.VMEM((4, rows, cols), f32),
            pltpu.VMEM((4, 2, rows, cols), jnp.bfloat16),
            pltpu.VMEM((OVER_X, cols), f32),
            pltpu.VMEM((rows, cols - OVER_X), f32),
            pltpu.VMEM((2, cols, rows), jnp.bfloat16),
            pltpu.VMEM((4, 2, rows, wide_half), f32),
            pltpu.VMEM((2, rows, wide_half), f32),
            pltpu.VMEM((2, rows, cols), f32),
            pltpu.VMEM((2, 2, cols, rows), jnp.bfloat16),
            pltpu.VMEM((2, 2, cols, rows), jnp.bfloat16),
            pltpu.VMEM((2, 2, CHUNKS, chunk, wide_half), f32),
            pltpu.VMEM((4, CHUNKS, chunk, wide_half), f32),
            *[pltpu.VMEM((CHUNKS, chunk, wide_half), f32)] * 2,
            *[pltpu.VMEM((HALF * chunk, wide_half), f32)] * 2,
            pltpu.VMEM((rows, wide_half), f32),
            pltpu.SemaphoreType.DMA((4,)),
            pltpu.SemaphoreType.DMA((2,)),
            pltpu.SemaphoreType.DMA((SENDS,)),
            pltpu.SemaphoreType.DMA((RECVS,)),
        ],
        compiler_params=pltpu.CompilerParams(
            collective_id=0, has_side_effects=True, vmem_limit_bytes=53 * 1024 * 1024
        ),
        name="rayleigh",
    )(slot_order, moments, eigen_basis)


def partner(value, axis, stride):
    mask = 2**stride
    pairs = [(source, source ^ mask) for source in range(lax.axis_size(axis))]
    return lax.ppermute(value, axis, pairs)


def body(moments, eigen_basis, slot_order):
    wide_pos = lax.axis_index("wide")
    subproblem = wide_pos // GROUP_WIDE
    position = wide_pos % GROUP_WIDE
    swapped = lax.dynamic_index_in_dim(slot_order, subproblem, 0, keepdims=False)
    narrow_pos = lax.axis_index("narrow")
    col_count = eigen_basis.shape[1]
    half_cols = col_count // 2
    full_basis = lax.all_gather(eigen_basis, "narrow", axis=1, tiled=True)
    first_half = lax.dynamic_slice_in_dim(full_basis, narrow_pos * half_cols, half_cols, 1)
    second_half = lax.dynamic_slice_in_dim(full_basis, K + narrow_pos * half_cols, half_cols, 1)
    local_panel = jnp.concatenate([first_half, second_half], axis=1)
    pair_block = partner(local_panel, "wide", 0)
    joined = jnp.where(
        position % 2 == 0,
        jnp.concatenate([local_panel, pair_block], axis=0),
        jnp.concatenate([pair_block, local_panel], axis=0),
    )
    quad_block = partner(joined, "wide", 1)
    col_panel = jnp.where(
        position // 2 % 2 == 0,
        jnp.concatenate([joined, quad_block], axis=0),
        jnp.concatenate([quad_block, joined], axis=0),
    )
    products = jnp.dot(
        lax.all_gather(moments, "narrow", axis=1, tiled=True),
        col_panel,
        precision=lax.Precision.HIGHEST,
        preferred_element_type=jnp.float32,
    )
    partials = []
    for slot_index in range(2):
        half_panel = products[:, slot_index * half_cols : (slot_index + 1) * half_cols]
        vectors_half = full_basis[:, slot_index * K : (slot_index + 1) * K]
        partials.append(
            lax.dot_general(
                vectors_half,
                half_panel,
                (((0,), (0,)), ((), ())),
                precision=lax.Precision.HIGHEST,
                preferred_element_type=jnp.float32,
            )
        )
    stacked = jnp.stack(partials)
    slot_pick = (position // 2 + swapped) % 2
    row_part = position % 2
    summed = stacked + partner(stacked, "wide", 0)
    summed = summed + partner(summed, "wide", 1)
    chosen = lax.dynamic_index_in_dim(summed, slot_pick, 0, keepdims=False)
    return lax.dynamic_slice_in_dim(chosen, row_part * (K // 2), K // 2, 0)


def solution(mesh):
    placed = (P("wide", "narrow"), P("wide", "narrow"), P())
    cube = mesh.shape["narrow"] == 4
    return jax.shard_map(
        fast_body if cube else body, mesh=mesh, in_specs=placed, out_specs=P("wide", "narrow"), check_vma=False
    )
```

```python
import jax
import jax.numpy as jnp
from jax import lax
from jax.experimental import pallas as pl
from jax.experimental.pallas import tpu as pltpu
from jax.sharding import PartitionSpec as P

GROUP_WIDE = 4
K = 1024
MESH = pl.DeviceIdType.MESH
CHUNKS = 16
HALF = CHUNKS // 2
THIN = tuple((t, t * HALF + j) for t in range(2) for j in range(HALF // 2, HALF))
PIECES = 4
OVER_X = 128
AHEAD_X = 1
AHEAD_Z = 0
SENDS = 22
RECVS = 36 + 2 * CHUNKS


def split(value):
    high = value.astype(jnp.bfloat16)
    low = (value - high.astype(jnp.float32)).astype(jnp.bfloat16)
    return high, low


def dot3(left, right):
    def dot(a, b):
        return jnp.dot(a, b, preferred_element_type=jnp.float32)

    return dot(left[0], right[0]) + (dot(left[0], right[1]) + dot(left[1], right[0]))


def kernel(
    slot_ref, a_ref, v_ref, o_ref,
    abuf, aparts, opp_x, opp_z, oparts, vbuf, sibling_x, left, left_t, leftx_t,
    partials, rows_in, zsend, zrecv, msend, mirror, obuf,
    local_sem, out_sem, send_sem, recv_sem,
):
    rows, cols = a_ref.shape
    wide_half = cols // 2
    piece = rows // PIECES
    chunk = rows // CHUNKS
    w = lax.axis_index("wide")
    n = lax.axis_index("narrow")
    x = w % 2
    z = (w // 2) % 2
    y = n // 2
    core = n % 2
    p = w % 4
    wx = w + 1 - 2 * x
    wz = w + 2 - 4 * z
    px = p + 1 - 2 * x
    pz = p + 2 - 4 * z
    pd = 3 - p
    ns = n + 1 - 2 * core
    ny = n + 2 - 4 * y
    q = 2 * y + core
    qy = 2 * (1 - y) + core
    near = z == y
    far = z != y
    third = jnp.where(near, pz, px)
    first = jnp.where(near, px, pz)

    barrier = pltpu.get_barrier_semaphore()
    for target in ((wz, n), (w, ns), (w, ny), (w, 3 - n), *((wx, m) for m in range(4))):
        pl.semaphore_signal(barrier, inc=1, device_id=target, device_id_type=MESH)

    def part(i):
        return pl.ds(i * piece, piece)

    def side(t):
        return pl.ds(t * wide_half, wide_half)

    local = [
        pltpu.make_async_copy(v_ref, left.at[core], local_sem.at[0]),
        pltpu.make_async_copy(a_ref, abuf.at[q], local_sem.at[1]),
        pltpu.make_async_copy(v_ref.at[:, side(0)], vbuf.at[p, 0], local_sem.at[2]),
        pltpu.make_async_copy(v_ref.at[:, side(1)], vbuf.at[p, 1], local_sem.at[3]),
    ]
    for copy in local:
        copy.start()

    taken = [0, 0]
    origin = []

    def fresh(kind, count=1):
        start = taken[kind]
        taken[kind] += count
        return start

    def remote(src, dst, target, send, recv):
        copy = pltpu.make_async_remote_copy(
            src_ref=src, dst_ref=dst, send_sem=send_sem.at[send], recv_sem=recv_sem.at[recv],
            device_id=target, device_id_type=MESH,
        )
        origin.append((copy, send))
        return copy

    def family(make, count, arrivals):
        send, recv = fresh(0), fresh(1, max(arrivals) + 1)
        return [remote(*make(i), send, recv + arrivals[i]) for i in range(count)]

    pieces = range(PIECES)
    each = list(pieces)
    half_each = [i % (PIECES // 2) for i in pieces]
    pairs = [(t, i) for t in range(2) for i in pieces]

    def both(flat):
        return [flat[:PIECES], flat[PIECES:]]

    def basis(i, target):
        t, k = pairs[i]
        return v_ref.at[part(k), side(t)], vbuf.at[p, t, part(k)], target

    def shared_x(i):
        t, k = pairs[i]
        return vbuf.at[px, t, part(k)], sibling_x.at[t, part(k)], (w, ns)

    count = 2 * PIECES
    vx = both(family(lambda i: basis(i, (wx, n)), count, list(range(count))))
    z_arrivals = [0] * PIECES + [1 + 2 * i // PIECES for i in pieces]
    taken_z = taken[1]
    vz = both(family(lambda i: basis(i, (wz, n)), count, z_arrivals))
    vxs = both(family(shared_x, count, list(range(count))))
    quarter = OVER_X // 2
    turned = pl.ds(OVER_X, cols - OVER_X)
    lean_rows = (OVER_X * cols + (rows - OVER_X) * (cols - OVER_X)) // cols
    lean_out = near == (core == x)
    lean_in = far == (core == x)
    lean_relay = far == (core != x)
    ay_sems, ayr_sems = (fresh(0), fresh(1, PIECES)), (fresh(0), fresh(1, PIECES))

    def lean(i):
        return i * piece >= OVER_X

    def moments_y(i, wanted):
        return remote(a_ref.at[part(i), wanted], abuf.at[q, part(i), wanted], (w, ny), ay_sems[0], ay_sems[1] + i)

    def moments_core(i, wanted):
        return remote(abuf.at[qy, part(i), wanted], abuf.at[qy, part(i), wanted], (w, ns), ayr_sems[0], ayr_sems[1] + i)

    full = pl.ds(0, cols)
    ay = [moments_y(i, full) for i in pieces]
    ayr = [moments_core(i, full) for i in pieces]
    ay_lean = [moments_y(i, turned) if lean(i) else ay[i] for i in pieces]
    ayr_lean = [moments_core(i, turned) if lean(i) else ayr[i] for i in pieces]

    def choose(condition, when_true, when_false):
        pl.when(condition)(when_true)
        pl.when(jnp.logical_not(condition))(when_false)

    def start_y(i):
        if lean(i):
            choose(lean_out, ay_lean[i].start, ay[i].start)
        else:
            ay[i].start()

    def relay_y(i):
        if lean(i):
            choose(lean_in, ay_lean[i].wait_recv, ay[i].wait_recv)
            choose(lean_in, ayr_lean[i].start, ayr[i].start)
        else:
            ay[i].wait_recv()
            ayr[i].start()

    def receive_relay(i):
        if lean(i):
            choose(lean_relay, ayr_lean[i].wait_recv, ayr[i].wait_recv)
        else:
            ayr[i].wait_recv()

    def rows_x(k):
        return pl.ds(k * quarter, quarter)

    xo = family(lambda k: (abuf.at[pd, rows_x(k)], opp_x.at[rows_x(k)], (wx, n)), 2, [0, 0])
    xos = family(lambda k: (opp_x.at[rows_x(k)], opp_x.at[rows_x(k)], (w, ns)), 2, [0, 0])
    zo = family(lambda i: (abuf.at[pd, part(i), turned], opp_z.at[part(i)], (wz, n)), PIECES, half_each)
    zos = family(lambda i: (opp_z.at[part(i)], opp_z.at[part(i)], (w, ns)), PIECES, half_each)
    vs = family(lambda i: (v_ref, left.at[core], (w, ns)), 1, [0])[0]
    as_ = family(lambda i: (a_ref, abuf.at[q], (w, ns)), 1, [0])[0]
    steps = range(CHUNKS)
    arrivals = fresh(1, CHUNKS)
    outside = core != y
    lead = jnp.where(outside, x, 1 - x)
    halves = (lead, 1 - lead)
    same_x = (outside.astype(jnp.int32), 1 - outside.astype(jnp.int32))
    block_sends = fresh(0, 8)
    block_cols = wide_half // 2
    right_cols = pl.ds(block_cols, block_cols)

    def ship_rows(t, s, j, wanted):
        apart = 1 - same_x[s]
        return remote(
            partials.at[t, s, j, :, wanted], rows_in.at[2 * apart + y, j, :, wanted],
            (jnp.where(same_x[s] == 1, w, wx), 2 * core + t), block_sends + 4 * t + 2 * s + j // HALF, arrivals + j,
        )

    all_cols = pl.ds(0, wide_half)
    sends = [[[ship_rows(t, s, j, all_cols) for j in steps] for s in range(2)] for t in range(2)]
    thin_sends = {(t, s, j): ship_rows(t, s, j, right_cols) for t, j in THIN for s in range(2)}

    def start_rows(t, s, j):
        if (t, j) in THIN:
            choose(halves[s] == core, thin_sends[t, s, j].start, sends[t][s][j].start)
        else:
            sends[t][s][j].start()

    z_sends, z_recvs = fresh(0, 2), fresh(1, CHUNKS)

    def exchange(j, wanted):
        return remote(zsend.at[j, :, wanted], zrecv.at[j, :, wanted], (wz, n), z_sends + j // HALF, z_recvs + j)

    zc = [exchange(j, all_cols) for j in steps]
    thin_zc = {j: exchange(j, right_cols) for _, j in THIN}
    reflect_send, reflect_recv = fresh(0), fresh(1)
    reflect = [
        remote(msend.at[pl.ds(j * chunk, chunk)], mirror.at[pl.ds(j * chunk, chunk)], (w + y - x, 2 * x + 1), reflect_send, reflect_recv)
        for j in range(HALF)
    ]
    leave = [
        pltpu.make_async_copy(obuf.at[pl.ds(j * chunk, chunk)], o_ref.at[pl.ds(j * chunk, chunk)], out_sem.at[j // HALF])
        for j in steps
    ]

    def all_sent(copies, ref):
        send = next(index for copy, index in origin if copy is copies[0])
        pltpu.make_async_remote_copy(
            src_ref=ref, dst_ref=ref, send_sem=send_sem.at[send], recv_sem=recv_sem.at[0], device_id=(w, ns), device_id_type=MESH,
        ).wait_send()

    def all_here(recv, ref):
        pltpu.make_async_remote_copy(
            src_ref=ref, dst_ref=ref, send_sem=send_sem.at[0], recv_sem=recv_sem.at[recv], device_id=(w, ns), device_id_type=MESH,
        ).wait_recv()

    def owned(i):
        return core == i // (PIECES // 2)

    def split_a(block, i):
        value = abuf[block, i * piece : (i + 1) * piece, :]
        high, low = split(value)
        aparts[block, 0, i * piece : (i + 1) * piece, :] = high
        aparts[block, 1, i * piece : (i + 1) * piece, :] = low

    def split_own(i):
        if not lean(i):
            split_a(p, i)
            return
        span = slice(i * piece, (i + 1) * piece)
        high, low = split(abuf[p, span, OVER_X:])
        aparts[p, 0, span, OVER_X:] = high
        aparts[p, 1, span, OVER_X:] = low
        high, low = split(abuf[p, :OVER_X, span].T)
        aparts[p, 0, span, :OVER_X] = high
        aparts[p, 1, span, :OVER_X] = low

    def turn_left(half, t, i, value):
        high, low = split(value.T)
        leftx_t[half, 0, t * wide_half : (t + 1) * wide_half, i * piece : (i + 1) * piece] = high
        leftx_t[half, 1, t * wide_half : (t + 1) * wide_half, i * piece : (i + 1) * piece] = low

    def turn_own(t, i):
        turn_left(core, t, i, vbuf[px, t, i * piece : (i + 1) * piece, :])

    def turn_sibling(t, i):
        turn_left(1 - core, t, i, sibling_x[t, i * piece : (i + 1) * piece, :])

    def turn_opp(i):
        high, low = split(opp_z[i * piece : (i + 1) * piece, :].T)
        oparts[0, OVER_X:, i * piece : (i + 1) * piece] = high
        oparts[1, OVER_X:, i * piece : (i + 1) * piece] = low

    def split_opp(k):
        high, low = split(opp_x[k * quarter : (k + 1) * quarter, :])
        oparts[0, k * quarter : (k + 1) * quarter, :] = high
        oparts[1, k * quarter : (k + 1) * quarter, :] = low

    def start_opp(i):
        for k in range(2):
            if ((k + 1) * quarter - 1) // piece == i:
                @pl.when(core == k)
                def _():
                    xo[k].start()

        @pl.when(owned(i))
        def _():
            zo[i].start()

    late_ay = far & (core == x)
    early_recv = near & (core != x)
    early_relay = near & (core == x)

    pl.semaphore_wait(barrier, 8)
    @pl.when(jnp.logical_not(late_ay))
    def _():
        for i in pieces:
            start_y(i)

    for i in pieces:
        vx[0][i].start()
        vz[0][i].start()

    as_.start()
    vs.start()
    for i in range(AHEAD_X):
        vx[1][i].start()
    for i in range(AHEAD_Z):
        vz[1][i].start()
    for copy in local:
        copy.wait()
    as_.wait_recv()

    @pl.when(far)
    def _():
        for i in pieces:
            start_opp(i)

    left_t[core, 0], left_t[core, 1] = split(left[core].T)
    for i in pieces:
        split_a(first, i)

    @pl.when(near)
    def _():
        for i in pieces:
            split_a(p, i)

    vs.wait_recv()
    left_t[1 - core, 0], left_t[1 - core, 1] = split(left[1 - core].T)
    for i in pieces:
        @pl.when(early_recv)
        def _():
            relay_y(i)
            start_opp(i)

        vx[0][i].wait_recv()
        vxs[0][i].start()
        turn_own(0, i)

        @pl.when(early_relay)
        def _():
            receive_relay(i)
            start_opp(i)

        if i == 1:
            @pl.when(late_ay)
            def _():
                for k in pieces:
                    start_y(k)

    for i in range(AHEAD_X, PIECES):
        vx[1][i].start()
    for i in range(AHEAD_Z, PIECES):
        vz[1][i].start()
    for i in pieces:
        vxs[0][i].wait_recv()
        turn_sibling(0, i)
    all_here(taken_z, vbuf.at[pz, 0])

    def term(t, block):
        return dot3((aparts[block, 0], aparts[block, 1]), split(vbuf[block, t]))

    total = term(0, first)
    right_p = split(vbuf[p, 0])
    right_third = split(vbuf[third, 0])

    def consume_x(i):
        vxs[1][i].wait_recv()
        turn_sibling(1, i)

    def forward_x(i):
        vx[1][i].wait_recv()
        vxs[1][i].start()
        turn_own(1, i)

    images = []

    def pass_rows(i):
        @pl.when(jnp.logical_not(early_recv))
        def _():
            relay_y(i)

    def finish_rows(i):
        @pl.when(jnp.logical_not(early_relay))
        def _():
            receive_relay(i)

        split_a(third, i)

        @pl.when(far)
        def _():
            split_own(i)

        span = part(i)
        value = total[i * piece : (i + 1) * piece]
        value += dot3((aparts[p, 0, span], aparts[p, 1, span]), right_p)
        value += dot3((aparts[third, 0, span], aparts[third, 1, span]), right_third)
        images.append(split(value))

    def other_part(t, k):
        span = pl.ds(pl.multiple_of(k * wide_half, wide_half), wide_half)
        return dot3((oparts.at[0, :, span][...], oparts.at[1, :, span][...]), split(vbuf[pz, t, span]))

    pass_rows(0)
    pass_rows(1)
    finish_rows(0)
    pass_rows(2)
    finish_rows(1)
    finish_rows(2)
    for k in range(2):
        @pl.when(core == k)
        def _():
            xo[k].wait_recv()
            xos[k].start()
            split_opp(k)

    pass_rows(3)
    for k in range(2):
        @pl.when(core != k)
        def _():
            xos[k].wait_recv()
            split_opp(k)

    for i in pieces:
        @pl.when(owned(i))
        def _():
            zo[i].wait_recv()
            zos[i].start()
            turn_opp(i)

    other = other_part(0, core)
    finish_rows(3)
    for i in pieces:
        @pl.when(jnp.logical_not(owned(i)))
        def _():
            zos[i].wait_recv()
            turn_opp(i)

    own_image = tuple(jnp.concatenate([pair[k] for pair in images], axis=0) for k in range(2))
    other_image = split(other + other_part(0, 1 - core))

    def block_of(half, start, size, image):
        span = pl.ds(start, size)
        own, other = image
        return dot3((left_t[half, 0, span], left_t[half, 1, span]), own) + dot3(
            (leftx_t[half, 0, span], leftx_t[half, 1, span]), other
        )

    swapped = slot_ref[w // GROUP_WIDE]
    same_flag = (((z + swapped + y) % 2) == 0).astype(jnp.int32)
    local_t = jnp.logical_not(outside)
    diagonal = x == y
    whole = core == 0

    def needed(t, s, g, body):
        if t == 0 or g == 1:
            body()

    def send_block(t, s, g, image):
        def body():
            cuts = 2 if s == 0 and g == t else 1
            count = HALF // cuts
            for c in range(cuts):
                first_j = g * HALF + c * count
                block = block_of(halves[s], first_j * chunk, count * chunk, image)
                if s == 0:
                    ship(block, first_j, count)
            if s == 1:
                place(block)

        def ship(block, first_j, count):
            for k in range(count):
                partials[t, s, first_j + k] = block[k * chunk : (k + 1) * chunk]
                start_rows(t, s, first_j + k)

        def place(block):
            pl.when(jnp.logical_not(local_t & (core == t)))(lambda: ship(block, g * HALF, HALF))

            @pl.when(local_t & (core == t))
            def _():
                for k in range(HALF):
                    rows_in[y, g * HALF + k] = block[k * chunk : (k + 1) * chunk]

        needed(t, s, g, body)

    def drain_block(t, s, g):
        def body():
            def sent(count):
                all_sent(sends[t][s][g * HALF :], partials.at[t, s, pl.ds(g * HALF, count)])

            if t == g:
                choose(halves[s] == core, lambda: sent(HALF - HALF // 4), lambda: sent(HALF))
            else:
                sent(HALF)

        def drain():
            if s == 0:
                body()
            else:
                pl.when(jnp.logical_not(local_t & (core == t)))(body)

        needed(t, s, g, drain)

    def by_width(j, body):
        if any(j == thin for _, thin in THIN):
            choose(diagonal & (core == j // HALF), lambda: body(True, block_cols), lambda: body(False, 0))
        else:
            body(False, 0)

    def gather_rows(j):
        def gather(thin, start):
            wanted = pl.ds(start, wide_half - start)

            @pl.when(local_t)
            def _():
                all_here(arrivals + j, rows_in.at[pl.ds(0, 3), j, :, wanted])

            @pl.when(outside)
            def _():
                all_here(arrivals + j, rows_in.at[:, j, :, wanted])

            same = rows_in[y, j, :, start:] + rows_in[2 + y, j, :, start:]
            other = rows_in[1 - y, j, :, start:] + rows_in[3 - y, j, :, start:]
            mask = jnp.full(same.shape, same_flag) == 1
            zsend[j, :, start:] = jnp.where(mask, other, same)
            (thin_zc if thin else zc)[j].start()
            obuf[pl.ds(j * chunk, chunk), start:] = jnp.where(mask, same, other)

        by_width(j, gather)

    def finish(j):
        def close(thin, start):
            (thin_zc if thin else zc)[j].wait_recv()
            total = obuf[pl.ds(j * chunk, chunk), start:] + zrecv[j, :, start:]
            obuf[pl.ds(j * chunk, chunk), start:] = total
            leave[j].start()
            if j >= HALF and not thin:
                @pl.when(core == 0)
                def _():
                    if j == HALF:
                        for s in range(2):
                            drain_block(1, s, 1)
                    msend[pl.ds((j - HALF) * chunk, chunk)] = total
                    reflect[j - HALF].start()

        by_width(j, close)
        if j % HALF == HALF // 2 - 1:
            @pl.when(diagonal & (core == j // HALF))
            def _():
                top = (j + 1) * chunk
                obuf[top : top + block_cols, :block_cols] = obuf[top - block_cols : top, block_cols:].T

    image = (own_image, other_image)
    for s in range(2):
        send_block(0, s, 0, image)
    for i in pieces:
        forward_x(i)
    for i in pieces:
        consume_x(i)
    for s in range(2):
        send_block(0, s, 1, image)
    total = term(1, p) + term(1, px)

    def half_term(left, t, k):
        span = pl.ds(k * wide_half, wide_half)
        return dot3((left.at[0, :, span][...], left.at[1, :, span][...]), split(vbuf[pz, t, span]))

    other = None
    for k in range(2):
        all_here(taken_z + 1 + k, vbuf.at[pz, 1, pl.ds(k * wide_half, wide_half)])
        total += half_term(aparts.at[pz], 1, k)
        more = half_term(oparts, 1, k)
        other = more if other is None else other + more
    image = (split(total), split(other))
    send_block(1, 0, 1, image)

    @pl.when(whole)
    def _():
        for j in range(HALF):
            gather_rows(j)

    send_block(1, 1, 1, image)

    for j in range(HALF, CHUNKS):
        gather_rows(j)

    @pl.when(whole)
    def _():
        for j in range(HALF):
            finish(j)
        choose(
            diagonal & (core == 0),
            lambda: all_sent(zc[:HALF], zsend.at[pl.ds(0, HALF - HALF // 4)]),
            lambda: all_sent(zc[:HALF], zsend.at[pl.ds(0, HALF)]),
        )

    for j in range(HALF, CHUNKS):
        finish(j)

    @pl.when(jnp.logical_not(whole))
    def _():
        all_here(reflect_recv, mirror)
        obuf[pl.ds(0, HALF * chunk), :] = mirror[...].T
        for j in range(HALF):
            leave[j].start()

    @pl.when(core == 0)
    def _():
        all_sent(reflect, msend)

    for copies in (vx[0], vz[0], vxs[0], [vs], [as_]):
        all_sent(copies, abuf.at[0])
    for copies, condition in ((ay, lean_out), (ayr, lean_in)):
        choose(
            condition,
            lambda: all_sent(copies, abuf.at[0, pl.ds(0, lean_rows)]),
            lambda: all_sent(copies, abuf.at[0]),
        )
    all_sent(xo, opp_x.at[pl.ds(0, quarter)])
    all_sent(xos, opp_x.at[pl.ds(0, quarter)])
    all_sent(zo, opp_z.at[pl.ds(0, rows // 2)])
    all_sent(zos, opp_z.at[pl.ds(0, rows // 2)])
    choose(
        diagonal & (core == 1),
        lambda: all_sent(zc[HALF:], zsend.at[pl.ds(HALF, HALF - HALF // 4)]),
        lambda: all_sent(zc[HALF:], zsend.at[pl.ds(HALF, HALF)]),
    )
    for s in range(2):
        for g in range(2):
            drain_block(0, s, g)

    @pl.when(core == 1)
    def _():
        for s in range(2):
            drain_block(1, s, 1)

    for g in range(2):
        group = pl.ds(g * HALF * chunk, HALF * chunk)
        pltpu.make_async_copy(obuf.at[group], o_ref.at[group], out_sem.at[g]).wait()


def fast_body(moments, eigen_basis, slot_order):
    rows, cols = moments.shape
    f32 = jnp.float32
    chunk = rows // CHUNKS
    wide_half = cols // 2
    return pl.pallas_call(
        kernel,
        out_shape=jax.ShapeDtypeStruct((rows, wide_half), f32),
        in_specs=[
            pl.BlockSpec(memory_space=pltpu.SMEM),
            pl.BlockSpec(memory_space=pl.ANY),
            pl.BlockSpec(memory_space=pl.ANY),
        ],
        out_specs=pl.BlockSpec(memory_space=pl.ANY),
        scratch_shapes=[
            pltpu.VMEM((4, rows, cols), f32),
            pltpu.VMEM((4, 2, rows, cols), jnp.bfloat16),
            pltpu.VMEM((OVER_X, cols), f32),
            pltpu.VMEM((rows, cols - OVER_X), f32),
            pltpu.VMEM((2, cols, rows), jnp.bfloat16),
            pltpu.VMEM((4, 2, rows, wide_half), f32),
            pltpu.VMEM((2, rows, wide_half), f32),
            pltpu.VMEM((2, rows, cols), f32),
            pltpu.VMEM((2, 2, cols, rows), jnp.bfloat16),
            pltpu.VMEM((2, 2, cols, rows), jnp.bfloat16),
            pltpu.VMEM((2, 2, CHUNKS, chunk, wide_half), f32),
            pltpu.VMEM((4, CHUNKS, chunk, wide_half), f32),
            *[pltpu.VMEM((CHUNKS, chunk, wide_half), f32)] * 2,
            *[pltpu.VMEM((HALF * chunk, wide_half), f32)] * 2,
            pltpu.VMEM((rows, wide_half), f32),
            pltpu.SemaphoreType.DMA((4,)),
            pltpu.SemaphoreType.DMA((2,)),
            pltpu.SemaphoreType.DMA((SENDS,)),
            pltpu.SemaphoreType.DMA((RECVS,)),
        ],
        compiler_params=pltpu.CompilerParams(
            collective_id=0, has_side_effects=True, vmem_limit_bytes=53 * 1024 * 1024
        ),
        name="rayleigh",
    )(slot_order, moments, eigen_basis)


def partner(value, axis, stride):
    mask = 2**stride
    pairs = [(source, source ^ mask) for source in range(lax.axis_size(axis))]
    return lax.ppermute(value, axis, pairs)


def body(moments, eigen_basis, slot_order):
    wide_pos = lax.axis_index("wide")
    subproblem = wide_pos // GROUP_WIDE
    position = wide_pos % GROUP_WIDE
    swapped = lax.dynamic_index_in_dim(slot_order, subproblem, 0, keepdims=False)
    narrow_pos = lax.axis_index("narrow")
    col_count = eigen_basis.shape[1]
    half_cols = col_count // 2
    full_basis = lax.all_gather(eigen_basis, "narrow", axis=1, tiled=True)
    first_half = lax.dynamic_slice_in_dim(full_basis, narrow_pos * half_cols, half_cols, 1)
    second_half = lax.dynamic_slice_in_dim(full_basis, K + narrow_pos * half_cols, half_cols, 1)
    local_panel = jnp.concatenate([first_half, second_half], axis=1)
    pair_block = partner(local_panel, "wide", 0)
    joined = jnp.where(
        position % 2 == 0,
        jnp.concatenate([local_panel, pair_block], axis=0),
        jnp.concatenate([pair_block, local_panel], axis=0),
    )
    quad_block = partner(joined, "wide", 1)
    col_panel = jnp.where(
        position // 2 % 2 == 0,
        jnp.concatenate([joined, quad_block], axis=0),
        jnp.concatenate([quad_block, joined], axis=0),
    )
    products = jnp.dot(
        lax.all_gather(moments, "narrow", axis=1, tiled=True),
        col_panel,
        precision=lax.Precision.HIGHEST,
        preferred_element_type=jnp.float32,
    )
    partials = []
    for slot_index in range(2):
        half_panel = products[:, slot_index * half_cols : (slot_index + 1) * half_cols]
        vectors_half = full_basis[:, slot_index * K : (slot_index + 1) * K]
        partials.append(
            lax.dot_general(
                vectors_half,
                half_panel,
                (((0,), (0,)), ((), ())),
                precision=lax.Precision.HIGHEST,
                preferred_element_type=jnp.float32,
            )
        )
    stacked = jnp.stack(partials)
    slot_pick = (position // 2 + swapped) % 2
    row_part = position % 2
    summed = stacked + partner(stacked, "wide", 0)
    summed = summed + partner(summed, "wide", 1)
    chosen = lax.dynamic_index_in_dim(summed, slot_pick, 0, keepdims=False)
    return lax.dynamic_slice_in_dim(chosen, row_part * (K // 2), K // 2, 0)


def solution(mesh):
    placed = (P("wide", "narrow"), P("wide", "narrow"), P())
    cube = mesh.shape["narrow"] == 4
    return jax.shard_map(
        fast_body if cube else body, mesh=mesh, in_specs=placed, out_specs=P("wide", "narrow"), check_vma=False
    )
```

```python
import jax
import jax.numpy as jnp
from jax import lax
from jax.experimental import pallas as pl
from jax.experimental.pallas import tpu as pltpu
from jax.sharding import PartitionSpec as P

GROUP_WIDE = 4
K = 1024
MESH = pl.DeviceIdType.MESH
CHUNKS = 16
HALF = CHUNKS // 2
THIN = tuple((t, t * HALF + j) for t in range(2) for j in range(HALF // 2, HALF))
PIECES = 4
OVER_X = 128
AHEAD_X = 1
AHEAD_Z = 0
SENDS = 22
RECVS = 36 + 2 * CHUNKS


def split(value):
    high = value.astype(jnp.bfloat16)
    low = (value - high.astype(jnp.float32)).astype(jnp.bfloat16)
    return high, low


def dot3(left, right):
    def dot(a, b):
        return jnp.dot(a, b, preferred_element_type=jnp.float32)

    return dot(left[0], right[0]) + (dot(left[0], right[1]) + dot(left[1], right[0]))


def kernel(
    slot_ref, a_ref, v_ref, o_ref,
    abuf, aparts, opp_x, opp_z, oparts, vbuf, sibling_x, left, left_t, leftx_t,
    partials, rows_in, zsend, zrecv, msend, mirror, obuf,
    local_sem, out_sem, send_sem, recv_sem,
):
    rows, cols = a_ref.shape
    wide_half = cols // 2
    piece = rows // PIECES
    chunk = rows // CHUNKS
    w = lax.axis_index("wide")
    n = lax.axis_index("narrow")
    x = w % 2
    z = (w // 2) % 2
    y = n // 2
    core = n % 2
    p = w % 4
    wx = w + 1 - 2 * x
    wz = w + 2 - 4 * z
    px = p + 1 - 2 * x
    pz = p + 2 - 4 * z
    pd = 3 - p
    ns = n + 1 - 2 * core
    ny = n + 2 - 4 * y
    q = 2 * y + core
    qy = 2 * (1 - y) + core
    near = z == y
    far = z != y
    third = jnp.where(near, pz, px)
    first = jnp.where(near, px, pz)

    barrier = pltpu.get_barrier_semaphore()
    for target in ((wz, n), (w, ns), (w, ny), (w, 3 - n), *((wx, m) for m in range(4))):
        pl.semaphore_signal(barrier, inc=1, device_id=target, device_id_type=MESH)

    def part(i):
        return pl.ds(i * piece, piece)

    def side(t):
        return pl.ds(t * wide_half, wide_half)

    local = [
        pltpu.make_async_copy(v_ref, left.at[core], local_sem.at[0]),
        pltpu.make_async_copy(a_ref, abuf.at[q], local_sem.at[1]),
        pltpu.make_async_copy(v_ref.at[:, side(0)], vbuf.at[p, 0], local_sem.at[2]),
        pltpu.make_async_copy(v_ref.at[:, side(1)], vbuf.at[p, 1], local_sem.at[3]),
    ]
    for copy in local:
        copy.start()

    taken = [0, 0]
    origin = []

    def fresh(kind, count=1):
        start = taken[kind]
        taken[kind] += count
        return start

    def remote(src, dst, target, send, recv):
        copy = pltpu.make_async_remote_copy(
            src_ref=src, dst_ref=dst, send_sem=send_sem.at[send], recv_sem=recv_sem.at[recv],
            device_id=target, device_id_type=MESH,
        )
        origin.append((copy, send))
        return copy

    def family(make, count, arrivals):
        send, recv = fresh(0), fresh(1, max(arrivals) + 1)
        return [remote(*make(i), send, recv + arrivals[i]) for i in range(count)]

    pieces = range(PIECES)
    each = list(pieces)
    half_each = [i % (PIECES // 2) for i in pieces]
    pairs = [(t, i) for t in range(2) for i in pieces]

    def both(flat):
        return [flat[:PIECES], flat[PIECES:]]

    def basis(i, target):
        t, k = pairs[i]
        return v_ref.at[part(k), side(t)], vbuf.at[p, t, part(k)], target

    def shared_x(i):
        t, k = pairs[i]
        return vbuf.at[px, t, part(k)], sibling_x.at[t, part(k)], (w, ns)

    count = 2 * PIECES
    vx = both(family(lambda i: basis(i, (wx, n)), count, list(range(count))))
    z_arrivals = [0] * PIECES + [1 + 2 * i // PIECES for i in pieces]
    taken_z = taken[1]
    vz = both(family(lambda i: basis(i, (wz, n)), count, z_arrivals))
    vxs = both(family(shared_x, count, list(range(count))))
    quarter = OVER_X // 2
    turned = pl.ds(OVER_X, cols - OVER_X)
    lean_rows = (OVER_X * cols + (rows - OVER_X) * (cols - OVER_X)) // cols
    lean_out = near == (core == x)
    lean_in = far == (core == x)
    lean_relay = far == (core != x)
    ay_sems, ayr_sems = (fresh(0), fresh(1, PIECES)), (fresh(0), fresh(1, PIECES))

    def lean(i):
        return i * piece >= OVER_X

    def moments_y(i, wanted):
        return remote(a_ref.at[part(i), wanted], abuf.at[q, part(i), wanted], (w, ny), ay_sems[0], ay_sems[1] + i)

    def moments_core(i, wanted):
        return remote(abuf.at[qy, part(i), wanted], abuf.at[qy, part(i), wanted], (w, ns), ayr_sems[0], ayr_sems[1] + i)

    full = pl.ds(0, cols)
    ay = [moments_y(i, full) for i in pieces]
    ayr = [moments_core(i, full) for i in pieces]
    ay_lean = [moments_y(i, turned) if lean(i) else ay[i] for i in pieces]
    ayr_lean = [moments_core(i, turned) if lean(i) else ayr[i] for i in pieces]

    def choose(condition, when_true, when_false):
        pl.when(condition)(when_true)
        pl.when(jnp.logical_not(condition))(when_false)

    def start_y(i):
        if lean(i):
            choose(lean_out, ay_lean[i].start, ay[i].start)
        else:
            ay[i].start()

    def relay_y(i):
        if lean(i):
            choose(lean_in, ay_lean[i].wait_recv, ay[i].wait_recv)
            choose(lean_in, ayr_lean[i].start, ayr[i].start)
        else:
            ay[i].wait_recv()
            ayr[i].start()

    def receive_relay(i):
        if lean(i):
            choose(lean_relay, ayr_lean[i].wait_recv, ayr[i].wait_recv)
        else:
            ayr[i].wait_recv()

    def rows_x(k):
        return pl.ds(k * quarter, quarter)

    xo = family(lambda k: (abuf.at[pd, rows_x(k)], opp_x.at[rows_x(k)], (wx, n)), 2, [0, 0])
    xos = family(lambda k: (opp_x.at[rows_x(k)], opp_x.at[rows_x(k)], (w, ns)), 2, [0, 0])
    zo = family(lambda i: (abuf.at[pd, part(i), turned], opp_z.at[part(i)], (wz, n)), PIECES, half_each)
    zos = family(lambda i: (opp_z.at[part(i)], opp_z.at[part(i)], (w, ns)), PIECES, half_each)
    vs = family(lambda i: (v_ref, left.at[core], (w, ns)), 1, [0])[0]
    as_ = family(lambda i: (a_ref, abuf.at[q], (w, ns)), 1, [0])[0]
    steps = range(CHUNKS)
    arrivals = fresh(1, CHUNKS)
    outside = core != y
    lead = jnp.where(outside, x, 1 - x)
    halves = (lead, 1 - lead)
    same_x = (outside.astype(jnp.int32), 1 - outside.astype(jnp.int32))
    block_sends = fresh(0, 8)
    block_cols = wide_half // 2
    right_cols = pl.ds(block_cols, block_cols)

    def ship_rows(t, s, j, wanted):
        apart = 1 - same_x[s]
        return remote(
            partials.at[t, s, j, :, wanted], rows_in.at[2 * apart + y, j, :, wanted],
            (jnp.where(same_x[s] == 1, w, wx), 2 * core + t), block_sends + 4 * t + 2 * s + j // HALF, arrivals + j,
        )

    all_cols = pl.ds(0, wide_half)
    sends = [[[ship_rows(t, s, j, all_cols) for j in steps] for s in range(2)] for t in range(2)]
    thin_sends = {(t, s, j): ship_rows(t, s, j, right_cols) for t, j in THIN for s in range(2)}

    def start_rows(t, s, j):
        if (t, j) in THIN:
            choose(halves[s] == core, thin_sends[t, s, j].start, sends[t][s][j].start)
        else:
            sends[t][s][j].start()

    z_sends, z_recvs = fresh(0, 2), fresh(1, CHUNKS)

    def exchange(j, wanted):
        return remote(zsend.at[j, :, wanted], zrecv.at[j, :, wanted], (wz, n), z_sends + j // HALF, z_recvs + j)

    zc = [exchange(j, all_cols) for j in steps]
    thin_zc = {j: exchange(j, right_cols) for _, j in THIN}
    reflect_send, reflect_recv = fresh(0), fresh(1)
    reflect = [
        remote(msend.at[pl.ds(j * chunk, chunk)], mirror.at[pl.ds(j * chunk, chunk)], (w + y - x, 2 * x + 1), reflect_send, reflect_recv)
        for j in range(HALF)
    ]
    leave = [
        pltpu.make_async_copy(obuf.at[pl.ds(j * chunk, chunk)], o_ref.at[pl.ds(j * chunk, chunk)], out_sem.at[j // HALF])
        for j in steps
    ]

    def all_sent(copies, ref):
        send = next(index for copy, index in origin if copy is copies[0])
        pltpu.make_async_remote_copy(
            src_ref=ref, dst_ref=ref, send_sem=send_sem.at[send], recv_sem=recv_sem.at[0], device_id=(w, ns), device_id_type=MESH,
        ).wait_send()

    def all_here(recv, ref):
        pltpu.make_async_remote_copy(
            src_ref=ref, dst_ref=ref, send_sem=send_sem.at[0], recv_sem=recv_sem.at[recv], device_id=(w, ns), device_id_type=MESH,
        ).wait_recv()

    def owned(i):
        return core == i // (PIECES // 2)

    def split_a(block, i):
        value = abuf[block, i * piece : (i + 1) * piece, :]
        high, low = split(value)
        aparts[block, 0, i * piece : (i + 1) * piece, :] = high
        aparts[block, 1, i * piece : (i + 1) * piece, :] = low

    def split_own(i):
        if not lean(i):
            split_a(p, i)
            return
        span = slice(i * piece, (i + 1) * piece)
        high, low = split(abuf[p, span, OVER_X:])
        aparts[p, 0, span, OVER_X:] = high
        aparts[p, 1, span, OVER_X:] = low
        high, low = split(abuf[p, :OVER_X, span].T)
        aparts[p, 0, span, :OVER_X] = high
        aparts[p, 1, span, :OVER_X] = low

    def turn_left(half, t, i, value):
        high, low = split(value.T)
        leftx_t[half, 0, t * wide_half : (t + 1) * wide_half, i * piece : (i + 1) * piece] = high
        leftx_t[half, 1, t * wide_half : (t + 1) * wide_half, i * piece : (i + 1) * piece] = low

    def turn_own(t, i):
        turn_left(core, t, i, vbuf[px, t, i * piece : (i + 1) * piece, :])

    def turn_sibling(t, i):
        turn_left(1 - core, t, i, sibling_x[t, i * piece : (i + 1) * piece, :])

    def turn_opp(i):
        high, low = split(opp_z[i * piece : (i + 1) * piece, :].T)
        oparts[0, OVER_X:, i * piece : (i + 1) * piece] = high
        oparts[1, OVER_X:, i * piece : (i + 1) * piece] = low

    def split_opp(k):
        high, low = split(opp_x[k * quarter : (k + 1) * quarter, :])
        oparts[0, k * quarter : (k + 1) * quarter, :] = high
        oparts[1, k * quarter : (k + 1) * quarter, :] = low

    def start_opp(i):
        for k in range(2):
            if ((k + 1) * quarter - 1) // piece == i:
                @pl.when(core == k)
                def _():
                    xo[k].start()

        @pl.when(owned(i))
        def _():
            zo[i].start()

    late_ay = far & (core == x)
    early_recv = near & (core != x)
    early_relay = near & (core == x)

    pl.semaphore_wait(barrier, 8)
    @pl.when(jnp.logical_not(late_ay))
    def _():
        for i in pieces:
            start_y(i)

    for i in pieces:
        vx[0][i].start()
        vz[0][i].start()

    as_.start()
    vs.start()
    for i in range(AHEAD_X):
        vx[1][i].start()
    for i in range(AHEAD_Z):
        vz[1][i].start()
    for copy in local:
        copy.wait()
    as_.wait_recv()

    @pl.when(far)
    def _():
        for i in pieces:
            start_opp(i)

    left_t[core, 0], left_t[core, 1] = split(left[core].T)
    for i in pieces:
        split_a(first, i)

    @pl.when(near)
    def _():
        for i in pieces:
            split_a(p, i)

    vs.wait_recv()
    left_t[1 - core, 0], left_t[1 - core, 1] = split(left[1 - core].T)
    for i in pieces:
        @pl.when(early_recv)
        def _():
            relay_y(i)
            start_opp(i)

        vx[0][i].wait_recv()
        vxs[0][i].start()
        turn_own(0, i)

        @pl.when(early_relay)
        def _():
            receive_relay(i)
            start_opp(i)

        if i == 1:
            @pl.when(late_ay)
            def _():
                for k in pieces:
                    start_y(k)

    for i in range(AHEAD_X, PIECES):
        vx[1][i].start()
    for i in range(AHEAD_Z, PIECES):
        vz[1][i].start()
    for i in pieces:
        vxs[0][i].wait_recv()
        turn_sibling(0, i)
    all_here(taken_z, vbuf.at[pz, 0])

    def term(t, block):
        return dot3((aparts[block, 0], aparts[block, 1]), split(vbuf[block, t]))

    total = term(0, first)
    right_p = split(vbuf[p, 0])
    right_third = split(vbuf[third, 0])

    def consume_x(i):
        vxs[1][i].wait_recv()
        turn_sibling(1, i)

    def forward_x(i):
        vx[1][i].wait_recv()
        vxs[1][i].start()
        turn_own(1, i)

    images = []

    def pass_rows(i):
        @pl.when(jnp.logical_not(early_recv))
        def _():
            relay_y(i)

    def finish_rows(i):
        @pl.when(jnp.logical_not(early_relay))
        def _():
            receive_relay(i)

        split_a(third, i)

        @pl.when(far)
        def _():
            split_own(i)

        span = part(i)
        value = total[i * piece : (i + 1) * piece]
        value += dot3((aparts[p, 0, span], aparts[p, 1, span]), right_p)
        value += dot3((aparts[third, 0, span], aparts[third, 1, span]), right_third)
        images.append(split(value))

    def other_part(t, k):
        span = pl.ds(pl.multiple_of(k * wide_half, wide_half), wide_half)
        return dot3((oparts.at[0, :, span][...], oparts.at[1, :, span][...]), split(vbuf[pz, t, span]))

    pass_rows(0)
    pass_rows(1)
    finish_rows(0)
    pass_rows(2)
    finish_rows(1)
    finish_rows(2)
    for k in range(2):
        @pl.when(core == k)
        def _():
            xo[k].wait_recv()
            xos[k].start()
            split_opp(k)

    pass_rows(3)
    for k in range(2):
        @pl.when(core != k)
        def _():
            xos[k].wait_recv()
            split_opp(k)

    for i in pieces:
        @pl.when(owned(i))
        def _():
            zo[i].wait_recv()
            zos[i].start()
            turn_opp(i)

    other = other_part(0, core)
    finish_rows(3)
    for i in pieces:
        @pl.when(jnp.logical_not(owned(i)))
        def _():
            zos[i].wait_recv()
            turn_opp(i)

    own_image = tuple(jnp.concatenate([pair[k] for pair in images], axis=0) for k in range(2))
    other_image = split(other + other_part(0, 1 - core))

    def block_of(half, start, size, image):
        span = pl.ds(start, size)
        own, other = image
        return dot3((left_t[half, 0, span], left_t[half, 1, span]), own) + dot3(
            (leftx_t[half, 0, span], leftx_t[half, 1, span]), other
        )

    swapped = slot_ref[w // GROUP_WIDE]
    same_flag = (((z + swapped + y) % 2) == 0).astype(jnp.int32)
    local_t = jnp.logical_not(outside)
    diagonal = x == y
    whole = core == 0

    def needed(t, s, g, body):
        if t == 0 or g == 1:
            body()

    def send_block(t, s, g, image):
        def body():
            cuts = 2 if s == 0 and g == t else 1
            count = HALF // cuts
            for c in range(cuts):
                first_j = g * HALF + c * count
                block = block_of(halves[s], first_j * chunk, count * chunk, image)
                if s == 0:
                    ship(block, first_j, count)
            if s == 1:
                place(block)

        def ship(block, first_j, count):
            for k in range(count):
                partials[t, s, first_j + k] = block[k * chunk : (k + 1) * chunk]
                start_rows(t, s, first_j + k)

        def place(block):
            pl.when(jnp.logical_not(local_t & (core == t)))(lambda: ship(block, g * HALF, HALF))

            @pl.when(local_t & (core == t))
            def _():
                for k in range(HALF):
                    rows_in[y, g * HALF + k] = block[k * chunk : (k + 1) * chunk]

        needed(t, s, g, body)

    def drain_block(t, s, g):
        def body():
            def sent(count):
                all_sent(sends[t][s][g * HALF :], partials.at[t, s, pl.ds(g * HALF, count)])

            if t == g:
                choose(halves[s] == core, lambda: sent(HALF - HALF // 4), lambda: sent(HALF))
            else:
                sent(HALF)

        def drain():
            if s == 0:
                body()
            else:
                pl.when(jnp.logical_not(local_t & (core == t)))(body)

        needed(t, s, g, drain)

    def by_width(j, body):
        if any(j == thin for _, thin in THIN):
            choose(diagonal & (core == j // HALF), lambda: body(True, block_cols), lambda: body(False, 0))
        else:
            body(False, 0)

    def gather_rows(j):
        def gather(thin, start):
            wanted = pl.ds(start, wide_half - start)

            @pl.when(local_t)
            def _():
                all_here(arrivals + j, rows_in.at[pl.ds(0, 3), j, :, wanted])

            @pl.when(outside)
            def _():
                all_here(arrivals + j, rows_in.at[:, j, :, wanted])

            same = rows_in[y, j, :, start:] + rows_in[2 + y, j, :, start:]
            other = rows_in[1 - y, j, :, start:] + rows_in[3 - y, j, :, start:]
            mask = jnp.full(same.shape, same_flag) == 1
            zsend[j, :, start:] = jnp.where(mask, other, same)
            (thin_zc if thin else zc)[j].start()
            obuf[pl.ds(j * chunk, chunk), start:] = jnp.where(mask, same, other)

        by_width(j, gather)

    def finish(j):
        def close(thin, start):
            (thin_zc if thin else zc)[j].wait_recv()
            total = obuf[pl.ds(j * chunk, chunk), start:] + zrecv[j, :, start:]
            obuf[pl.ds(j * chunk, chunk), start:] = total
            leave[j].start()
            if j >= HALF and not thin:
                @pl.when(core == 0)
                def _():
                    if j == HALF:
                        for s in range(2):
                            drain_block(1, s, 1)
                    msend[pl.ds((j - HALF) * chunk, chunk)] = total
                    reflect[j - HALF].start()

        by_width(j, close)
        if j % HALF == HALF // 2 - 1:
            @pl.when(diagonal & (core == j // HALF))
            def _():
                top = (j + 1) * chunk
                obuf[top : top + block_cols, :block_cols] = obuf[top - block_cols : top, block_cols:].T

    image = (own_image, other_image)
    for s in range(2):
        send_block(0, s, 0, image)
    for i in pieces:
        forward_x(i)
    for i in pieces:
        consume_x(i)
    for s in range(2):
        send_block(0, s, 1, image)
    total = term(1, p) + term(1, px)

    def half_term(left, t, k):
        span = pl.ds(k * wide_half, wide_half)
        return dot3((left.at[0, :, span][...], left.at[1, :, span][...]), split(vbuf[pz, t, span]))

    other = None
    for k in range(2):
        all_here(taken_z + 1 + k, vbuf.at[pz, 1, pl.ds(k * wide_half, wide_half)])
        total += half_term(aparts.at[pz], 1, k)
        more = half_term(oparts, 1, k)
        other = more if other is None else other + more
    image = (split(total), split(other))
    send_block(1, 1, 1, image)

    @pl.when(whole)
    def _():
        for j in range(HALF):
            gather_rows(j)

    send_block(1, 0, 1, image)

    for j in range(HALF, CHUNKS):
        gather_rows(j)

    @pl.when(whole)
    def _():
        for j in range(HALF):
            finish(j)
        choose(
            diagonal & (core == 0),
            lambda: all_sent(zc[:HALF], zsend.at[pl.ds(0, HALF - HALF // 4)]),
            lambda: all_sent(zc[:HALF], zsend.at[pl.ds(0, HALF)]),
        )

    for j in range(HALF, CHUNKS):
        finish(j)

    @pl.when(jnp.logical_not(whole))
    def _():
        all_here(reflect_recv, mirror)
        obuf[pl.ds(0, HALF * chunk), :] = mirror[...].T
        for j in range(HALF):
            leave[j].start()

    @pl.when(core == 0)
    def _():
        all_sent(reflect, msend)

    for copies in (vx[0], vz[0], vxs[0], [vs], [as_]):
        all_sent(copies, abuf.at[0])
    for copies, condition in ((ay, lean_out), (ayr, lean_in)):
        choose(
            condition,
            lambda: all_sent(copies, abuf.at[0, pl.ds(0, lean_rows)]),
            lambda: all_sent(copies, abuf.at[0]),
        )
    all_sent(xo, opp_x.at[pl.ds(0, quarter)])
    all_sent(xos, opp_x.at[pl.ds(0, quarter)])
    all_sent(zo, opp_z.at[pl.ds(0, rows // 2)])
    all_sent(zos, opp_z.at[pl.ds(0, rows // 2)])
    choose(
        diagonal & (core == 1),
        lambda: all_sent(zc[HALF:], zsend.at[pl.ds(HALF, HALF - HALF // 4)]),
        lambda: all_sent(zc[HALF:], zsend.at[pl.ds(HALF, HALF)]),
    )
    for s in range(2):
        for g in range(2):
            drain_block(0, s, g)

    @pl.when(core == 1)
    def _():
        for s in range(2):
            drain_block(1, s, 1)

    for g in range(2):
        group = pl.ds(g * HALF * chunk, HALF * chunk)
        pltpu.make_async_copy(obuf.at[group], o_ref.at[group], out_sem.at[g]).wait()


def fast_body(moments, eigen_basis, slot_order):
    rows, cols = moments.shape
    f32 = jnp.float32
    chunk = rows // CHUNKS
    wide_half = cols // 2
    return pl.pallas_call(
        kernel,
        out_shape=jax.ShapeDtypeStruct((rows, wide_half), f32),
        in_specs=[
            pl.BlockSpec(memory_space=pltpu.SMEM),
            pl.BlockSpec(memory_space=pl.ANY),
            pl.BlockSpec(memory_space=pl.ANY),
        ],
        out_specs=pl.BlockSpec(memory_space=pl.ANY),
        scratch_shapes=[
            pltpu.VMEM((4, rows, cols), f32),
            pltpu.VMEM((4, 2, rows, cols), jnp.bfloat16),
            pltpu.VMEM((OVER_X, cols), f32),
            pltpu.VMEM((rows, cols - OVER_X), f32),
            pltpu.VMEM((2, cols, rows), jnp.bfloat16),
            pltpu.VMEM((4, 2, rows, wide_half), f32),
            pltpu.VMEM((2, rows, wide_half), f32),
            pltpu.VMEM((2, rows, cols), f32),
            pltpu.VMEM((2, 2, cols, rows), jnp.bfloat16),
            pltpu.VMEM((2, 2, cols, rows), jnp.bfloat16),
            pltpu.VMEM((2, 2, CHUNKS, chunk, wide_half), f32),
            pltpu.VMEM((4, CHUNKS, chunk, wide_half), f32),
            *[pltpu.VMEM((CHUNKS, chunk, wide_half), f32)] * 2,
            *[pltpu.VMEM((HALF * chunk, wide_half), f32)] * 2,
            pltpu.VMEM((rows, wide_half), f32),
            pltpu.SemaphoreType.DMA((4,)),
            pltpu.SemaphoreType.DMA((2,)),
            pltpu.SemaphoreType.DMA((SENDS,)),
            pltpu.SemaphoreType.DMA((RECVS,)),
        ],
        compiler_params=pltpu.CompilerParams(
            collective_id=0, has_side_effects=True, vmem_limit_bytes=53 * 1024 * 1024
        ),
        name="rayleigh",
    )(slot_order, moments, eigen_basis)


def partner(value, axis, stride):
    mask = 2**stride
    pairs = [(source, source ^ mask) for source in range(lax.axis_size(axis))]
    return lax.ppermute(value, axis, pairs)


def body(moments, eigen_basis, slot_order):
    wide_pos = lax.axis_index("wide")
    subproblem = wide_pos // GROUP_WIDE
    position = wide_pos % GROUP_WIDE
    swapped = lax.dynamic_index_in_dim(slot_order, subproblem, 0, keepdims=False)
    narrow_pos = lax.axis_index("narrow")
    col_count = eigen_basis.shape[1]
    half_cols = col_count // 2
    full_basis = lax.all_gather(eigen_basis, "narrow", axis=1, tiled=True)
    first_half = lax.dynamic_slice_in_dim(full_basis, narrow_pos * half_cols, half_cols, 1)
    second_half = lax.dynamic_slice_in_dim(full_basis, K + narrow_pos * half_cols, half_cols, 1)
    local_panel = jnp.concatenate([first_half, second_half], axis=1)
    pair_block = partner(local_panel, "wide", 0)
    joined = jnp.where(
        position % 2 == 0,
        jnp.concatenate([local_panel, pair_block], axis=0),
        jnp.concatenate([pair_block, local_panel], axis=0),
    )
    quad_block = partner(joined, "wide", 1)
    col_panel = jnp.where(
        position // 2 % 2 == 0,
        jnp.concatenate([joined, quad_block], axis=0),
        jnp.concatenate([quad_block, joined], axis=0),
    )
    products = jnp.dot(
        lax.all_gather(moments, "narrow", axis=1, tiled=True),
        col_panel,
        precision=lax.Precision.HIGHEST,
        preferred_element_type=jnp.float32,
    )
    partials = []
    for slot_index in range(2):
        half_panel = products[:, slot_index * half_cols : (slot_index + 1) * half_cols]
        vectors_half = full_basis[:, slot_index * K : (slot_index + 1) * K]
        partials.append(
            lax.dot_general(
                vectors_half,
                half_panel,
                (((0,), (0,)), ((), ())),
                precision=lax.Precision.HIGHEST,
                preferred_element_type=jnp.float32,
            )
        )
    stacked = jnp.stack(partials)
    slot_pick = (position // 2 + swapped) % 2
    row_part = position % 2
    summed = stacked + partner(stacked, "wide", 0)
    summed = summed + partner(summed, "wide", 1)
    chosen = lax.dynamic_index_in_dim(summed, slot_pick, 0, keepdims=False)
    return lax.dynamic_slice_in_dim(chosen, row_part * (K // 2), K // 2, 0)


def solution(mesh):
    placed = (P("wide", "narrow"), P("wide", "narrow"), P())
    cube = mesh.shape["narrow"] == 4
    return jax.shard_map(
        fast_body if cube else body, mesh=mesh, in_specs=placed, out_specs=P("wide", "narrow"), check_vma=False
    )
```
